512 devices in a mesh: grp: 32 (over z_lo, y), blk: 16 (over z_hi, x, core).
Axes of the slice: x: 4, y: 4, z: 16 (z_hi: 2, z_lo: 8; z = z_hi * 8 + z_lo), core: 2. Of those that a mesh axis runs over, the one named last changes fastest.
Arguments:
- image: bfloat16 [4096, 1024], P(('blk', 'grp')), may hold values from -16 to 16
- text: bfloat16 [4096, 1024], P(('grp', 'blk')), may hold values from -16 to 16
- mimage: bfloat16 [4096, 1024], P(('blk', 'grp')), may hold values from -16 to 16
- mtext: bfloat16 [4096, 1024], P(('grp', 'blk')), may hold values from -16 to 16
Outputs:
- grad_image: float32 [4096, 1024], P(('blk', 'grp'))
- grad_text: float32 [4096, 1024], P(('grp', 'blk'))
- loss: float32 [], replicated
The draws below stay inside these ranges and needn't reach their ends.
All inputs are finite; a program needn't handle non-finite values.
Results may differ from the reference program's by a relative error of at most 0.0037.
Values may be sent and summed in bfloat16 or wider, within the bound.
No kernel may reach another device: no remote copies, remote signals or barrier semaphores. Data moves between devices by JAX's collectives and lax.ppermute only.
A program may use at most 64 MiB of HBM per device.

```python
import math
import jax
import jax.numpy as jnp
from jax import lax

D = 1024
BATCH = 4096


def make_pairs(key):
    keys = [jax.random.fold_in(key, 101 + number) for number in range(10)]
    shape = (BATCH, D)
    base_image = jnp.clip(jax.random.normal(keys[0], shape, jnp.float32), -3.0, 3.0)
    base_text = jnp.clip(jax.random.normal(keys[1], shape, jnp.float32), -3.0, 3.0)
    noise_image = jnp.clip(jax.random.normal(keys[2], shape, jnp.float32), -3.0, 3.0)
    noise_text = jnp.clip(jax.random.normal(keys[3], shape, jnp.float32), -3.0, 3.0)
    scale_image = jnp.exp(jax.random.uniform(keys[4], (BATCH, 1), jnp.float32, 0.0, math.log(3.0)))
    scale_text = jnp.exp(jax.random.uniform(keys[5], (BATCH, 1), jnp.float32, 0.0, math.log(3.0)))
    image_out = base_image * scale_image
    text_out = base_text * scale_text
    mimage_out = 0.8 * image_out + 0.6 * noise_image * scale_image
    mtext_out = 0.8 * text_out + 0.6 * noise_text * scale_text
    return (image_out, text_out, mimage_out, mtext_out)


def draw_image(key, part):
    return make_pairs(key)[0].astype(jnp.bfloat16)


def draw_text(key, part):
    return make_pairs(key)[1].astype(jnp.bfloat16)


def draw_mimage(key, part):
    return make_pairs(key)[2].astype(jnp.bfloat16)


def draw_mtext(key, part):
    return make_pairs(key)[3].astype(jnp.bfloat16)


def setup_inputs(seed: int = 0) -> dict:
    key_list = jax.random.split(jax.random.key(seed), 5)
    return {
        "image": draw_image(jax.random.fold_in(key_list[4], 71), 0),
        "text": draw_text(jax.random.fold_in(key_list[4], 71), 0),
        "mimage": draw_mimage(jax.random.fold_in(key_list[4], 71), 0),
        "mtext": draw_mtext(jax.random.fold_in(key_list[4], 71), 0),
    }


mix_weight = 0.4
very_low = -1.0e30


def reference(image, text, mimage, mtext):
    scale_factor = D ** -0.5
    image_all = image.astype(jnp.float32)
    text_all = text.astype(jnp.float32)
    mimage_all = mimage.astype(jnp.float32)
    mtext_all = mtext.astype(jnp.float32)
    block_rows = math.gcd(BATCH, 512)
    block_count = BATCH // block_rows
    column_ids = lax.iota(jnp.int32, BATCH)

    def scores_of(block_index):
        first_row = (block_index * block_rows).astype(jnp.int32)
        image_block = lax.dynamic_slice_in_dim(image_all, first_row, block_rows, 0)
        mimage_block = lax.dynamic_slice_in_dim(mimage_all, first_row, block_rows, 0)
        score_on = jnp.dot(image_block, text_all.T, precision=lax.Precision.HIGHEST) * scale_factor
        score_mom = jnp.dot(mimage_block, mtext_all.T, precision=lax.Precision.HIGHEST) * scale_factor
        return first_row, image_block, score_on, score_mom

    def fold_columns(run_max, run_total, scores):
        new_max = jnp.maximum(run_max, jnp.max(scores, axis=0))
        new_total = run_total * jnp.exp(run_max - new_max) + jnp.sum(jnp.exp(scores - new_max[None, :]), axis=0)
        return new_max, new_total

    def row_lse(scores):
        top_row = jnp.max(scores, axis=1)
        return top_row + jnp.log(jnp.sum(jnp.exp(scores - top_row[:, None]), axis=1))

    def first_pass(carry, block_index):
        cmax_on, csum_on, cmax_mom, csum_mom = carry
        first_row, image_block, score_on, score_mom = scores_of(block_index)
        cmax_on, csum_on = fold_columns(cmax_on, csum_on, score_on)
        cmax_mom, csum_mom = fold_columns(cmax_mom, csum_mom, score_mom)
        return (cmax_on, csum_on, cmax_mom, csum_mom), (row_lse(score_on), row_lse(score_mom))

    low_cols = jnp.full((BATCH,), very_low, jnp.float32)
    zero_cols = jnp.zeros((BATCH,), jnp.float32)
    blocks = jnp.arange(block_count, dtype=jnp.int32)
    col_stats, row_parts = lax.scan(first_pass, (low_cols, zero_cols, low_cols, zero_cols), blocks)
    col_online = col_stats[0] + jnp.log(col_stats[1])
    col_momentum = col_stats[2] + jnp.log(col_stats[3])
    row_online = row_parts[0].reshape(BATCH)
    row_momentum = row_parts[1].reshape(BATCH)

    def second_pass(carry, block_index):
        grad_text_acc, cross_term = carry
        first_row, image_block, score_on, score_mom = scores_of(block_index)
        row_on = lax.dynamic_slice_in_dim(row_online, first_row, block_rows, 0)
        row_mom = lax.dynamic_slice_in_dim(row_momentum, first_row, block_rows, 0)
        row_ids = first_row + lax.iota(jnp.int32, block_rows)
        diagonal = (row_ids[:, None] == column_ids[None, :]).astype(jnp.float32)
        prob_row = jnp.exp(score_on - row_on[:, None])
        prob_col = jnp.exp(score_on - col_online[None, :])
        target_row = mix_weight * jnp.exp(score_mom - row_mom[:, None]) + (1.0 - mix_weight) * diagonal
        target_col = mix_weight * jnp.exp(score_mom - col_momentum[None, :]) + (1.0 - mix_weight) * diagonal
        grad_tile = 0.5 * ((prob_row - target_row) + (prob_col - target_col))
        grad_round = lax.optimization_barrier(grad_tile.astype(jnp.bfloat16)).astype(jnp.float32)
        grad_rows = jnp.dot(grad_round, text_all, precision=lax.Precision.HIGHEST)
        grad_text_acc = grad_text_acc + jnp.dot(grad_round.T, image_block, precision=lax.Precision.HIGHEST)
        cross_term = cross_term + jnp.sum((target_row + target_col) * score_on)
        return (grad_text_acc, cross_term), grad_rows

    start_carry = (jnp.zeros((BATCH, D), jnp.float32), jnp.zeros((), jnp.float32))
    final_carry, grad_blocks = lax.scan(second_pass, start_carry, blocks)
    grad_image = grad_blocks.reshape(BATCH, D)
    grad_text = final_carry[0]
    loss = (jnp.sum(row_online) + jnp.sum(col_online) - final_carry[1]) / (2.0 * BATCH)
    return grad_image, grad_text, loss
```

```python
import jax
import jax.numpy as jnp
from jax import lax
from jax.sharding import Mesh, PartitionSpec as P

mix_weight = 0.4
plane = ("x", "y", "c")
column = ("zh", "zl")


def share(block, axes, count):
    sent = jnp.broadcast_to(block[None], (count,) + block.shape)
    return lax.all_to_all(sent, axes, 0, 0, tiled=True)


def scores(left, right):
    product = lax.dot_general(left, right, (((1,), (1,)), ((), ())), preferred_element_type=jnp.float32)
    return product * left.shape[1] ** (-0.5)


def stats_of(score_on, score_mom, along):
    max_on = jnp.max(score_on, axis=along)
    sum_on = jnp.sum(jnp.exp(score_on - jnp.expand_dims(max_on, along)), axis=along)
    max_mom = jnp.max(score_mom, axis=along)
    weight = jnp.exp(score_mom - jnp.expand_dims(max_mom, along))
    return [max_on, sum_on, max_mom, jnp.sum(weight, axis=along), jnp.sum(weight * score_on, axis=along)]


def combine(parts):
    max_on, sum_on, max_mom, sum_mom, cross = (parts[:, k] for k in range(5))
    top_on = jnp.max(max_on, axis=0)
    lse_on = top_on + jnp.log(jnp.sum(sum_on * jnp.exp(max_on - top_on), axis=0))
    top_mom = jnp.max(max_mom, axis=0)
    rescale = jnp.exp(max_mom - top_mom)
    total = jnp.sum(sum_mom * rescale, axis=0)
    lse_mom = top_mom + jnp.log(total)
    loss = jnp.sum(lse_on - mix_weight * jnp.sum(cross * rescale, axis=0) / total)
    return lse_on, lse_mom, loss


def local(image, text, mimage, mtext):
    rows, width = image.shape
    n_plane = lax.axis_size(plane)
    n_column = lax.axis_size(column)
    got_i = share(jnp.concatenate([image, mimage], axis=0), plane, n_plane)
    got_t = share(jnp.concatenate([text, mtext], axis=0), column, n_column)
    images = got_i[:, :rows].reshape(n_plane * rows, width)
    mimages = got_i[:, rows:].reshape(n_plane * rows, width)
    texts = got_t[:, :rows].reshape(n_column * rows, width)
    mtexts = got_t[:, rows:].reshape(n_column * rows, width)

    score_on = scores(images, texts)
    score_mom = scores(mimages, mtexts)

    def ids(n, axes, other):
        pos = lax.iota(jnp.int32, n * rows)
        peer, row = pos // rows, pos % rows
        return peer, row

    peer, row = ids(n_plane, plane, None)
    px, py, pc = peer // 8, (peer // 2) % 4, peer % 2
    zh, zl = lax.axis_index("zh"), lax.axis_index("zl")
    image_ids = ((zh * 8 + px * 2 + pc) * 32 + zl * 4 + py) * rows + row
    peer, row = ids(n_column, column, None)
    qh, ql = peer // 8, peer % 8
    x, y, c = lax.axis_index("x"), lax.axis_index("y"), lax.axis_index("c")
    text_ids = ((ql * 4 + y) * 16 + qh * 8 + x * 2 + c) * rows + row
    diagonal = image_ids[:, None] == text_ids[None, :]

    row_parts = jnp.stack(stats_of(score_on, score_mom, 1))
    col_parts = jnp.stack(stats_of(score_on, score_mom, 0))
    own = jnp.sum(jnp.where(diagonal, score_on, 0.0), axis=0)
    col_parts = jnp.concatenate([col_parts, own[None]], axis=0)
    row_got = share(row_parts, plane, n_plane)
    col_got = share(col_parts, column, n_column)
    row_on, row_mom, row_loss = combine(row_got)
    col_on, col_mom, col_loss = combine(col_got)
    col_loss = col_loss - 2.0 * (1.0 - mix_weight) * jnp.sum(col_got[:, 5])

    delta = jnp.where(diagonal, 1.0 - mix_weight, 0.0)
    target_row = mix_weight * jnp.exp(score_mom - row_mom[:, None]) + delta
    target_col = mix_weight * jnp.exp(score_mom - col_mom[None, :]) + delta
    prob_row = jnp.exp(score_on - row_on[:, None])
    prob_col = jnp.exp(score_on - col_on[None, :])
    grad = (0.5 * ((prob_row - target_row) + (prob_col - target_col))).astype(jnp.bfloat16)

    part_image = jnp.dot(grad, texts, preferred_element_type=jnp.float32)
    part_text = lax.dot_general(grad, images, (((0,), (0,)), ((), ())), preferred_element_type=jnp.float32)
    got_image = lax.all_to_all(part_image.reshape(n_plane, rows, width), plane, 0, 0, tiled=True)
    got_text = lax.all_to_all(part_text.reshape(n_column, rows, width), column, 0, 0, tiled=True)
    grad_image = jnp.sum(got_image, axis=0)
    grad_text = jnp.sum(got_text, axis=0)

    row_losses = share(jnp.full((1, 128), row_loss), column, n_column)
    col_losses = share(jnp.full((1, 128), col_loss), plane, n_plane)
    total_pairs = rows * n_plane * n_column
    loss = (jnp.sum(row_losses[:, 0, 0]) + jnp.sum(col_losses[:, 0, 0])) / (2.0 * total_pairs)
    return grad_image, grad_text, loss


def solution(mesh):
    fine = Mesh(mesh.devices.reshape(8, 4, 2, 4, 2), ("zl", "y", "zh", "x", "c"))
    by_image = P(("zh", "x", "c", "zl", "y"), None)
    by_text = P(("zl", "y", "zh", "x", "c"), None)
    return jax.shard_map(
        local,
        mesh=fine,
        in_specs=(by_image, by_text, by_image, by_text),
        out_specs=(by_image, by_text, P()),
        check_vma=False,
    )
```

```python
import jax
import jax.numpy as jnp
from jax import lax
from jax.sharding import Mesh, PartitionSpec as P

mix_weight = 0.4
column = ("zh", "zl")


def share(block, axes, count):
    sent = jnp.broadcast_to(block[None], (count,) + block.shape)
    return lax.all_to_all(sent, axes, 0, 0, tiled=True)


def swap(block):
    return lax.ppermute(block, "c", [(0, 1), (1, 0)])


def share_ring(block):
    return lax.all_gather(lax.all_gather(block, "x"), "y")


def scatter_ring(parts, axis, extra):
    here = lax.axis_index(axis)
    parts = parts.reshape(4, -1, parts.shape[-1])
    total = lax.dynamic_index_in_dim(parts, here, 0, False)
    tail = jnp.full((8, parts.shape[-1]), extra)
    rows = total.shape[0]
    got = []
    for k in (2, 1, 3):
        block = lax.dynamic_index_in_dim(parts, (here + k) % 4, 0, False)
        sent = jnp.concatenate([block, tail], axis=0)
        got.append(lax.ppermute(sent, axis, [(i, (i + k) % 4) for i in range(4)]))
    for piece in got:
        total = total + piece[:rows]
        extra = extra + piece[rows, 0]
    return total, extra


def scores(left, right):
    product = lax.dot_general(left, right, (((1,), (1,)), ((), ())), preferred_element_type=jnp.float32)
    return product * left.shape[1] ** (-0.5)


def stats_of(score_on, score_mom, along):
    max_on = jnp.max(score_on, axis=along)
    sum_on = jnp.sum(jnp.exp(score_on - jnp.expand_dims(max_on, along)), axis=along)
    max_mom = jnp.max(score_mom, axis=along)
    weight = jnp.exp(score_mom - jnp.expand_dims(max_mom, along))
    return [max_on, sum_on, max_mom, jnp.sum(weight, axis=along), jnp.sum(weight * score_on, axis=along)]


def combine(parts):
    max_on, sum_on, max_mom, sum_mom, cross = (parts[:, k] for k in range(5))
    top_on = jnp.max(max_on, axis=0)
    lse_on = top_on + jnp.log(jnp.sum(sum_on * jnp.exp(max_on - top_on), axis=0))
    top_mom = jnp.max(max_mom, axis=0)
    rescale = jnp.exp(max_mom - top_mom)
    total = jnp.sum(sum_mom * rescale, axis=0)
    lse_mom = top_mom + jnp.log(total)
    loss = jnp.sum(lse_on - mix_weight * jnp.sum(cross * rescale, axis=0) / total)
    return lse_on, lse_mom, loss


def local(image, text, mimage, mtext):
    rows, width = image.shape
    x, y, c, zh, zl = (lax.axis_index(a) for a in ("x", "y", "c", "zh", "zl"))
    n_plane, n_column = 32, 16
    half = n_plane // 2 * rows
    got_t = share(jnp.concatenate([text, mtext], axis=0), column, n_column)
    mine = share_ring(jnp.concatenate([image, mimage], axis=0)).reshape(16, 2 * rows, width)
    got_i = jnp.concatenate([mine, swap(mine)], axis=0)
    images = got_i[:, :rows].reshape(n_plane * rows, width)
    mimages = got_i[:, rows:].reshape(n_plane * rows, width)
    texts = got_t[:, :rows].reshape(n_column * rows, width)
    mtexts = got_t[:, rows:].reshape(n_column * rows, width)

    score_on = scores(images, texts)
    score_mom = scores(mimages, mtexts)

    pos = lax.iota(jnp.int32, n_plane * rows)
    peer, row = pos // rows, pos % rows
    pc, py, px = peer // 16, (peer // 4) % 4, peer % 4
    pc = jnp.where(pc == 0, c, 1 - c)
    image_ids = ((zh * 8 + px * 2 + pc) * 32 + zl * 4 + py) * rows + row
    pos = lax.iota(jnp.int32, n_column * rows)
    peer, row = pos // rows, pos % rows
    text_ids = (((peer % 8) * 4 + y) * 16 + (peer // 8) * 8 + x * 2 + c) * rows + row
    diagonal = image_ids[:, None] == text_ids[None, :]

    none = jnp.zeros((n_plane * rows,), jnp.float32)
    row_parts = jnp.stack(stats_of(score_on, score_mom, 1) + [none] * 3)
    own = jnp.sum(jnp.where(diagonal, score_on, 0.0), axis=0)
    col_parts = jnp.stack(stats_of(score_on, score_mom, 0) + [own] + [none[: n_column * rows]] * 2)
    col_got = share(col_parts, column, n_column)
    other = swap(jnp.concatenate([row_parts[:, half:], row_parts[:, :half]], axis=1))
    row_got = share_ring(jnp.concatenate([row_parts, other], axis=0)).reshape(n_plane, 8, n_plane * rows)
    row_on, row_mom, row_loss = combine(row_got)
    col_on, col_mom, col_loss = combine(col_got)
    col_loss = col_loss - 2.0 * (1.0 - mix_weight) * jnp.sum(col_got[:, 5])

    delta = jnp.where(diagonal, 1.0 - mix_weight, 0.0)
    target_row = mix_weight * jnp.exp(score_mom - row_mom[:, None]) + delta
    target_col = mix_weight * jnp.exp(score_mom - col_mom[None, :]) + delta
    prob_row = jnp.exp(score_on - row_on[:, None])
    prob_col = jnp.exp(score_on - col_on[None, :])
    grad = (0.5 * ((prob_row - target_row) + (prob_col - target_col))).astype(jnp.bfloat16)

    part_text = lax.dot_general(grad, images, (((0,), (0,)), ((), ())), preferred_element_type=jnp.float32)
    tail = jnp.full((n_column, rows, 128), row_loss)
    sent_text = jnp.concatenate([part_text.reshape(n_column, rows, width), tail], axis=2)
    got_text = lax.all_to_all(sent_text, column, 0, 0, tiled=True)

    part_image = jnp.dot(grad, texts, preferred_element_type=jnp.float32)
    got = swap(jnp.concatenate([part_image[half:], jnp.full((8, width), col_loss)], axis=0))
    part_image = part_image[:half] + got[:half]
    part_image, col_loss = scatter_ring(part_image, "y", col_loss + got[half, 0])
    grad_image, col_loss = scatter_ring(part_image, "x", col_loss)

    grad_text = jnp.sum(got_text[:, :, :width], axis=0)
    loss = (jnp.sum(got_text[:, 0, width]) + col_loss) / (2.0 * rows * n_plane * n_column)
    return grad_image, grad_text, loss


def solution(mesh):
    fine = Mesh(mesh.devices.reshape(8, 4, 2, 4, 2), ("zl", "y", "zh", "x", "c"))
    by_image = P(("zh", "x", "c", "zl", "y"), None)
    by_text = P(("zl", "y", "zh", "x", "c"), None)
    return jax.shard_map(
        local,
        mesh=fine,
        in_specs=(by_image, by_text, by_image, by_text),
        out_specs=(by_image, by_text, P()),
        check_vma=False,
    )
```

```python
import jax
import jax.numpy as jnp
from jax import lax
from jax.experimental import pallas as pl
from jax.experimental.pallas import tpu as pltpu
from jax.sharding import Mesh, PartitionSpec as P

mix_weight = 0.4
very_low = -1e30
column = ("zh", "zl")
n_plane, n_column, rows = 32, 16, 8
f32, bf16 = jnp.float32, jnp.bfloat16
side = 16 * rows


def call(body, outs, *args, flops=0, exps=0):
    whole = pl.BlockSpec(memory_space=pltpu.VMEM)
    specs = [pl.BlockSpec(memory_space=pltpu.SMEM) if a.dtype == jnp.int32 else whole for a in args]
    moved = sum(a.size * a.dtype.itemsize for a in list(args) + outs)
    return pl.pallas_call(
        body,
        out_shape=outs,
        in_specs=specs,
        out_specs=[whole] * len(outs),
        cost_estimate=pl.CostEstimate(flops=flops, bytes_accessed=moved, transcendentals=exps),
        compiler_params=pltpu.CompilerParams(vmem_limit_bytes=40 * 2**20),
    )(*args)


def shape(*dims, dtype=f32):
    return jax.ShapeDtypeStruct(dims, dtype)


def pack_kernel(text_ref, mtext_ref, image_ref, mimage_ref, send_ref, pair_ref):
    def pair(a_ref, b_ref):
        return jnp.concatenate([a_ref[...].astype(f32), b_ref[...].astype(f32)], axis=0).astype(bf16)

    both = pair(text_ref, mtext_ref)
    for peer in range(n_column):
        send_ref[peer] = both
    pair_ref[...] = pair(image_ref, mimage_ref)


def lanes(height):
    lane = lax.broadcasted_iota(jnp.int32, (height, 2 * side), 1)
    return lane, (lane & rows) == 0


def diagonal_of(pos_ref):
    x, y, c, zh, zl = (pos_ref[k] for k in range(5))
    row = lax.broadcasted_iota(jnp.int32, (2 * side, 2 * side), 0)
    lane, valid = lanes(2 * side)
    pc, py, px = row >> 7, (row >> 5) & 3, (row >> 3) & 3
    image_block = (zh * 8 + px * 2 + pc) * 32 + zl * 4 + py
    qh, ql = lane >> 7, (lane >> 4) & 7
    text_block = (ql * 4 + y) * 16 + qh * 8 + x * 2 + c
    return valid & (image_block == text_block) & ((row & 7) == (lane & 7))


def score_kernel(pos_ref, mine_ref, other_ref, text_ref, on_ref, mom_ref, row_ref, col_ref):
    width = text_ref.shape[-1]
    texts = text_ref[...].reshape(2 * side, width)

    def product(ref):
        out = lax.dot_general(
            ref[...].reshape(2 * side, width), texts, (((1,), (1,)), ((), ())), preferred_element_type=f32
        )
        return (out * width ** (-0.5)).reshape(16, 2, rows, 2 * side)

    mine, other = product(mine_ref), product(other_ref)
    first = pos_ref[2] == 0
    low, high = jnp.where(first, mine, other), jnp.where(first, other, mine)
    _, valid = lanes(2 * side)

    def both(which):
        return jnp.concatenate([part[:, which].reshape(side, 2 * side) for part in (low, high)], axis=0)

    on = jnp.where(valid, both(0), very_low)
    mom = jnp.where(valid, pltpu.roll(both(1), 2 * side - rows, 1), very_low)
    on_ref[...] = on
    mom_ref[...] = mom

    def stats(along):
        max_on = jnp.max(on, axis=along, keepdims=True)
        sum_on = jnp.sum(jnp.exp(on - max_on), axis=along, keepdims=True)
        max_mom = jnp.max(mom, axis=along, keepdims=True)
        weight = jnp.exp(mom - max_mom)
        sum_mom = jnp.sum(weight, axis=along, keepdims=True)
        return [max_on, sum_on, max_mom, sum_mom, jnp.sum(weight * on, axis=along, keepdims=True)]

    slot = lax.broadcasted_iota(jnp.int32, (2 * side, 128), 1)
    by_row = jnp.zeros((2 * side, 128), f32)
    for k, value in enumerate(stats(1)):
        by_row = jnp.where(slot == k, value, by_row)
    by_row = by_row.T[:8]
    for peer in range(n_plane):
        row_ref[peer] = by_row
    own = jnp.sum(jnp.where(diagonal_of(pos_ref), on, 0.0), axis=0, keepdims=True)
    slot = lax.broadcasted_iota(jnp.int32, (8, 2 * side), 0)
    by_col = jnp.zeros((8, 2 * side), f32)
    for k, value in enumerate(stats(0) + [own]):
        by_col = jnp.where(slot == k, value, by_col)
    col_ref[...] = by_col


def combine(got):
    max_on, sum_on, max_mom, sum_mom, cross = (got[:, k : k + 1] for k in range(5))
    top_on = jnp.max(max_on, axis=0)
    lse_on = top_on + jnp.log(jnp.sum(sum_on * jnp.exp(max_on - top_on), axis=0))
    top_mom = jnp.max(max_mom, axis=0)
    rescale = jnp.exp(max_mom - top_mom)
    total = jnp.sum(sum_mom * rescale, axis=0)
    return lse_on, top_mom + jnp.log(total), lse_on - mix_weight * jnp.sum(cross * rescale, axis=0) / total


def row_kernel(got_ref, col_ref, lse_ref, send_ref):
    lse_on, lse_mom, loss = combine(got_ref[...])
    slot = lax.broadcasted_iota(jnp.int32, (128, 2 * side), 0)
    lse_ref[...] = jnp.where(slot == 0, lse_on, lse_mom).T
    slot = lax.broadcasted_iota(jnp.int32, (8, 2 * side), 0)
    send = jnp.where(slot == 6, jnp.sum(loss), col_ref[...])
    for peer in range(n_column):
        send_ref[peer] = send


def grad_kernel(pos_ref, on_ref, mom_ref, lse_ref, got_ref, mine_ref, other_ref, text_ref, out_ref, keep_ref, send_ref):
    width = text_ref.shape[-1]
    got = got_ref[...]
    col_on, col_mom, loss = combine(got)
    loss = loss - 2.0 * (1.0 - mix_weight) * jnp.sum(got[:, 5:6], axis=0)
    _, valid_row = lanes(1)
    row_total = jnp.sum(jnp.sum(got[:, 6:7], axis=0)[:, :1])
    share_of_loss = jnp.sum(jnp.where(valid_row, loss, 0.0)) + row_total / n_plane

    _, valid = lanes(2 * side)
    on, mom = on_ref[...], mom_ref[...]
    row_on, row_mom = lse_ref[:, 0:1], lse_ref[:, 1:2]
    delta = jnp.where(diagonal_of(pos_ref), 1.0 - mix_weight, 0.0)
    target_row = mix_weight * jnp.exp(mom - row_mom) + delta
    target_col = mix_weight * jnp.exp(mom - col_mom) + delta
    grad = 0.5 * ((jnp.exp(on - row_on) - target_row) + (jnp.exp(on - col_on) - target_col))
    grad = jnp.where(valid, grad, 0.0)
    first = pos_ref[2] == 0
    low, high = grad[:side], grad[side:]
    mine, other = jnp.where(first, low, high), jnp.where(first, high, low)
    texts = text_ref[...].reshape(2 * side, width)

    def down(part, ref):
        part = part.reshape(16, 1, rows, 2 * side)
        part = jnp.concatenate([part, jnp.zeros_like(part)], axis=1).reshape(2 * side, 2 * side)
        return lax.dot_general(
            part.astype(bf16), ref[...].reshape(2 * side, width), (((0,), (0,)), ((), ())), preferred_element_type=f32
        )

    by_text = down(mine, mine_ref) + down(other, other_ref)
    out_ref[...] = by_text.reshape(16, 2, rows, width)[:, 0]
    for part, ref in ((mine, keep_ref), (other, send_ref)):
        ref[:, :width] = jnp.dot(part.astype(bf16), texts, preferred_element_type=f32)
        ref[:, width:] = jnp.full((side, 128), share_of_loss, f32)


def local(image, text, mimage, mtext):
    width = image.shape[1]
    pos = jnp.stack([lax.axis_index(a) for a in ("x", "y", "c", "zh", "zl")] + [0] * 3).astype(jnp.int32)

    def swap(block):
        return lax.ppermute(block, "c", [(0, 1), (1, 0)])

    sent, pair = call(
        pack_kernel, [shape(n_column, 16, width, dtype=bf16), shape(16, width, dtype=bf16)], text, mtext, image, mimage
    )
    texts = lax.all_to_all(sent, column, 0, 0, tiled=True)
    mine = lax.all_gather(lax.all_gather(pair, "x"), "y").reshape(16, 16, width)
    other = swap(mine)

    on, mom, row_parts, col_parts = call(
        score_kernel,
        [shape(256, 256), shape(256, 256), shape(n_plane, 8, 256), shape(8, 256)],
        pos, mine, other, texts,
        flops=2**28, exps=2**18,
    )
    row_got = lax.all_to_all(row_parts, ("x", "y", "c"), 0, 0, tiled=True)
    row_lse, col_sent = call(row_kernel, [shape(256, 128), shape(n_column, 8, 256)], row_got, col_parts, exps=2**14)
    col_got = lax.all_to_all(col_sent, column, 0, 0, tiled=True)

    by_text, keep, send = call(
        grad_kernel,
        [shape(n_column, rows, width), shape(side, width + 128), shape(side, width + 128)],
        pos, on, mom, row_lse, col_got, mine, other, texts,
        flops=2**29, exps=2**18,
    )
    got_text = lax.all_to_all(by_text, column, 0, 0, tiled=True)
    by_image = (keep + swap(send)).reshape(16, rows, width + 128)
    by_image, got_text = lax.optimization_barrier((by_image, got_text))
    grad_text = jnp.sum(got_text, axis=0)
    got_image = lax.all_to_all(by_image, ("y", "x"), 0, 0, tiled=True)
    grad_image = jnp.sum(got_image[:, :, :width], axis=0)
    loss = jnp.sum(got_image[:, 0, width]) / (2.0 * rows * n_plane * n_column)
    return grad_image, grad_text, loss


def solution(mesh):
    fine = Mesh(mesh.devices.reshape(8, 4, 2, 4, 2), ("zl", "y", "zh", "x", "c"))
    by_image = P(("zh", "x", "c", "zl", "y"), None)
    by_text = P(("zl", "y", "zh", "x", "c"), None)
    return jax.shard_map(
        local,
        mesh=fine,
        in_specs=(by_image, by_text, by_image, by_text),
        out_specs=(by_image, by_text, P()),
        check_vma=False,
    )
```

```python
import jax
import jax.numpy as jnp
from jax import lax
from jax.experimental import pallas as pl
from jax.experimental.pallas import tpu as pltpu
from jax.sharding import Mesh, PartitionSpec as P

mix_weight = 0.4
very_low = -1e30
column = ("zh", "zl")
n_plane, n_column, rows = 32, 16, 8
f32, bf16 = jnp.float32, jnp.bfloat16
side = 16 * rows


def call(body, outs, *args, flops=0, exps=0, **more):
    whole = pl.BlockSpec(memory_space=pltpu.VMEM)
    specs = [pl.BlockSpec(memory_space=pltpu.SMEM) if a.dtype == jnp.int32 else whole for a in args]
    moved = sum(a.size * a.dtype.itemsize for a in list(args) + outs)
    params = dict(in_specs=specs, out_specs=[whole] * len(outs))
    params.update(more)
    return pl.pallas_call(
        body,
        out_shape=outs,
        cost_estimate=pl.CostEstimate(flops=flops, bytes_accessed=moved, transcendentals=exps),
        compiler_params=pltpu.CompilerParams(vmem_limit_bytes=40 * 2**20),
        **params,
    )(*args)


def shape(*dims, dtype=f32):
    return jax.ShapeDtypeStruct(dims, dtype)


def pack_kernel(text_ref, mtext_ref, image_ref, mimage_ref, send_ref, pair_ref, held, sems):
    loads = [
        pltpu.make_async_copy(ref, held.at[k], sems.at[k])
        for k, ref in enumerate((text_ref, mtext_ref, image_ref, mimage_ref))
    ]
    for load in loads:
        load.start()
    for load in loads:
        load.wait()

    def pair(k):
        return jnp.concatenate([held[k].astype(f32), held[k + 1].astype(f32)], axis=0).astype(bf16)

    both = pair(0)
    for peer in range(n_column):
        send_ref[peer] = both
    pair_ref[...] = pair(2)


def lanes(height):
    lane = lax.broadcasted_iota(jnp.int32, (height, 2 * side), 1)
    return lane, (lane & rows) == 0


def diagonal_of(pos_ref):
    x, y, c, zh, zl = (pos_ref[k] for k in range(5))
    row = lax.broadcasted_iota(jnp.int32, (2 * side, 2 * side), 0)
    lane, valid = lanes(2 * side)
    pc, py, px = row >> 7, (row >> 5) & 3, (row >> 3) & 3
    image_block = (zh * 8 + px * 2 + pc) * 32 + zl * 4 + py
    qh, ql = lane >> 7, (lane >> 4) & 7
    text_block = (ql * 4 + y) * 16 + qh * 8 + x * 2 + c
    return valid & (image_block == text_block) & ((row & 7) == (lane & 7))


def score_kernel(pos_ref, mine_ref, other_ref, text_ref, on_ref, mom_ref, row_ref, col_ref):
    width = text_ref.shape[-1]
    texts = text_ref[...].reshape(2 * side, width)

    def product(ref):
        out = lax.dot_general(
            ref[...].reshape(2 * side, width), texts, (((1,), (1,)), ((), ())), preferred_element_type=f32
        )
        return (out * width ** (-0.5)).reshape(16, 2, rows, 2 * side)

    mine, other = product(mine_ref), product(other_ref)
    first = pos_ref[2] == 0
    low, high = jnp.where(first, mine, other), jnp.where(first, other, mine)
    _, valid = lanes(2 * side)

    def both(which):
        return jnp.concatenate([part[:, which].reshape(side, 2 * side) for part in (low, high)], axis=0)

    on = jnp.where(valid, both(0), very_low)
    mom = jnp.where(valid, pltpu.roll(both(1), 2 * side - rows, 1), very_low)
    on_ref[...] = on
    mom_ref[...] = mom

    def stats(along):
        max_on = jnp.max(on, axis=along, keepdims=True)
        sum_on = jnp.sum(jnp.exp(on - max_on), axis=along, keepdims=True)
        max_mom = jnp.max(mom, axis=along, keepdims=True)
        weight = jnp.exp(mom - max_mom)
        sum_mom = jnp.sum(weight, axis=along, keepdims=True)
        mean = jnp.sum(weight * on, axis=along, keepdims=True) / sum_mom
        return [max_on + jnp.log(sum_on), max_mom + jnp.log(sum_mom), mean]

    slot = lax.broadcasted_iota(jnp.int32, (2 * side, 128), 1)
    by_row = jnp.zeros((2 * side, 128), f32)
    for k, value in enumerate(stats(1)):
        by_row = jnp.where(slot == k, value, by_row)
    by_row = by_row.T[:8]
    slot = lax.broadcasted_iota(jnp.int32, (8, side), 0)
    by_row = jnp.where(slot < 4, by_row[:, :side], pltpu.roll(by_row[:, side:], 4, 0))
    for peer in range(n_plane):
        row_ref[peer] = by_row
    own = jnp.sum(jnp.where(diagonal_of(pos_ref), on, 0.0), axis=0, keepdims=True)
    slot = lax.broadcasted_iota(jnp.int32, (8, 2 * side), 0)
    by_col = jnp.zeros((8, 2 * side), f32)
    for k, value in enumerate(stats(0) + [own]):
        by_col = jnp.where(slot == k, value, by_col)
    lane = lax.broadcasted_iota(jnp.int32, (8, side), 1)
    col_ref[...] = jnp.where((lane & rows) == 0, by_col[:, :side], pltpu.roll(by_col[:, side:], rows, 1))


def combine(got):
    top = jnp.max(got, axis=0)
    spread = jnp.exp(got - top[None])
    total = jnp.sum(spread, axis=0)
    lse = top + jnp.log(total)
    weight = pltpu.roll(spread, 1, 1)
    mean = jnp.sum(weight * got, axis=0) / pltpu.roll(total, 1, 0)
    return lse, mean


def row_kernel(got_ref, col_ref, lse_ref, send_ref):
    lse, mean = combine(got_ref[...])
    slot = lax.broadcasted_iota(jnp.int32, (8, side), 0)
    loss = jnp.sum(jnp.where((slot & 3) == 0, lse, jnp.where((slot & 3) == 2, -mix_weight * mean, 0.0)))
    lse_ref[...] = jnp.concatenate([lse] + [jnp.zeros((8, side), f32)] * 15, axis=0).T
    send = jnp.where(slot == 4, loss, col_ref[...])
    for peer in range(n_column):
        send_ref[peer] = send


def grad_kernel(
    pos_ref, on_ref, mom_ref, lse_ref, got_ref, mine_ref, other_ref, text_ref, out_ref, keep_ref, send_ref
):
    width = text_ref.shape[-1]
    got = got_ref[...]
    lse, mean = combine(got)
    sums = jnp.sum(got, axis=0)
    slot = lax.broadcasted_iota(jnp.int32, (8, side), 0)
    loss = jnp.where(slot == 3, -2.0 * (1.0 - mix_weight) * sums, 0.0)
    loss = jnp.where(slot == 0, lse, jnp.where(slot == 2, -mix_weight * mean, loss))
    loss = jnp.where(slot == 4, sums * (1.0 / (n_plane * side)), loss)
    share_of_loss = jnp.sum(loss)

    _, valid = lanes(2 * side)
    on, mom = on_ref[...], mom_ref[...]

    def spread(row):
        return jnp.concatenate([row, pltpu.roll(row, side - rows, 1)], axis=1)

    both = spread(lse)
    col_on, col_mom = both[0:1], both[1:2]
    row_on = jnp.concatenate([lse_ref[:, 0:1], lse_ref[:, 4:5]], axis=0)
    row_mom = jnp.concatenate([lse_ref[:, 1:2], lse_ref[:, 5:6]], axis=0)
    delta = jnp.where(diagonal_of(pos_ref), 1.0 - mix_weight, 0.0)
    target_row = mix_weight * jnp.exp(mom - row_mom) + delta
    target_col = mix_weight * jnp.exp(mom - col_mom) + delta
    grad = 0.5 * ((jnp.exp(on - row_on) - target_row) + (jnp.exp(on - col_on) - target_col))
    grad = jnp.where(valid, grad, 0.0)
    first = pos_ref[2] == 0
    low, high = grad[:side], grad[side:]
    mine, other = jnp.where(first, low, high), jnp.where(first, high, low)
    texts = text_ref[...].reshape(2 * side, width)

    def down(part, ref):
        part = part.reshape(16, 1, rows, 2 * side)
        part = jnp.concatenate([part, jnp.zeros_like(part)], axis=1).reshape(2 * side, 2 * side)
        return lax.dot_general(
            part.astype(bf16), ref[...].reshape(2 * side, width), (((0,), (0,)), ((), ())), preferred_element_type=f32
        )

    by_text = down(mine, mine_ref) + down(other, other_ref)
    out_ref[...] = by_text.reshape(16, 2, rows, width)[:, 0]
    for part, ref in ((mine, keep_ref), (other, send_ref)):
        ref[:, :width] = jnp.dot(part.astype(bf16), texts, preferred_element_type=f32)
        ref[:, width:] = jnp.full((side, 128), share_of_loss, f32)


def core_kernel(pos_ref, keep_ref, got_ref, own_ref, *send_refs):
    for k, ref in enumerate((own_ref,) + send_refs):
        at = pl.ds(pl.multiple_of(((pos_ref[1] + k) & 3) * 32, 32), 32)
        ref[...] = keep_ref[at, :] + got_ref[at, :]


def y_kernel(pos_ref, keep_ref, a_ref, b_ref, c_ref, own_ref, *send_refs):
    for k, ref in enumerate((own_ref,) + send_refs):
        at = pl.ds(pl.multiple_of(((pos_ref[0] + k) & 3) * rows, rows), rows)
        ref[...] = (keep_ref[at, :] + a_ref[at, :]) + (b_ref[at, :] + c_ref[at, :])


def x_kernel(keep_ref, a_ref, b_ref, c_ref, grad_ref, loss_ref):
    total = (keep_ref[...] + a_ref[...]) + (b_ref[...] + c_ref[...])
    width = grad_ref.shape[1]
    grad_ref[...] = total[:, :width]
    loss_ref[...] = total[:, width:] * (1.0 / (2.0 * rows * n_plane * n_column))


def local(image, text, mimage, mtext):
    width = image.shape[1]
    wide = width + 128
    pos = jnp.stack([lax.axis_index(a) for a in ("x", "y", "c", "zh", "zl")] + [0] * 3).astype(jnp.int32)

    def swap(block):
        return lax.ppermute(block, "c", [(0, 1), (1, 0)])

    def ahead(blocks, axis):
        return [lax.ppermute(block, axis, [(i, (i + k) % 4) for i in range(4)]) for k, block in enumerate(blocks, 1)]

    sent, pair = call(
        pack_kernel, [shape(n_column, 16, width, dtype=bf16), shape(16, width, dtype=bf16)], text, mtext, image, mimage,
        in_specs=[pl.BlockSpec(memory_space=pltpu.HBM)] * 4,
        scratch_shapes=[pltpu.VMEM((4, rows, width), bf16), pltpu.SemaphoreType.DMA((4,))],
    )
    texts = lax.all_to_all(sent, column, 0, 0, tiled=True)
    mine = lax.all_gather(lax.all_gather(pair, "x"), "y").reshape(16, 16, width)
    other = swap(mine)

    on, mom, row_parts, col_parts = call(
        score_kernel,
        [shape(256, 256), shape(256, 256), shape(n_plane, 8, side), shape(8, side)],
        pos, mine, other, texts,
        flops=2**28, exps=2**18,
    )
    row_got = lax.all_to_all(row_parts, ("x", "y", "c"), 0, 0, tiled=True)
    row_lse, col_sent = call(row_kernel, [shape(side, side), shape(n_column, 8, side)], row_got, col_parts, exps=2**14)
    col_got = lax.all_to_all(col_sent, column, 0, 0, tiled=True)

    by_text, keep, send = call(
        grad_kernel,
        [shape(n_column, rows, width), shape(side, wide), shape(side, wide)],
        pos, on, mom, row_lse, col_got, mine, other, texts,
        flops=2**29, exps=2**18,
    )
    got_text = lax.all_to_all(by_text, column, 0, 0, tiled=True)
    keep, *send = call(core_kernel, [shape(32, wide)] * 4, pos, keep, swap(send))
    keep, *send = call(y_kernel, [shape(rows, wide)] * 4, pos, keep, *ahead(send, "y"))
    grad_image, loss = call(x_kernel, [shape(rows, width), shape(rows, 128)], keep, *ahead(send, "x"))
    grad_text = jnp.sum(got_text, axis=0)
    return grad_image, grad_text, loss[0, 0]


def solution(mesh):
    fine = Mesh(mesh.devices.reshape(8, 4, 2, 4, 2), ("zl", "y", "zh", "x", "c"))
    by_image = P(("zh", "x", "c", "zl", "y"), None)
    by_text = P(("zl", "y", "zh", "x", "c"), None)
    return jax.shard_map(
        local,
        mesh=fine,
        in_specs=(by_image, by_text, by_image, by_text),
        out_specs=(by_image, by_text, P()),
        check_vma=False,
    )
```

```python
import jax
import jax.numpy as jnp
from jax import lax
from jax.experimental import pallas as pl
from jax.experimental.pallas import tpu as pltpu
from jax.sharding import Mesh, PartitionSpec as P

mix_weight = 0.4
very_low = -1e30
column = ("zh", "zl")
n_plane, n_column, rows = 32, 16, 8
f32, bf16 = jnp.float32, jnp.bfloat16
side = 16 * rows


def call(body, outs, *args, flops=0, exps=0, **more):
    whole = pl.BlockSpec(memory_space=pltpu.VMEM)
    specs = [pl.BlockSpec(memory_space=pltpu.SMEM) if a.dtype == jnp.int32 else whole for a in args]
    moved = sum(a.size * a.dtype.itemsize for a in list(args) + outs)
    params = dict(in_specs=specs, out_specs=[whole] * len(outs))
    params.update(more)
    return pl.pallas_call(
        body,
        out_shape=outs,
        cost_estimate=pl.CostEstimate(flops=flops, bytes_accessed=moved, transcendentals=exps),
        compiler_params=pltpu.CompilerParams(vmem_limit_bytes=40 * 2**20),
        **params,
    )(*args)


def shape(*dims, dtype=f32):
    return jax.ShapeDtypeStruct(dims, dtype)


def lanes(height):
    lane = lax.broadcasted_iota(jnp.int32, (height, 2 * side), 1)
    return lane, (lane & rows) == 0


def diagonal_of(pos_ref):
    x, y, c, zh, zl = (pos_ref[k] for k in range(5))
    row = lax.broadcasted_iota(jnp.int32, (2 * side, 2 * side), 0)
    lane, valid = lanes(2 * side)
    pc, py, px = row >> 7, (row >> 5) & 3, (row >> 3) & 3
    image_block = (zh * 8 + px * 2 + pc) * 32 + zl * 4 + py
    qh, ql = lane >> 7, (lane >> 4) & 7
    text_block = (ql * 4 + y) * 16 + qh * 8 + x * 2 + c
    return valid & (image_block == text_block) & ((row & 7) == (lane & 7))


def score_kernel(pos_ref, mine_ref, other_ref, text_ref, on_ref, mom_ref, row_ref, col_ref):
    width = text_ref.shape[-1]
    texts = text_ref[...].reshape(2 * side, width)

    def product(ref):
        out = lax.dot_general(
            ref[...].reshape(2 * side, width), texts, (((1,), (1,)), ((), ())), preferred_element_type=f32
        )
        return (out * width ** (-0.5)).reshape(16, 2, rows, 2 * side)

    mine, other = product(mine_ref), product(other_ref)
    first = pos_ref[2] == 0
    low, high = jnp.where(first, mine, other), jnp.where(first, other, mine)
    _, valid = lanes(2 * side)

    def both(which):
        return jnp.concatenate([part[:, which].reshape(side, 2 * side) for part in (low, high)], axis=0)

    on = jnp.where(valid, both(0), very_low)
    mom = jnp.where(valid, pltpu.roll(both(1), 2 * side - rows, 1), very_low)
    on_ref[...] = on
    mom_ref[...] = mom

    def stats(along):
        max_on = jnp.max(on, axis=along, keepdims=True)
        sum_on = jnp.sum(jnp.exp(on - max_on), axis=along, keepdims=True)
        max_mom = jnp.max(mom, axis=along, keepdims=True)
        weight = jnp.exp(mom - max_mom)
        sum_mom = jnp.sum(weight, axis=along, keepdims=True)
        mean = jnp.sum(weight * on, axis=along, keepdims=True) / sum_mom
        return [max_on + jnp.log(sum_on), max_mom + jnp.log(sum_mom), mean]

    slot = lax.broadcasted_iota(jnp.int32, (2 * side, 128), 1)
    by_row = jnp.zeros((2 * side, 128), f32)
    for k, value in enumerate(stats(1)):
        by_row = jnp.where(slot == k, value, by_row)
    by_row = by_row.T[:8]
    slot = lax.broadcasted_iota(jnp.int32, (8, side), 0)
    by_row = jnp.where(slot < 4, by_row[:, :side], pltpu.roll(by_row[:, side:], 4, 0))
    for peer in range(n_plane):
        row_ref[peer] = by_row
    own = jnp.sum(jnp.where(diagonal_of(pos_ref), on, 0.0), axis=0, keepdims=True)
    slot = lax.broadcasted_iota(jnp.int32, (8, 2 * side), 0)
    by_col = jnp.zeros((8, 2 * side), f32)
    for k, value in enumerate(stats(0) + [own]):
        by_col = jnp.where(slot == k, value, by_col)
    lane = lax.broadcasted_iota(jnp.int32, (8, side), 1)
    col_ref[...] = jnp.where((lane & rows) == 0, by_col[:, :side], pltpu.roll(by_col[:, side:], rows, 1))


def combine(got):
    top = jnp.max(got, axis=0)
    spread = jnp.exp(got - top[None])
    total = jnp.sum(spread, axis=0)
    lse = top + jnp.log(total)
    weight = pltpu.roll(spread, 1, 1)
    mean = jnp.sum(weight * got, axis=0) / pltpu.roll(total, 1, 0)
    return lse, mean


def row_kernel(got_ref, col_ref, lse_ref, send_ref):
    lse, mean = combine(got_ref[...])
    slot = lax.broadcasted_iota(jnp.int32, (8, side), 0)
    loss = jnp.sum(jnp.where((slot & 3) == 0, lse, jnp.where((slot & 3) == 2, -mix_weight * mean, 0.0)))
    lse_ref[...] = jnp.concatenate([lse] + [jnp.zeros((8, side), f32)] * 15, axis=0).T
    send = jnp.where(slot == 4, loss, col_ref[...])
    for peer in range(n_column):
        send_ref[peer] = send


def grad_kernel(
    pos_ref, on_ref, mom_ref, lse_ref, got_ref, mine_ref, other_ref, text_ref, out_ref, keep_ref, send_ref
):
    width = text_ref.shape[-1]
    got = got_ref[...]
    lse, mean = combine(got)
    sums = jnp.sum(got, axis=0)
    slot = lax.broadcasted_iota(jnp.int32, (8, side), 0)
    loss = jnp.where(slot == 3, -2.0 * (1.0 - mix_weight) * sums, 0.0)
    loss = jnp.where(slot == 0, lse, jnp.where(slot == 2, -mix_weight * mean, loss))
    loss = jnp.where(slot == 4, sums * (1.0 / (n_plane * side)), loss)
    share_of_loss = jnp.sum(loss)

    _, valid = lanes(2 * side)
    on, mom = on_ref[...], mom_ref[...]

    def spread(row):
        return jnp.concatenate([row, pltpu.roll(row, side - rows, 1)], axis=1)

    both = spread(lse)
    col_on, col_mom = both[0:1], both[1:2]
    row_on = jnp.concatenate([lse_ref[:, 0:1], lse_ref[:, 4:5]], axis=0)
    row_mom = jnp.concatenate([lse_ref[:, 1:2], lse_ref[:, 5:6]], axis=0)
    delta = jnp.where(diagonal_of(pos_ref), 1.0 - mix_weight, 0.0)
    target_row = mix_weight * jnp.exp(mom - row_mom) + delta
    target_col = mix_weight * jnp.exp(mom - col_mom) + delta
    grad = 0.5 * ((jnp.exp(on - row_on) - target_row) + (jnp.exp(on - col_on) - target_col))
    grad = jnp.where(valid, grad, 0.0)
    first = pos_ref[2] == 0
    low, high = grad[:side], grad[side:]
    mine, other = jnp.where(first, low, high), jnp.where(first, high, low)
    texts = text_ref[...].reshape(2 * side, width)

    def down(part, ref):
        part = part.reshape(16, 1, rows, 2 * side)
        part = jnp.concatenate([part, jnp.zeros_like(part)], axis=1).reshape(2 * side, 2 * side)
        return lax.dot_general(
            part.astype(bf16), ref[...].reshape(2 * side, width), (((0,), (0,)), ((), ())), preferred_element_type=f32
        )

    by_text = down(mine, mine_ref) + down(other, other_ref)
    out_ref[...] = by_text.reshape(16, 2, rows, width)[:, 0].astype(bf16)
    for part, ref in ((mine, keep_ref), (other, send_ref)):
        ref[:, :width] = jnp.dot(part.astype(bf16), texts, preferred_element_type=f32)
        ref[:, width:] = jnp.full((side, 128), share_of_loss, f32)


def core_kernel(keep_ref, got_ref, out_ref):
    total = keep_ref[...] + got_ref[...]
    width = total.shape[1] - 128
    loss = total[:, width:]
    lane = lax.broadcasted_iota(jnp.int32, loss.shape, 1)
    pieces = jnp.zeros_like(loss)
    for k in range(3):
        piece = loss.astype(bf16).astype(f32)
        pieces = jnp.where(lane == k, piece, pieces)
        loss = loss - piece
    out_ref[:, :, :width] = total[:, :width].reshape(16, rows, width).astype(bf16)
    out_ref[:, :, width:] = pieces.reshape(16, rows, 128).astype(bf16)


def last_kernel(got_ref, grad_ref, loss_ref):
    total = jnp.sum(got_ref[...].astype(f32), axis=0)
    width = grad_ref.shape[1]
    grad_ref[...] = total[:, :width]
    loss_ref[0, 0] = jnp.sum(total[:1, width:]) * (1.0 / (2.0 * rows * n_plane * n_column))


def local(image, text, mimage, mtext):
    width = image.shape[1]
    wide = width + 128
    pos = jnp.stack([lax.axis_index(a) for a in ("x", "y", "c", "zh", "zl")] + [0] * 3).astype(jnp.int32)

    def swap(block):
        return lax.ppermute(block, "c", [(0, 1), (1, 0)])

    both = jnp.concatenate([text, mtext], axis=0)
    sent = jnp.broadcast_to(both[None], (n_column,) + both.shape)
    pair = jnp.concatenate([image, mimage], axis=0)
    texts = lax.all_to_all(sent, column, 0, 0, tiled=True)
    mine = lax.all_gather(lax.all_gather(pair, "x"), "y").reshape(16, 16, width)
    other = swap(mine)

    on, mom, row_parts, col_parts = call(
        score_kernel,
        [shape(256, 256), shape(256, 256), shape(n_plane, 8, side), shape(8, side)],
        pos, mine, other, texts,
        flops=2**28, exps=2**18,
    )
    row_got = lax.all_to_all(row_parts, ("x", "y", "c"), 0, 0, tiled=True)
    row_lse, col_sent = call(row_kernel, [shape(side, side), shape(n_column, 8, side)], row_got, col_parts, exps=2**14)
    col_got = lax.all_to_all(col_sent, column, 0, 0, tiled=True)

    by_text, keep, send = call(
        grad_kernel,
        [shape(n_column, rows, width, dtype=bf16), shape(side, wide), shape(side, wide)],
        pos, on, mom, row_lse, col_got, mine, other, texts,
        flops=2**29, exps=2**18,
    )
    got_text = lax.all_to_all(by_text, column, 0, 0, tiled=True)
    (by_image,) = call(core_kernel, [shape(16, rows, wide, dtype=bf16)], keep, swap(send))
    by_image, got_text = lax.optimization_barrier((by_image, got_text))
    got_image = lax.all_to_all(by_image, ("y", "x"), 0, 0, tiled=True)
    grad_text = jnp.sum(got_text.astype(f32), axis=0)
    grad_image, loss = call(
        last_kernel, [shape(rows, width), shape(1, 1)], got_image,
        out_specs=[pl.BlockSpec(memory_space=pltpu.VMEM), pl.BlockSpec(memory_space=pltpu.SMEM)],
    )
    return grad_image, grad_text, loss[0, 0]


def solution(mesh):
    fine = Mesh(mesh.devices.reshape(8, 4, 2, 4, 2), ("zl", "y", "zh", "x", "c"))
    by_image = P(("zh", "x", "c", "zl", "y"), None)
    by_text = P(("zl", "y", "zh", "x", "c"), None)
    return jax.shard_map(
        local,
        mesh=fine,
        in_specs=(by_image, by_text, by_image, by_text),
        out_specs=(by_image, by_text, P()),
        check_vma=False,
    )
```

```python
import jax
import jax.numpy as jnp
from jax import lax
from jax.experimental import pallas as pl
from jax.experimental.pallas import tpu as pltpu
from jax.sharding import Mesh, PartitionSpec as P

mix_weight = 0.4
very_low = -1e30
column = ("zh", "zl")
n_plane, n_column, rows = 32, 16, 8
f32, bf16 = jnp.float32, jnp.bfloat16
side = 16 * rows


def call(body, outs, *args, flops=0, exps=0, **more):
    whole = pl.BlockSpec(memory_space=pltpu.VMEM)
    specs = [pl.BlockSpec(memory_space=pltpu.SMEM) if a.dtype == jnp.int32 else whole for a in args]
    moved = sum(a.size * a.dtype.itemsize for a in list(args) + outs)
    params = dict(in_specs=specs, out_specs=[whole] * len(outs))
    params.update(more)
    return pl.pallas_call(
        body,
        out_shape=outs,
        cost_estimate=pl.CostEstimate(flops=flops, bytes_accessed=moved, transcendentals=exps),
        compiler_params=pltpu.CompilerParams(vmem_limit_bytes=40 * 2**20),
        **params,
    )(*args)


def shape(*dims, dtype=f32):
    return jax.ShapeDtypeStruct(dims, dtype)


def lanes(height):
    lane = lax.broadcasted_iota(jnp.int32, (height, 2 * side), 1)
    return lane, (lane & rows) == 0


def diagonal_of(pos_ref):
    x, y, c, zh, zl = (pos_ref[k] for k in range(5))
    row = lax.broadcasted_iota(jnp.int32, (2 * side, 2 * side), 0)
    lane, valid = lanes(2 * side)
    pc, py, px = row >> 7, (row >> 5) & 3, (row >> 3) & 3
    image_block = (zh * 8 + px * 2 + pc) * 32 + zl * 4 + py
    qh, ql = lane >> 7, (lane >> 4) & 7
    text_block = (ql * 4 + y) * 16 + qh * 8 + x * 2 + c
    return valid & (image_block == text_block) & ((row & 7) == (lane & 7))


def score_kernel(pos_ref, mine_ref, other_ref, text_ref, on_ref, mom_ref, row_ref, col_ref):
    width = text_ref.shape[-1]
    texts = text_ref[...].reshape(2 * side, width)

    def product(ref):
        out = lax.dot_general(
            ref[...].reshape(2 * side, width), texts, (((1,), (1,)), ((), ())), preferred_element_type=f32
        )
        return (out * width ** (-0.5)).reshape(16, 2, rows, 2 * side)

    mine, other = product(mine_ref), product(other_ref)
    first = pos_ref[2] == 0
    low, high = jnp.where(first, mine, other), jnp.where(first, other, mine)
    _, valid = lanes(2 * side)

    def both(which):
        return jnp.concatenate([part[:, which].reshape(side, 2 * side) for part in (low, high)], axis=0)

    on = jnp.where(valid, both(0), very_low)
    mom = jnp.where(valid, pltpu.roll(both(1), 2 * side - rows, 1), very_low)
    on_ref[...] = on
    mom_ref[...] = mom

    def stats(along):
        max_on = jnp.max(on, axis=along, keepdims=True)
        sum_on = jnp.sum(jnp.exp(on - max_on), axis=along, keepdims=True)
        max_mom = jnp.max(mom, axis=along, keepdims=True)
        weight = jnp.exp(mom - max_mom)
        sum_mom = jnp.sum(weight, axis=along, keepdims=True)
        mean = jnp.sum(weight * on, axis=along, keepdims=True) / sum_mom
        return [max_on + jnp.log(sum_on), max_mom + jnp.log(sum_mom), mean]

    slot = lax.broadcasted_iota(jnp.int32, (2 * side, 128), 1)
    by_row = jnp.zeros((2 * side, 128), f32)
    for k, value in enumerate(stats(1)):
        by_row = jnp.where(slot == k, value, by_row)
    by_row = by_row.T[:8]
    slot = lax.broadcasted_iota(jnp.int32, (8, side), 0)
    by_row = jnp.where(slot < 4, by_row[:, :side], pltpu.roll(by_row[:, side:], 4, 0))
    for peer in range(n_plane):
        row_ref[peer] = by_row
    own = jnp.sum(jnp.where(diagonal_of(pos_ref), on, 0.0), axis=0, keepdims=True)
    slot = lax.broadcasted_iota(jnp.int32, (8, 2 * side), 0)
    by_col = jnp.zeros((8, 2 * side), f32)
    for k, value in enumerate(stats(0) + [own]):
        by_col = jnp.where(slot == k, value, by_col)
    lane = lax.broadcasted_iota(jnp.int32, (8, side), 1)
    col_ref[...] = jnp.where((lane & rows) == 0, by_col[:, :side], pltpu.roll(by_col[:, side:], rows, 1))


def combine(got):
    top = jnp.max(got, axis=0)
    spread = jnp.exp(got - top[None])
    total = jnp.sum(spread, axis=0)
    lse = top + jnp.log(total)
    weight = pltpu.roll(spread, 1, 1)
    mean = jnp.sum(weight * got, axis=0) / pltpu.roll(total, 1, 0)
    return lse, mean


def row_kernel(got_ref, col_ref, lse_ref, send_ref):
    lse, mean = combine(got_ref[...])
    slot = lax.broadcasted_iota(jnp.int32, (8, side), 0)
    loss = jnp.sum(jnp.where((slot & 3) == 0, lse, jnp.where((slot & 3) == 2, -mix_weight * mean, 0.0)))
    lse_ref[...] = jnp.concatenate([lse] + [jnp.zeros((8, side), f32)] * 15, axis=0).T
    send = jnp.where(slot == 4, loss, col_ref[...])
    for peer in range(n_column):
        send_ref[peer] = send


def grad_kernel(
    pos_ref, on_ref, mom_ref, lse_ref, got_ref, mine_ref, other_ref, text_ref, out_ref, keep_ref, send_ref
):
    width = text_ref.shape[-1]
    got = got_ref[...]
    lse, mean = combine(got)
    sums = jnp.sum(got, axis=0)
    slot = lax.broadcasted_iota(jnp.int32, (8, side), 0)
    loss = jnp.where(slot == 3, -2.0 * (1.0 - mix_weight) * sums, 0.0)
    loss = jnp.where(slot == 0, lse, jnp.where(slot == 2, -mix_weight * mean, loss))
    loss = jnp.where(slot == 4, sums * (1.0 / (n_plane * side)), loss)
    share_of_loss = jnp.sum(loss)

    _, valid = lanes(2 * side)
    on, mom = on_ref[...], mom_ref[...]

    def spread(row):
        return jnp.concatenate([row, pltpu.roll(row, side - rows, 1)], axis=1)

    both = spread(lse)
    col_on, col_mom = both[0:1], both[1:2]
    row_on = jnp.concatenate([lse_ref[:, 0:1], lse_ref[:, 4:5]], axis=0)
    row_mom = jnp.concatenate([lse_ref[:, 1:2], lse_ref[:, 5:6]], axis=0)
    delta = jnp.where(diagonal_of(pos_ref), 1.0 - mix_weight, 0.0)
    target_row = mix_weight * jnp.exp(mom - row_mom) + delta
    target_col = mix_weight * jnp.exp(mom - col_mom) + delta
    grad = 0.5 * ((jnp.exp(on - row_on) - target_row) + (jnp.exp(on - col_on) - target_col))
    grad = jnp.where(valid, grad, 0.0)
    first = pos_ref[2] == 0
    low, high = grad[:side], grad[side:]
    mine, other = jnp.where(first, low, high), jnp.where(first, high, low)
    texts = text_ref[...].reshape(2 * side, width)

    lane = lax.broadcasted_iota(jnp.int32, (side, side), 1)

    def down(part, ref):
        part = jnp.where((lane & rows) == 0, part[:, :side], pltpu.roll(part[:, side:], rows, 1))
        part = part.reshape(16, 1, rows, side)
        part = jnp.concatenate([part, jnp.zeros_like(part)], axis=1).reshape(2 * side, side)
        return lax.dot_general(
            part.astype(bf16), ref[...].reshape(2 * side, width), (((0,), (0,)), ((), ())), preferred_element_type=f32
        )

    by_text = (down(mine, mine_ref) + down(other, other_ref)).reshape(8, 2, rows, width)
    for k in range(2):
        out_ref[8 * k : 8 * k + 8] = by_text[:, k].astype(bf16)
    for part, ref in ((mine, keep_ref), (other, send_ref)):
        ref[:, :width] = jnp.dot(part.astype(bf16), texts, preferred_element_type=f32)
        ref[:, width:] = jnp.full((side, 128), share_of_loss, f32)


def core_kernel(keep_ref, got_ref, out_ref):
    total = keep_ref[...] + got_ref[...]
    width = total.shape[1] - 128
    loss = total[:, width:]
    lane = lax.broadcasted_iota(jnp.int32, loss.shape, 1)
    pieces = jnp.zeros_like(loss)
    for k in range(3):
        piece = loss.astype(bf16).astype(f32)
        pieces = jnp.where(lane == k, piece, pieces)
        loss = loss - piece
    out_ref[:, :, :width] = total[:, :width].reshape(16, rows, width).astype(bf16)
    out_ref[:, :, width:] = pieces.reshape(16, rows, 128).astype(bf16)


def last_kernel(got_ref, grad_ref, loss_ref):
    total = jnp.sum(got_ref[...].astype(f32), axis=0)
    width = grad_ref.shape[1]
    grad_ref[...] = total[:, :width]
    loss_ref[0, 0] = jnp.sum(total[:1, width:]) * (1.0 / (2.0 * rows * n_plane * n_column))


def local(image, text, mimage, mtext):
    width = image.shape[1]
    wide = width + 128
    pos = jnp.stack([lax.axis_index(a) for a in ("x", "y", "c", "zh", "zl")] + [0] * 3).astype(jnp.int32)

    def swap(block):
        return lax.ppermute(block, "c", [(0, 1), (1, 0)])

    both = jnp.concatenate([text, mtext], axis=0)
    sent = jnp.broadcast_to(both[None], (n_column,) + both.shape)
    pair = jnp.concatenate([image, mimage], axis=0)
    texts = lax.all_to_all(sent, column, 0, 0, tiled=True)
    mine = lax.all_gather(pair, ("y", "x"))
    other = swap(mine)

    on, mom, row_parts, col_parts = call(
        score_kernel,
        [shape(256, 256), shape(256, 256), shape(n_plane, 8, side), shape(8, side)],
        pos, mine, other, texts,
        flops=2**28, exps=2**18,
    )
    row_got = lax.all_to_all(row_parts, ("x", "y", "c"), 0, 0, tiled=True)
    row_lse, col_sent = call(row_kernel, [shape(side, side), shape(n_column, 8, side)], row_got, col_parts, exps=2**14)
    col_got = lax.all_to_all(col_sent, column, 0, 0, tiled=True)

    by_text, keep, send = call(
        grad_kernel,
        [shape(n_column, rows, width, dtype=bf16), shape(side, wide), shape(side, wide)],
        pos, on, mom, row_lse, col_got, mine, other, texts,
        flops=2**29, exps=2**18,
    )
    got_text = lax.all_to_all(by_text, column, 0, 0, tiled=True)
    (by_image,) = call(core_kernel, [shape(16, rows, wide, dtype=bf16)], keep, swap(send))
    by_image, got_text = lax.optimization_barrier((by_image, got_text))
    got_image = lax.all_to_all(by_image, ("y", "x"), 0, 0, tiled=True)
    grad_text = jnp.sum(got_text.astype(f32), axis=0)
    grad_image, loss = call(
        last_kernel, [shape(rows, width), shape(1, 1)], got_image,
        out_specs=[pl.BlockSpec(memory_space=pltpu.VMEM), pl.BlockSpec(memory_space=pltpu.SMEM)],
    )
    return grad_image, grad_text, loss[0, 0]


def solution(mesh):
    fine = Mesh(mesh.devices.reshape(8, 4, 2, 4, 2), ("zl", "y", "zh", "x", "c"))
    by_image = P(("zh", "x", "c", "zl", "y"), None)
    by_text = P(("zl", "y", "zh", "x", "c"), None)
    return jax.shard_map(
        local,
        mesh=fine,
        in_specs=(by_image, by_text, by_image, by_text),
        out_specs=(by_image, by_text, P()),
        check_vma=False,
    )
```

```python
import jax
import jax.numpy as jnp
from jax import lax
from jax.experimental import pallas as pl
from jax.experimental.pallas import tpu as pltpu
from jax.sharding import Mesh, PartitionSpec as P

mix_weight = 0.4
very_low = -1e30
column = ("zh", "zl")
n_plane, n_column, rows = 32, 16, 8
f32, bf16 = jnp.float32, jnp.bfloat16
side = 16 * rows


def call(body, outs, *args, flops=0, exps=0, **more):
    whole = pl.BlockSpec(memory_space=pltpu.VMEM)
    specs = [pl.BlockSpec(memory_space=pltpu.SMEM) if a.dtype == jnp.int32 else whole for a in args]
    moved = sum(a.size * a.dtype.itemsize for a in list(args) + outs)
    params = dict(in_specs=specs, out_specs=[whole] * len(outs))
    params.update(more)
    return pl.pallas_call(
        body,
        out_shape=outs,
        cost_estimate=pl.CostEstimate(flops=flops, bytes_accessed=moved, transcendentals=exps),
        compiler_params=pltpu.CompilerParams(vmem_limit_bytes=40 * 2**20),
        **params,
    )(*args)


def shape(*dims, dtype=f32):
    return jax.ShapeDtypeStruct(dims, dtype)


def lanes(height):
    lane = lax.broadcasted_iota(jnp.int32, (height, 2 * side), 1)
    return lane, (lane & rows) == 0


def diagonal_of(pos_ref):
    x, y, c, zh, zl = (pos_ref[k] for k in range(5))
    row = lax.broadcasted_iota(jnp.int32, (2 * side, 2 * side), 0)
    lane, valid = lanes(2 * side)
    pc, px = row >> 7, (row >> 4) & 3
    py = ((row >> 3) & 1) * 2 + ((row >> 6) & 1)
    image_block = (zh * 8 + px * 2 + pc) * 32 + zl * 4 + py
    qh, ql = lane >> 7, (lane >> 4) & 7
    text_block = (ql * 4 + y) * 16 + qh * 8 + x * 2 + c
    return valid & (image_block == text_block) & ((row & 7) == (lane & 7))


def order_kernel(pos_ref, own_ref, other_ref, out_ref):
    place = pos_ref[1] >> 1
    out_ref[place] = own_ref[...]
    out_ref[1 - place] = other_ref[...]


def score_kernel(pos_ref, mine_ref, other_ref, text_ref, on_ref, mom_ref, row_ref, col_ref):
    width = text_ref.shape[-1]
    texts = text_ref[...].reshape(2 * side, width)

    def product(ref):
        out = lax.dot_general(
            ref[...].reshape(2 * side, width), texts, (((1,), (1,)), ((), ())), preferred_element_type=f32
        )
        return (out * width ** (-0.5)).reshape(16, 2, rows, 2 * side)

    mine, other = product(mine_ref), product(other_ref)
    first = pos_ref[2] == 0
    low, high = jnp.where(first, mine, other), jnp.where(first, other, mine)
    _, valid = lanes(2 * side)

    def both(which):
        return jnp.concatenate([part[:, which].reshape(side, 2 * side) for part in (low, high)], axis=0)

    on = jnp.where(valid, both(0), very_low)
    mom = jnp.where(valid, pltpu.roll(both(1), 2 * side - rows, 1), very_low)
    on_ref[...] = on
    mom_ref[...] = mom

    def stats(along):
        max_on = jnp.max(on, axis=along, keepdims=True)
        sum_on = jnp.sum(jnp.exp(on - max_on), axis=along, keepdims=True)
        max_mom = jnp.max(mom, axis=along, keepdims=True)
        weight = jnp.exp(mom - max_mom)
        sum_mom = jnp.sum(weight, axis=along, keepdims=True)
        mean = jnp.sum(weight * on, axis=along, keepdims=True) / sum_mom
        return [max_on + jnp.log(sum_on), max_mom + jnp.log(sum_mom), mean]

    slot = lax.broadcasted_iota(jnp.int32, (2 * side, 128), 1)
    by_row = jnp.zeros((2 * side, 128), f32)
    for k, value in enumerate(stats(1)):
        by_row = jnp.where(slot == k, value, by_row)
    by_row = by_row.T[:8]
    slot = lax.broadcasted_iota(jnp.int32, (8, side), 0)
    by_row = jnp.where(slot < 4, by_row[:, :side], pltpu.roll(by_row[:, side:], 4, 0))
    for peer in range(n_plane):
        row_ref[peer] = by_row
    own = jnp.sum(jnp.where(diagonal_of(pos_ref), on, 0.0), axis=0, keepdims=True)
    slot = lax.broadcasted_iota(jnp.int32, (8, 2 * side), 0)
    by_col = jnp.zeros((8, 2 * side), f32)
    for k, value in enumerate(stats(0) + [own]):
        by_col = jnp.where(slot == k, value, by_col)
    lane = lax.broadcasted_iota(jnp.int32, (8, side), 1)
    col_ref[...] = jnp.where((lane & rows) == 0, by_col[:, :side], pltpu.roll(by_col[:, side:], rows, 1))


def combine(got):
    top = jnp.max(got, axis=0)
    spread = jnp.exp(got - top[None])
    total = jnp.sum(spread, axis=0)
    lse = top + jnp.log(total)
    weight = pltpu.roll(spread, 1, 1)
    mean = jnp.sum(weight * got, axis=0) / pltpu.roll(total, 1, 0)
    return lse, mean


def row_kernel(got_ref, col_ref, lse_ref, send_ref):
    lse, mean = combine(got_ref[...])
    slot = lax.broadcasted_iota(jnp.int32, (8, side), 0)
    loss = jnp.sum(jnp.where((slot & 3) == 0, lse, jnp.where((slot & 3) == 2, -mix_weight * mean, 0.0)))
    lse_ref[...] = jnp.concatenate([lse] + [jnp.zeros((8, side), f32)] * 15, axis=0).T
    send = jnp.where(slot == 4, loss, col_ref[...])
    for peer in range(n_column):
        send_ref[peer] = send


def grad_kernel(
    pos_ref, on_ref, mom_ref, lse_ref, got_ref, mine_ref, other_ref, text_ref, out_ref, keep_ref, send_ref
):
    width = text_ref.shape[-1]
    got = got_ref[...]
    lse, mean = combine(got)
    sums = jnp.sum(got, axis=0)
    slot = lax.broadcasted_iota(jnp.int32, (8, side), 0)
    loss = jnp.where(slot == 3, -2.0 * (1.0 - mix_weight) * sums, 0.0)
    loss = jnp.where(slot == 0, lse, jnp.where(slot == 2, -mix_weight * mean, loss))
    loss = jnp.where(slot == 4, sums * (1.0 / (n_plane * side)), loss)
    share_of_loss = jnp.sum(loss)

    _, valid = lanes(2 * side)
    on, mom = on_ref[...], mom_ref[...]

    def spread(row):
        return jnp.concatenate([row, pltpu.roll(row, side - rows, 1)], axis=1)

    both = spread(lse)
    col_on, col_mom = both[0:1], both[1:2]
    row_on = jnp.concatenate([lse_ref[:, 0:1], lse_ref[:, 4:5]], axis=0)
    row_mom = jnp.concatenate([lse_ref[:, 1:2], lse_ref[:, 5:6]], axis=0)
    delta = jnp.where(diagonal_of(pos_ref), 1.0 - mix_weight, 0.0)
    target_row = mix_weight * jnp.exp(mom - row_mom) + delta
    target_col = mix_weight * jnp.exp(mom - col_mom) + delta
    grad = 0.5 * ((jnp.exp(on - row_on) - target_row) + (jnp.exp(on - col_on) - target_col))
    grad = jnp.where(valid, grad, 0.0)
    first = pos_ref[2] == 0
    low, high = grad[:side], grad[side:]
    mine, other = jnp.where(first, low, high), jnp.where(first, high, low)
    texts = text_ref[...].reshape(2 * side, width)

    lane = lax.broadcasted_iota(jnp.int32, (side, side), 1)

    def down(part, ref):
        part = jnp.where((lane & rows) == 0, part[:, :side], pltpu.roll(part[:, side:], rows, 1))
        part = part.reshape(16, 1, rows, side)
        part = jnp.concatenate([part, jnp.zeros_like(part)], axis=1).reshape(2 * side, side)
        return lax.dot_general(
            part.astype(bf16), ref[...].reshape(2 * side, width), (((0,), (0,)), ((), ())), preferred_element_type=f32
        )

    by_text = (down(mine, mine_ref) + down(other, other_ref)).reshape(8, 2, rows, width)
    for k in range(2):
        out_ref[8 * k : 8 * k + 8] = by_text[:, k].astype(bf16)
    for part, ref in ((mine, keep_ref), (other, send_ref)):
        ref[:, :width] = jnp.dot(part.astype(bf16), texts, preferred_element_type=f32)
        ref[:, width:] = jnp.full((side, 128), share_of_loss, f32)


def core_kernel(keep_ref, got_ref, out_ref):
    total = keep_ref[...] + got_ref[...]
    width = total.shape[1] - 128
    loss = total[:, width:]
    lane = lax.broadcasted_iota(jnp.int32, loss.shape, 1)
    pieces = jnp.zeros_like(loss)
    for k in range(3):
        piece = loss.astype(bf16).astype(f32)
        pieces = jnp.where(lane == k, piece, pieces)
        loss = loss - piece
    out_ref[:, :, :width] = total[:, :width].reshape(16, rows, width).astype(bf16)
    out_ref[:, :, width:] = pieces.reshape(16, rows, 128).astype(bf16)


def last_kernel(got_ref, grad_ref, loss_ref):
    total = jnp.sum(got_ref[...].astype(f32), axis=0)
    width = grad_ref.shape[1]
    grad_ref[...] = total[:, :width]
    loss_ref[0, 0] = jnp.sum(total[:1, width:]) * (1.0 / (2.0 * rows * n_plane * n_column))


def local(image, text, mimage, mtext):
    width = image.shape[1]
    wide = width + 128
    x, yh, yl, c, zh, zl = (lax.axis_index(a) for a in ("x", "yh", "yl", "c", "zh", "zl"))
    pos = jnp.stack([x, yh * 2 + yl, c, zh, zl, 0, 0, 0]).astype(jnp.int32)

    def swap(block, axis="c"):
        return lax.ppermute(block, axis, [(0, 1), (1, 0)])

    both = jnp.concatenate([text, mtext], axis=0)
    pair = jnp.concatenate([image, mimage], axis=0)
    both, pair = lax.optimization_barrier((both, pair))
    sent = jnp.broadcast_to(both[None], (n_column,) + both.shape)
    texts = lax.all_to_all(sent, column, 0, 0, tiled=True)
    across = swap(pair, "yh")
    (pair,) = call(order_kernel, [shape(2, 16, width, dtype=bf16)], pos, pair, across, flops=2**35)
    mine = lax.all_gather(pair, ("yl", "x")).reshape(16, 16, width)
    other = swap(mine)

    on, mom, row_parts, col_parts = call(
        score_kernel,
        [shape(256, 256), shape(256, 256), shape(n_plane, 8, side), shape(8, side)],
        pos, mine, other, texts,
        flops=2**28, exps=2**18,
    )
    row_got = lax.all_to_all(row_parts, ("x", "yh", "yl", "c"), 0, 0, tiled=True)
    row_lse, col_sent = call(row_kernel, [shape(side, side), shape(n_column, 8, side)], row_got, col_parts, exps=2**14)
    col_got = lax.all_to_all(col_sent, column, 0, 0, tiled=True)

    by_text, keep, send = call(
        grad_kernel,
        [shape(n_column, rows, width, dtype=bf16), shape(side, wide), shape(side, wide)],
        pos, on, mom, row_lse, col_got, mine, other, texts,
        flops=2**29, exps=2**18,
    )
    got_text = lax.all_to_all(by_text, column, 0, 0, tiled=True)
    (by_image,) = call(core_kernel, [shape(16, rows, wide, dtype=bf16)], keep, swap(send))
    by_image, got_text = lax.optimization_barrier((by_image, got_text))
    got_image = lax.all_to_all(by_image, ("yl", "x", "yh"), 0, 0, tiled=True)
    grad_text = jnp.sum(got_text.astype(f32), axis=0)
    grad_image, loss = call(
        last_kernel, [shape(rows, width), shape(1, 1)], got_image,
        out_specs=[pl.BlockSpec(memory_space=pltpu.VMEM), pl.BlockSpec(memory_space=pltpu.SMEM)],
    )
    return grad_image, grad_text, loss[0, 0]


def solution(mesh):
    fine = Mesh(mesh.devices.reshape(8, 2, 2, 2, 4, 2), ("zl", "yh", "yl", "zh", "x", "c"))
    by_image = P(("zh", "x", "c", "zl", "yh", "yl"), None)
    by_text = P(("zl", "yh", "yl", "zh", "x", "c"), None)
    return jax.shard_map(
        local,
        mesh=fine,
        in_specs=(by_image, by_text, by_image, by_text),
        out_specs=(by_image, by_text, P()),
        check_vma=False,
    )
```

```python
import jax
import jax.numpy as jnp
from jax import lax
from jax.experimental import pallas as pl
from jax.experimental.pallas import tpu as pltpu
from jax.sharding import Mesh, PartitionSpec as P

mix_weight = 0.4
very_low = -1e30
column = ("zh", "zl")
n_plane, n_column, rows = 32, 16, 8
f32, bf16 = jnp.float32, jnp.bfloat16
side = 16 * rows


def call(body, outs, *args, flops=0, exps=0, **more):
    whole = pl.BlockSpec(memory_space=pltpu.VMEM)
    specs = [pl.BlockSpec(memory_space=pltpu.SMEM) if a.dtype == jnp.int32 else whole for a in args]
    moved = sum(a.size * a.dtype.itemsize for a in list(args) + outs)
    params = dict(in_specs=specs, out_specs=[whole] * len(outs))
    params.update(more)
    return pl.pallas_call(
        body,
        out_shape=outs,
        cost_estimate=pl.CostEstimate(flops=flops, bytes_accessed=moved, transcendentals=exps),
        compiler_params=pltpu.CompilerParams(vmem_limit_bytes=40 * 2**20),
        **params,
    )(*args)


def shape(*dims, dtype=f32):
    return jax.ShapeDtypeStruct(dims, dtype)


def first_half(height):
    return (lax.broadcasted_iota(jnp.int32, (height, side), 1) & rows) == 0


def diagonal_of(pos_ref):
    x, y, c, zh, zl = (pos_ref[k] for k in range(5))
    row = lax.broadcasted_iota(jnp.int32, (2 * side, 1), 0)
    pc, px, py = row >> 7, (row >> 5) & 3, ((row >> 3) & 1) * 2 + ((row >> 4) & 1)
    image = ((zh * 8 + px * 2 + pc) * 32 + zl * 4 + py) * rows + (row & 7)
    lane = lax.broadcasted_iota(jnp.int32, (1, side), 1)
    qh, ql = (lane >> 3) & 1, lane >> 4
    text = ((ql * 4 + y) * 16 + qh * 8 + x * 2 + c) * rows + (lane & 7)
    return image == text


def order_kernel(pos_ref, own_ref, other_ref, out_ref):
    place = pos_ref[0]
    out_ref[place] = own_ref[...]
    out_ref[1 - place] = other_ref[...]


def score_kernel(pos_ref, mine_ref, other_ref, text_ref, on_ref, mom_ref, row_ref, col_ref):
    width = text_ref.shape[-1]
    texts = text_ref[...].reshape(2 * side, width)

    def product(ref):
        out = lax.dot_general(
            ref[...].reshape(2 * side, width), texts, (((1,), (1,)), ((), ())), preferred_element_type=f32
        )
        return (out * width ** (-0.5)).reshape(16, 2, rows, 2 * side)

    mine, other = product(mine_ref), product(other_ref)
    first = pos_ref[2] == 0
    low, high = jnp.where(first, mine, other), jnp.where(first, other, mine)
    packed = first_half(2 * side)

    def both(which):
        whole = jnp.concatenate([part[:, which].reshape(side, 2 * side) for part in (low, high)], axis=0)
        return whole[:, :side], whole[:, side:]

    left, right = both(0)
    on = jnp.where(packed, left, pltpu.roll(right, rows, 1))
    left, right = both(1)
    mom = jnp.where(packed, pltpu.roll(left, side - rows, 1), right)
    on_ref[...] = on
    mom_ref[...] = mom

    def stats(along):
        max_on = jnp.max(on, axis=along, keepdims=True)
        sum_on = jnp.sum(jnp.exp(on - max_on), axis=along, keepdims=True)
        max_mom = jnp.max(mom, axis=along, keepdims=True)
        weight = jnp.exp(mom - max_mom)
        sum_mom = jnp.sum(weight, axis=along, keepdims=True)
        mean = jnp.sum(weight * on, axis=along, keepdims=True) / sum_mom
        return [max_on + jnp.log(sum_on), max_mom + jnp.log(sum_mom), mean]

    slot = lax.broadcasted_iota(jnp.int32, (2 * side, 128), 1)
    by_row = jnp.zeros((2 * side, 128), f32)
    for k, value in enumerate(stats(1)):
        by_row = jnp.where(slot == k, value, by_row)
    by_row = by_row.T[:8]
    slot = lax.broadcasted_iota(jnp.int32, (8, side), 0)
    by_row = jnp.where(slot < 4, by_row[:, :side], pltpu.roll(by_row[:, side:], 4, 0))
    for peer in range(n_plane):
        row_ref[peer] = by_row
    own = jnp.sum(jnp.where(diagonal_of(pos_ref), on, 0.0), axis=0, keepdims=True)
    slot = lax.broadcasted_iota(jnp.int32, (8, side), 0)
    by_col = jnp.zeros((8, side), f32)
    for k, value in enumerate(stats(0) + [own]):
        by_col = jnp.where(slot == k, value, by_col)
    col_ref[...] = by_col


def combine(got):
    top = jnp.max(got, axis=0)
    spread = jnp.exp(got - top[None])
    total = jnp.sum(spread, axis=0)
    lse = top + jnp.log(total)
    weight = pltpu.roll(spread, 1, 1)
    mean = jnp.sum(weight * got, axis=0) / pltpu.roll(total, 1, 0)
    return lse, mean


def row_kernel(got_ref, col_ref, lse_ref, send_ref):
    lse, mean = combine(got_ref[...])
    slot = lax.broadcasted_iota(jnp.int32, (8, side), 0)
    loss = jnp.sum(jnp.where((slot & 3) == 0, lse, jnp.where((slot & 3) == 2, -mix_weight * mean, 0.0)))
    lse_ref[...] = jnp.concatenate([lse] + [jnp.zeros((8, side), f32)] * 15, axis=0).T
    send = jnp.where(slot == 4, loss, col_ref[...])
    for peer in range(n_column):
        send_ref[peer] = send


def grad_kernel(
    pos_ref, on_ref, mom_ref, lse_ref, got_ref, mine_ref, other_ref, text_ref, out_ref, keep_ref, send_ref
):
    width = text_ref.shape[-1]
    got = got_ref[...]
    lse, mean = combine(got)
    sums = jnp.sum(got, axis=0)
    slot = lax.broadcasted_iota(jnp.int32, (8, side), 0)
    loss = jnp.where(slot == 3, -2.0 * (1.0 - mix_weight) * sums, 0.0)
    loss = jnp.where(slot == 0, lse, jnp.where(slot == 2, -mix_weight * mean, loss))
    loss = jnp.where(slot == 4, sums * (1.0 / (n_plane * side)), loss)
    share_of_loss = jnp.sum(loss)

    on, mom = on_ref[...], mom_ref[...]
    col_on, col_mom = lse[0:1], lse[1:2]
    row_on = jnp.concatenate([lse_ref[:, 0:1], lse_ref[:, 4:5]], axis=0)
    row_mom = jnp.concatenate([lse_ref[:, 1:2], lse_ref[:, 5:6]], axis=0)
    delta = jnp.where(diagonal_of(pos_ref), 1.0 - mix_weight, 0.0)
    target_row = mix_weight * jnp.exp(mom - row_mom) + delta
    target_col = mix_weight * jnp.exp(mom - col_mom) + delta
    grad = 0.5 * ((jnp.exp(on - row_on) - target_row) + (jnp.exp(on - col_on) - target_col))
    first = pos_ref[2] == 0
    low, high = grad[:side], grad[side:]
    mine, other = jnp.where(first, low, high), jnp.where(first, high, low)
    texts = text_ref[...].reshape(2 * side, width)

    def down(part, ref):
        part = part.reshape(16, 1, rows, side)
        part = jnp.concatenate([part, jnp.zeros_like(part)], axis=1).reshape(2 * side, side)
        return lax.dot_general(
            part.astype(bf16), ref[...].reshape(2 * side, width), (((0,), (0,)), ((), ())), preferred_element_type=f32
        )

    by_text = (down(mine, mine_ref) + down(other, other_ref)).reshape(8, 2, rows, width)
    for k in range(2):
        out_ref[8 * k : 8 * k + 8] = by_text[:, k].astype(bf16)
    packed = first_half(side)
    for part, ref in ((mine, keep_ref), (other, send_ref)):
        halves = [jnp.where(packed, half, 0.0) for half in (part, pltpu.roll(part, side - rows, 1))]
        part = jnp.concatenate(halves, axis=1)
        ref[:, :width] = jnp.dot(part.astype(bf16), texts, preferred_element_type=f32)
        ref[:, width:] = jnp.full((side, 128), share_of_loss, f32)


def core_kernel(keep_ref, got_ref, out_ref):
    total = keep_ref[...] + got_ref[...]
    width = total.shape[1] - 128
    loss = total[:, width:]
    lane = lax.broadcasted_iota(jnp.int32, loss.shape, 1)
    pieces = jnp.zeros_like(loss)
    for k in range(3):
        piece = loss.astype(bf16).astype(f32)
        pieces = jnp.where(lane == k, piece, pieces)
        loss = loss - piece
    out_ref[:, :, :width] = total[:, :width].reshape(16, rows, width).astype(bf16)
    out_ref[:, :, width:] = pieces.reshape(16, rows, 128).astype(bf16)


def last_kernel(got_ref, grad_ref, loss_ref):
    total = jnp.sum(got_ref[...].astype(f32), axis=0)
    width = grad_ref.shape[1]
    grad_ref[...] = total[:, :width]
    loss_ref[0, 0] = jnp.sum(total[:1, width:]) * (1.0 / (2.0 * rows * n_plane * n_column))


def local(image, text, mimage, mtext):
    width = image.shape[1]
    wide = width + 128
    x, yh, yl, c, zh, zl = (lax.axis_index(a).astype(jnp.int32) for a in ("x", "yh", "yl", "c", "zh", "zl"))
    pos = jnp.stack([x, yh * 2 + yl, c, zh, zl, 0, 0, 0])
    yh, yl = yh[None], yl[None]

    def swap(block, axis="c"):
        return lax.ppermute(block, axis, [(0, 1), (1, 0)])

    both = jnp.concatenate([text, mtext], axis=0)
    pair = jnp.concatenate([image, mimage], axis=0)
    both, pair = lax.optimization_barrier((both, pair))
    sent = jnp.broadcast_to(both[None], (n_column,) + both.shape)
    texts = lax.all_to_all(sent, column, 0, 0, tiled=True)
    across = swap(pair, "yh")
    (pair,) = call(order_kernel, [shape(2, 16, width, dtype=bf16)], yh, pair, across, flops=2**35)
    (pair,) = call(order_kernel, [shape(2, 2, 16, width, dtype=bf16)], yl, pair, swap(pair, "yl"))
    mine = lax.all_gather(pair, "x").reshape(16, 16, width)
    other = swap(mine)

    on, mom, row_parts, col_parts = call(
        score_kernel,
        [shape(2 * side, side), shape(2 * side, side), shape(n_plane, 8, side), shape(8, side)],
        pos, mine, other, texts,
        flops=2**28, exps=2**18,
    )
    row_got = lax.all_to_all(row_parts, ("x", "yh", "yl", "c"), 0, 0, tiled=True)
    row_lse, col_sent = call(row_kernel, [shape(side, side), shape(n_column, 8, side)], row_got, col_parts, exps=2**14)
    col_got = lax.all_to_all(col_sent, column, 0, 0, tiled=True)

    by_text, keep, send = call(
        grad_kernel,
        [shape(n_column, rows, width, dtype=bf16), shape(side, wide), shape(side, wide)],
        pos, on, mom, row_lse, col_got, mine, other, texts,
        flops=2**29, exps=2**18,
    )
    got_text = lax.all_to_all(by_text, column, 0, 0, tiled=True)
    (by_image,) = call(core_kernel, [shape(16, rows, wide, dtype=bf16)], keep, swap(send))
    by_image, got_text = lax.optimization_barrier((by_image, got_text))
    got_image = lax.all_to_all(by_image, ("x", "yl", "yh"), 0, 0, tiled=True)
    grad_text = jnp.sum(got_text.astype(f32), axis=0)
    grad_image, loss = call(
        last_kernel, [shape(rows, width), shape(1, 1)], got_image,
        out_specs=[pl.BlockSpec(memory_space=pltpu.VMEM), pl.BlockSpec(memory_space=pltpu.SMEM)],
    )
    return grad_image, grad_text, loss[0, 0]


def solution(mesh):
    fine = Mesh(mesh.devices.reshape(8, 2, 2, 2, 4, 2), ("zl", "yh", "yl", "zh", "x", "c"))
    by_image = P(("zh", "x", "c", "zl", "yh", "yl"), None)
    by_text = P(("zl", "yh", "yl", "zh", "x", "c"), None)
    return jax.shard_map(
        local,
        mesh=fine,
        in_specs=(by_image, by_text, by_image, by_text),
        out_specs=(by_image, by_text, P()),
        check_vma=False,
    )
```

```python
import jax
import jax.numpy as jnp
from jax import lax
from jax.experimental import pallas as pl
from jax.experimental.pallas import tpu as pltpu
from jax.sharding import Mesh, PartitionSpec as P

mix_weight = 0.4
very_low = -1e30
column = ("zh", "zl")
n_plane, n_column, rows = 32, 16, 8
f32, bf16 = jnp.float32, jnp.bfloat16
side = 16 * rows


def call(body, outs, *args, flops=0, exps=0, **more):
    whole = pl.BlockSpec(memory_space=pltpu.VMEM)
    specs = [pl.BlockSpec(memory_space=pltpu.SMEM) if a.dtype == jnp.int32 else whole for a in args]
    moved = sum(a.size * a.dtype.itemsize for a in list(args) + outs)
    params = dict(in_specs=specs, out_specs=[whole] * len(outs))
    params.update(more)
    return pl.pallas_call(
        body,
        out_shape=outs,
        cost_estimate=pl.CostEstimate(flops=flops, bytes_accessed=moved, transcendentals=exps),
        compiler_params=pltpu.CompilerParams(vmem_limit_bytes=40 * 2**20),
        **params,
    )(*args)


def shape(*dims, dtype=f32):
    return jax.ShapeDtypeStruct(dims, dtype)


def first_half(height):
    return (lax.broadcasted_iota(jnp.int32, (height, side), 1) & rows) == 0


def diagonal_of(pos_ref):
    x, y, c, zh, zl = (pos_ref[k] for k in range(5))
    row = lax.broadcasted_iota(jnp.int32, (2 * side, 1), 0)
    pc, px, py = row >> 7, (row >> 5) & 3, ((row >> 3) & 1) * 2 + ((row >> 4) & 1)
    image = ((zh * 8 + px * 2 + pc) * 32 + zl * 4 + py) * rows + (row & 7)
    lane = lax.broadcasted_iota(jnp.int32, (1, side), 1)
    qh, ql = (lane >> 3) & 1, lane >> 4
    text = ((ql * 4 + y) * 16 + qh * 8 + x * 2 + c) * rows + (lane & 7)
    return image == text


def order_kernel(pos_ref, own_ref, other_ref, out_ref):
    place = pos_ref[0]
    out_ref[place] = own_ref[...]
    out_ref[1 - place] = other_ref[...]


def score_kernel(pos_ref, mine_ref, other_ref, text_ref, on_ref, mom_ref, row_ref, col_ref):
    width = text_ref.shape[-1]
    texts = text_ref[...].reshape(2 * side, width)

    def product(ref):
        out = lax.dot_general(
            ref[...].reshape(2 * side, width), texts, (((1,), (1,)), ((), ())), preferred_element_type=f32
        )
        return (out * width ** (-0.5)).reshape(16, 2, rows, 2 * side)

    mine, other = product(mine_ref), product(other_ref)
    first = pos_ref[2] == 0
    low, high = jnp.where(first, mine, other), jnp.where(first, other, mine)
    packed = first_half(2 * side)

    def both(which):
        whole = jnp.concatenate([part[:, which].reshape(side, 2 * side) for part in (low, high)], axis=0)
        return whole[:, :side], whole[:, side:]

    left, right = both(0)
    on = jnp.where(packed, left, pltpu.roll(right, rows, 1))
    left, right = both(1)
    mom = jnp.where(packed, pltpu.roll(left, side - rows, 1), right)
    on_ref[...] = on
    mom_ref[...] = mom

    def stats(along):
        max_on = jnp.max(on, axis=along, keepdims=True)
        sum_on = jnp.sum(jnp.exp(on - max_on), axis=along, keepdims=True)
        max_mom = jnp.max(mom, axis=along, keepdims=True)
        weight = jnp.exp(mom - max_mom)
        sum_mom = jnp.sum(weight, axis=along, keepdims=True)
        mean = jnp.sum(weight * on, axis=along, keepdims=True) / sum_mom
        return [max_on + jnp.log(sum_on), max_mom + jnp.log(sum_mom), mean]

    slot = lax.broadcasted_iota(jnp.int32, (2 * side, 128), 1)
    by_row = jnp.zeros((2 * side, 128), f32)
    for k, value in enumerate(stats(1)):
        by_row = jnp.where(slot == k, value, by_row)
    by_row = by_row.T[:8]
    slot = lax.broadcasted_iota(jnp.int32, (8, side), 0)
    by_row = jnp.where(slot < 4, by_row[:, :side], pltpu.roll(by_row[:, side:], 4, 0))
    for peer in range(n_plane):
        row_ref[peer] = by_row
    own = jnp.sum(jnp.where(diagonal_of(pos_ref), on, 0.0), axis=0, keepdims=True)
    slot = lax.broadcasted_iota(jnp.int32, (8, side), 0)
    by_col = jnp.zeros((8, side), f32)
    for k, value in enumerate(stats(0) + [own]):
        by_col = jnp.where(slot == k, value, by_col)
    col_ref[...] = by_col


def combine(got):
    top = jnp.max(got, axis=0)
    spread = jnp.exp(got - top[None])
    total = jnp.sum(spread, axis=0)
    lse = top + jnp.log(total)
    weight = pltpu.roll(spread, 1, 1)
    mean = jnp.sum(weight * got, axis=0) / pltpu.roll(total, 1, 0)
    return lse, mean


def row_kernel(got_ref, col_ref, lse_ref, send_ref):
    lse, mean = combine(got_ref[...])
    slot = lax.broadcasted_iota(jnp.int32, (8, side), 0)
    loss = jnp.sum(jnp.where((slot & 3) == 0, lse, jnp.where((slot & 3) == 2, -mix_weight * mean, 0.0)))
    lse_ref[...] = jnp.concatenate([lse] + [jnp.zeros((8, side), f32)] * 15, axis=0).T
    send = jnp.where(slot == 4, loss, col_ref[...])
    for peer in range(n_column):
        send_ref[peer] = send


def grad_kernel(
    pos_ref, on_ref, mom_ref, lse_ref, got_ref, mine_ref, other_ref, text_ref, out_ref, keep_ref, send_ref
):
    width = text_ref.shape[-1]
    got = got_ref[...]
    lse, mean = combine(got)
    sums = jnp.sum(got, axis=0)
    slot = lax.broadcasted_iota(jnp.int32, (8, side), 0)
    loss = jnp.where(slot == 3, -2.0 * (1.0 - mix_weight) * sums, 0.0)
    loss = jnp.where(slot == 0, lse, jnp.where(slot == 2, -mix_weight * mean, loss))
    loss = jnp.where(slot == 4, sums * (1.0 / (n_plane * side)), loss)
    share_of_loss = jnp.sum(loss)

    on, mom = on_ref[...], mom_ref[...]
    col_on, col_mom = lse[0:1], lse[1:2]
    row_on = jnp.concatenate([lse_ref[:, 0:1], lse_ref[:, 4:5]], axis=0)
    row_mom = jnp.concatenate([lse_ref[:, 1:2], lse_ref[:, 5:6]], axis=0)
    delta = jnp.where(diagonal_of(pos_ref), 1.0 - mix_weight, 0.0)
    target_row = mix_weight * jnp.exp(mom - row_mom) + delta
    target_col = mix_weight * jnp.exp(mom - col_mom) + delta
    grad = 0.5 * ((jnp.exp(on - row_on) - target_row) + (jnp.exp(on - col_on) - target_col))
    first = pos_ref[2] == 0
    low, high = grad[:side], grad[side:]
    mine, other = jnp.where(first, low, high), jnp.where(first, high, low)
    texts = text_ref[...].reshape(2 * side, width)

    def down(part, ref):
        part = part.reshape(16, 1, rows, side)
        part = jnp.concatenate([part, jnp.zeros_like(part)], axis=1).reshape(2 * side, side)
        return lax.dot_general(
            part.astype(bf16), ref[...].reshape(2 * side, width), (((0,), (0,)), ((), ())), preferred_element_type=f32
        )

    by_text = (down(mine, mine_ref) + down(other, other_ref)).reshape(8, 2, rows, width)
    for k in range(2):
        out_ref[8 * k : 8 * k + 8] = by_text[:, k].astype(bf16)
    packed = first_half(side)
    for part, ref in ((mine, keep_ref), (other, send_ref)):
        halves = [jnp.where(packed, half, 0.0) for half in (part, pltpu.roll(part, side - rows, 1))]
        part = jnp.concatenate(halves, axis=1)
        ref[:, :width] = jnp.dot(part.astype(bf16), texts, preferred_element_type=f32)
        ref[:, width:] = jnp.full((side, 128), share_of_loss, f32)


def core_kernel(keep_ref, got_ref, out_ref):
    total = keep_ref[...] + got_ref[...]
    width = total.shape[1] - 128
    loss = total[:, width:]
    lane = lax.broadcasted_iota(jnp.int32, loss.shape, 1)
    pieces = jnp.zeros_like(loss)
    for k in range(3):
        piece = loss.astype(bf16).astype(f32)
        pieces = jnp.where(lane == k, piece, pieces)
        loss = loss - piece
    out_ref[:, :, :width] = total[:, :width].reshape(16, rows, width).astype(bf16)
    out_ref[:, :, width:] = pieces.reshape(16, rows, 128).astype(bf16)


def last_kernel(image_ref, text_ref, grad_image_ref, grad_text_ref, loss_ref):
    total = jnp.sum(image_ref[...].astype(f32), axis=0)
    width = grad_image_ref.shape[1]
    grad_image_ref[...] = total[:, :width]
    grad_text_ref[...] = jnp.sum(text_ref[...].astype(f32), axis=0)
    loss_ref[0, 0] = jnp.sum(total[:1, width:]) * (1.0 / (2.0 * rows * n_plane * n_column))


def local(image, text, mimage, mtext):
    width = image.shape[1]
    wide = width + 128
    x, yh, yl, c, zh, zl = (lax.axis_index(a).astype(jnp.int32) for a in ("x", "yh", "yl", "c", "zh", "zl"))
    pos = jnp.stack([x, yh * 2 + yl, c, zh, zl, 0, 0, 0])
    yh, yl = yh[None], yl[None]

    def swap(block, axis="c"):
        return lax.ppermute(block, axis, [(0, 1), (1, 0)])

    both = jnp.concatenate([text, mtext], axis=0)
    pair = jnp.concatenate([image, mimage], axis=0)
    both, pair = lax.optimization_barrier((both, pair))
    sent = jnp.broadcast_to(both[None], (n_column,) + both.shape)
    texts = lax.all_to_all(sent, column, 0, 0, tiled=True)
    across = swap(pair, "yh")
    (pair,) = call(order_kernel, [shape(2, 16, width, dtype=bf16)], yh, pair, across, flops=2**35)
    (pair,) = call(order_kernel, [shape(2, 2, 16, width, dtype=bf16)], yl, pair, swap(pair, "yl"))
    mine = lax.all_gather(pair, "x").reshape(16, 16, width)
    other = swap(mine)

    on, mom, row_parts, col_parts = call(
        score_kernel,
        [shape(2 * side, side), shape(2 * side, side), shape(n_plane, 8, side), shape(8, side)],
        pos, mine, other, texts,
        flops=2**28, exps=2**18,
    )
    row_got = lax.all_to_all(row_parts, ("x", "yh", "yl", "c"), 0, 0, tiled=True)
    row_lse, col_sent = call(row_kernel, [shape(side, side), shape(n_column, 8, side)], row_got, col_parts, exps=2**14)
    col_got = lax.all_to_all(col_sent, column, 0, 0, tiled=True)

    by_text, keep, send = call(
        grad_kernel,
        [shape(n_column, rows, width, dtype=bf16), shape(side, wide), shape(side, wide)],
        pos, on, mom, row_lse, col_got, mine, other, texts,
        flops=2**29, exps=2**18,
    )
    got = swap(send)
    got_text = lax.all_to_all(by_text, column, 0, 0, tiled=True)
    (by_image,) = call(core_kernel, [shape(16, rows, wide, dtype=bf16)], keep, got)
    by_image, got_text = lax.optimization_barrier((by_image, got_text))
    got_image = lax.all_to_all(by_image, ("x", "yl", "yh"), 0, 0, tiled=True)
    vmem = pl.BlockSpec(memory_space=pltpu.VMEM)
    grad_image, grad_text, loss = call(
        last_kernel, [shape(rows, width), shape(rows, width), shape(1, 1)], got_image, got_text,
        out_specs=[vmem, vmem, pl.BlockSpec(memory_space=pltpu.SMEM)],
    )
    return grad_image, grad_text, loss[0, 0]


def solution(mesh):
    fine = Mesh(mesh.devices.reshape(8, 2, 2, 2, 4, 2), ("zl", "yh", "yl", "zh", "x", "c"))
    by_image = P(("zh", "x", "c", "zl", "yh", "yl"), None)
    by_text = P(("zl", "yh", "yl", "zh", "x", "c"), None)
    return jax.shard_map(
        local,
        mesh=fine,
        in_specs=(by_image, by_text, by_image, by_text),
        out_specs=(by_image, by_text, P()),
        check_vma=False,
    )
```

```python
import jax
import jax.numpy as jnp
from jax import lax
from jax.experimental import pallas as pl
from jax.experimental.pallas import tpu as pltpu
from jax.sharding import Mesh, PartitionSpec as P

mix_weight = 0.4
very_low = -1e30
column = ("zq", "zh", "zp")
n_plane, n_column, rows = 32, 16, 8
f32, bf16 = jnp.float32, jnp.bfloat16
side = 16 * rows


def call(body, outs, *args, flops=0, exps=0, **more):
    whole = pl.BlockSpec(memory_space=pltpu.VMEM)
    specs = [pl.BlockSpec(memory_space=pltpu.SMEM) if a.dtype == jnp.int32 else whole for a in args]
    moved = sum(a.size * a.dtype.itemsize for a in list(args) + outs)
    params = dict(in_specs=specs, out_specs=[whole] * len(outs))
    params.update(more)
    return pl.pallas_call(
        body,
        out_shape=outs,
        cost_estimate=pl.CostEstimate(flops=flops, bytes_accessed=moved, transcendentals=exps),
        compiler_params=pltpu.CompilerParams(vmem_limit_bytes=40 * 2**20),
        **params,
    )(*args)


def shape(*dims, dtype=f32):
    return jax.ShapeDtypeStruct(dims, dtype)


def first_half(height):
    return (lax.broadcasted_iota(jnp.int32, (height, side), 1) & rows) == 0


def diagonal_of(pos_ref):
    x, y, c, zh, zl = (pos_ref[k] for k in range(5))
    row = lax.broadcasted_iota(jnp.int32, (2 * side, 1), 0)
    pc, py, px = row >> 7, (row >> 5) & 3, (row >> 3) & 3
    image = ((zh * 8 + px * 2 + pc) * 32 + zl * 4 + py) * rows + (row & 7)
    lane = lax.broadcasted_iota(jnp.int32, (1, side), 1)
    part = (lane >> 4) & 3
    qh, ql = part >> 1, (part & 1) * 4 + ((lane >> 3) & 1) * 2 + (lane >> 6)
    text = ((ql * 4 + y) * 16 + qh * 8 + x * 2 + c) * rows + (lane & 7)
    return image == text


def order_kernel(place_ref, *refs):
    for k, ref in enumerate(refs[:4]):
        refs[4][(place_ref[0] - k) & 3] = ref[...]


def score_kernel(
    pos_ref, mine_ref, other_ref, a_ref, b_ref, c_ref, d_ref, on_ref, mom_ref, row_ref, col_ref, text_ref
):
    width = text_ref.shape[-1]
    for k, ref in enumerate((a_ref, b_ref, c_ref, d_ref)):
        text_ref[(pos_ref[5] - k) & 3] = ref[...]
    texts = text_ref[...].reshape(2 * side, width)

    def product(ref):
        out = lax.dot_general(
            ref[...].reshape(2 * side, width), texts, (((1,), (1,)), ((), ())), preferred_element_type=f32
        )
        return (out * width ** (-0.5)).reshape(16, 2, rows, 2 * side)

    mine, other = product(mine_ref), product(other_ref)
    first = pos_ref[2] == 0
    low, high = jnp.where(first, mine, other), jnp.where(first, other, mine)
    packed = first_half(2 * side)

    def both(which):
        whole = jnp.concatenate([part[:, which].reshape(side, 2 * side) for part in (low, high)], axis=0)
        return whole[:, :side], whole[:, side:]

    left, right = both(0)
    on = jnp.where(packed, left, pltpu.roll(right, rows, 1))
    left, right = both(1)
    mom = jnp.where(packed, pltpu.roll(left, side - rows, 1), right)
    on_ref[...] = on
    mom_ref[...] = mom

    def stats(along):
        max_on = jnp.max(on, axis=along, keepdims=True)
        sum_on = jnp.sum(jnp.exp(on - max_on), axis=along, keepdims=True)
        max_mom = jnp.max(mom, axis=along, keepdims=True)
        weight = jnp.exp(mom - max_mom)
        sum_mom = jnp.sum(weight, axis=along, keepdims=True)
        mean = jnp.sum(weight * on, axis=along, keepdims=True) / sum_mom
        return [max_on + jnp.log(sum_on), max_mom + jnp.log(sum_mom), mean]

    slot = lax.broadcasted_iota(jnp.int32, (2 * side, 128), 1)
    by_row = jnp.zeros((2 * side, 128), f32)
    for k, value in enumerate(stats(1)):
        by_row = jnp.where(slot == k, value, by_row)
    by_row = by_row.T[:8]
    slot = lax.broadcasted_iota(jnp.int32, (8, side), 0)
    by_row = jnp.where(slot < 4, by_row[:, :side], pltpu.roll(by_row[:, side:], 4, 0))
    for peer in range(n_plane):
        row_ref[peer] = by_row
    own = jnp.sum(jnp.where(diagonal_of(pos_ref), on, 0.0), axis=0, keepdims=True)
    slot = lax.broadcasted_iota(jnp.int32, (8, side), 0)
    by_col = jnp.zeros((8, side), f32)
    for k, value in enumerate(stats(0) + [own]):
        by_col = jnp.where(slot == k, value, by_col)
    col_ref[...] = by_col


def combine(got):
    top = jnp.max(got, axis=0)
    spread = jnp.exp(got - top[None])
    total = jnp.sum(spread, axis=0)
    lse = top + jnp.log(total)
    weight = pltpu.roll(spread, 1, 1)
    mean = jnp.sum(weight * got, axis=0) / pltpu.roll(total, 1, 0)
    return lse, mean


def row_kernel(got_ref, col_ref, lse_ref, send_ref):
    lse, mean = combine(got_ref[...])
    slot = lax.broadcasted_iota(jnp.int32, (8, side), 0)
    loss = jnp.sum(jnp.where((slot & 3) == 0, lse, jnp.where((slot & 3) == 2, -mix_weight * mean, 0.0)))
    lse_ref[...] = jnp.concatenate([lse] + [jnp.zeros((8, side), f32)] * 15, axis=0).T
    send = jnp.where(slot == 4, loss, col_ref[...])
    for peer in range(n_column):
        send_ref[peer] = send


def grad_kernel(
    pos_ref, on_ref, mom_ref, lse_ref, got_ref, mine_ref, other_ref, text_ref, out_ref, keep_ref, send_ref
):
    width = text_ref.shape[-1]
    got = got_ref[...]
    lse, mean = combine(got)
    sums = jnp.sum(got, axis=0)
    slot = lax.broadcasted_iota(jnp.int32, (8, side), 0)
    loss = jnp.where(slot == 3, -2.0 * (1.0 - mix_weight) * sums, 0.0)
    loss = jnp.where(slot == 0, lse, jnp.where(slot == 2, -mix_weight * mean, loss))
    loss = jnp.where(slot == 4, sums * (1.0 / (n_plane * side)), loss)
    share_of_loss = jnp.sum(loss)

    on, mom = on_ref[...], mom_ref[...]
    col_on, col_mom = lse[0:1], lse[1:2]
    row_on = jnp.concatenate([lse_ref[:, 0:1], lse_ref[:, 4:5]], axis=0)
    row_mom = jnp.concatenate([lse_ref[:, 1:2], lse_ref[:, 5:6]], axis=0)
    delta = jnp.where(diagonal_of(pos_ref), 1.0 - mix_weight, 0.0)
    target_row = mix_weight * jnp.exp(mom - row_mom) + delta
    target_col = mix_weight * jnp.exp(mom - col_mom) + delta
    grad = 0.5 * ((jnp.exp(on - row_on) - target_row) + (jnp.exp(on - col_on) - target_col))
    first = pos_ref[2] == 0
    low, high = grad[:side], grad[side:]
    mine, other = jnp.where(first, low, high), jnp.where(first, high, low)
    texts = text_ref[...].reshape(2 * side, width)

    def down(part, ref):
        part = part.reshape(16, 1, rows, side)
        part = jnp.concatenate([part, jnp.zeros_like(part)], axis=1).reshape(2 * side, side)
        return lax.dot_general(
            part.astype(bf16), ref[...].reshape(2 * side, width), (((0,), (0,)), ((), ())), preferred_element_type=f32
        )

    by_text = (down(mine, mine_ref) + down(other, other_ref)).reshape(8, 2, rows, width)
    for k in range(2):
        out_ref[8 * k : 8 * k + 8] = by_text[:, k].astype(bf16)
    packed = first_half(side)
    for part, ref in ((mine, keep_ref), (other, send_ref)):
        halves = [jnp.where(packed, half, 0.0) for half in (part, pltpu.roll(part, side - rows, 1))]
        part = jnp.concatenate(halves, axis=1)
        ref[:, :width] = jnp.dot(part.astype(bf16), texts, preferred_element_type=f32)
        ref[:, width:] = jnp.full((side, 128), share_of_loss, f32)


def core_kernel(keep_ref, got_ref, out_ref):
    total = keep_ref[...] + got_ref[...]
    width = total.shape[1] - 128
    loss = total[:, width:]
    lane = lax.broadcasted_iota(jnp.int32, loss.shape, 1)
    pieces = jnp.zeros_like(loss)
    for k in range(3):
        piece = loss.astype(bf16).astype(f32)
        pieces = jnp.where(lane == k, piece, pieces)
        loss = loss - piece
    out_ref[:, :, :width] = total[:, :width].reshape(16, rows, width).astype(bf16)
    out_ref[:, :, width:] = pieces.reshape(16, rows, 128).astype(bf16)


def last_kernel(image_ref, text_ref, grad_image_ref, grad_text_ref, loss_ref):
    total = jnp.sum(image_ref[...].astype(f32), axis=0)
    width = grad_image_ref.shape[1]
    grad_image_ref[...] = total[:, :width]
    grad_text_ref[...] = jnp.sum(text_ref[...].astype(f32), axis=0)
    loss_ref[0, 0] = jnp.sum(total[:1, width:]) * (1.0 / (2.0 * rows * n_plane * n_column))


def local(image, text, mimage, mtext):
    width = image.shape[1]
    wide = width + 128
    x, y, c, zh, zp, zq = (lax.axis_index(a).astype(jnp.int32) for a in ("x", "y", "c", "zh", "zp", "zq"))
    pos = jnp.stack([x, y, c, zh, zp * 4 + zq, zq, zq, zq])

    def swap(block):
        return lax.ppermute(block, "c", [(0, 1), (1, 0)])

    def group(block, axes, names):
        return [block] + [lax.ppermute(block, axes, [(names[i], names[(i + k) % 4]) for i in range(4)]) for k in (1, 2, 3)]

    both = jnp.concatenate([text, mtext], axis=0)
    pair = jnp.concatenate([image, mimage], axis=0)
    both, pair = lax.optimization_barrier((both, pair))
    sent = jnp.broadcast_to(pair[None], (16,) + pair.shape)
    mine = lax.all_to_all(sent, ("y", "x"), 0, 0, tiled=True)
    place = (zh * 2 + zp)[None]
    (far,) = call(order_kernel, [shape(4, 16, width, dtype=bf16)], place, *group(both, ("zp", "zh"), (0, 2, 1, 3)), flops=2**35)
    texts = group(far, "zq", (0, 1, 2, 3))
    other = swap(mine)

    on, mom, row_parts, col_parts, texts = call(
        score_kernel,
        [shape(2 * side, side), shape(2 * side, side), shape(n_plane, 8, side), shape(8, side), shape(4, 4, 16, width, dtype=bf16)],
        pos, mine, other, *texts,
        flops=2**28, exps=2**18,
    )
    row_got = lax.all_to_all(row_parts, ("x", "y", "c"), 0, 0, tiled=True)
    row_lse, col_sent = call(row_kernel, [shape(side, side), shape(n_column, 8, side)], row_got, col_parts, exps=2**14)
    col_got = lax.all_to_all(col_sent, column, 0, 0, tiled=True)

    by_text, keep, send = call(
        grad_kernel,
        [shape(n_column, rows, width, dtype=bf16), shape(side, wide), shape(side, wide)],
        pos, on, mom, row_lse, col_got, mine, other, texts,
        flops=2**29, exps=2**18,
    )
    got = swap(send)
    got_text = lax.all_to_all(by_text, column, 0, 0, tiled=True)
    (by_image,) = call(core_kernel, [shape(16, rows, wide, dtype=bf16)], keep, got)
    by_image, got_text = lax.optimization_barrier((by_image, got_text))
    got_image = lax.all_to_all(by_image, ("y", "x"), 0, 0, tiled=True)
    vmem = pl.BlockSpec(memory_space=pltpu.VMEM)
    grad_image, grad_text, loss = call(
        last_kernel, [shape(rows, width), shape(rows, width), shape(1, 1)], got_image, got_text,
        out_specs=[vmem, vmem, pl.BlockSpec(memory_space=pltpu.SMEM)],
    )
    return grad_image, grad_text, loss[0, 0]


def solution(mesh):
    fine = Mesh(mesh.devices.reshape(2, 4, 4, 2, 4, 2), ("zp", "zq", "y", "zh", "x", "c"))
    by_image = P(("zh", "x", "c", "zp", "zq", "y"), None)
    by_text = P(("zp", "zq", "y", "zh", "x", "c"), None)
    return jax.shard_map(
        local,
        mesh=fine,
        in_specs=(by_image, by_text, by_image, by_text),
        out_specs=(by_image, by_text, P()),
        check_vma=False,
    )
```

```python
import jax
import jax.numpy as jnp
from jax import lax
from jax.experimental import pallas as pl
from jax.experimental.pallas import tpu as pltpu
from jax.sharding import Mesh, PartitionSpec as P

mix_weight = 0.4
very_low = -1e30
column = ("zh", "zl")
n_plane, n_column, rows = 32, 16, 8
f32, bf16 = jnp.float32, jnp.bfloat16
side = 16 * rows


def call(body, outs, *args, flops=0, exps=0, **more):
    whole = pl.BlockSpec(memory_space=pltpu.VMEM)
    specs = [pl.BlockSpec(memory_space=pltpu.SMEM) if a.dtype == jnp.int32 else whole for a in args]
    moved = sum(a.size * a.dtype.itemsize for a in list(args) + outs)
    params = dict(in_specs=specs, out_specs=[whole] * len(outs))
    params.update(more)
    return pl.pallas_call(
        body,
        out_shape=outs,
        cost_estimate=pl.CostEstimate(flops=flops, bytes_accessed=moved, transcendentals=exps),
        compiler_params=pltpu.CompilerParams(vmem_limit_bytes=40 * 2**20),
        **params,
    )(*args)


def shape(*dims, dtype=f32):
    return jax.ShapeDtypeStruct(dims, dtype)


def first_half(height):
    return (lax.broadcasted_iota(jnp.int32, (height, side), 1) & rows) == 0


def diagonal_of(pos_ref):
    x, y, c, zh, zl = (pos_ref[k] for k in range(5))
    row = lax.broadcasted_iota(jnp.int32, (2 * side, 1), 0)
    pc, px, py = row >> 7, (row >> 5) & 3, ((row >> 3) & 1) * 2 + ((row >> 4) & 1)
    image = ((zh * 8 + px * 2 + pc) * 32 + zl * 4 + py) * rows + (row & 7)
    lane = lax.broadcasted_iota(jnp.int32, (1, side), 1)
    qh, ql = (lane >> 3) & 1, lane >> 4
    text = ((ql * 4 + y) * 16 + qh * 8 + x * 2 + c) * rows + (lane & 7)
    return image == text


def order_kernel(pos_ref, own_ref, other_ref, out_ref):
    place = pos_ref[0]
    out_ref[place] = own_ref[...]
    out_ref[1 - place] = other_ref[...]


def score_kernel(pos_ref, mine_ref, other_ref, text_ref, on_ref, mom_ref, row_ref, col_ref):
    width = text_ref.shape[-1]
    texts = text_ref[...].reshape(2 * side, width)

    def product(ref):
        out = lax.dot_general(
            ref[...].reshape(2 * side, width), texts, (((1,), (1,)), ((), ())), preferred_element_type=f32
        )
        return (out * width ** (-0.5)).reshape(16, 2, rows, 2 * side)

    mine, other = product(mine_ref), product(other_ref)
    first = pos_ref[2] == 0
    low, high = jnp.where(first, mine, other), jnp.where(first, other, mine)
    packed = first_half(2 * side)

    def both(which):
        whole = jnp.concatenate([part[:, which].reshape(side, 2 * side) for part in (low, high)], axis=0)
        return whole[:, :side], whole[:, side:]

    left, right = both(0)
    on = jnp.where(packed, left, pltpu.roll(right, rows, 1))
    left, right = both(1)
    mom = jnp.where(packed, pltpu.roll(left, side - rows, 1), right)
    on_ref[...] = on
    mom_ref[...] = mom

    def stats(along):
        max_on = jnp.max(on, axis=along, keepdims=True)
        sum_on = jnp.sum(jnp.exp(on - max_on), axis=along, keepdims=True)
        max_mom = jnp.max(mom, axis=along, keepdims=True)
        weight = jnp.exp(mom - max_mom)
        sum_mom = jnp.sum(weight, axis=along, keepdims=True)
        mean = jnp.sum(weight * on, axis=along, keepdims=True) / sum_mom
        return [max_on + jnp.log(sum_on), max_mom + jnp.log(sum_mom), mean]

    slot = lax.broadcasted_iota(jnp.int32, (2 * side, 128), 1)
    by_row = jnp.zeros((2 * side, 128), f32)
    for k, value in enumerate(stats(1)):
        by_row = jnp.where(slot == k, value, by_row)
    by_row = by_row.T[:8]
    slot = lax.broadcasted_iota(jnp.int32, (8, side), 0)
    by_row = jnp.where(slot < 4, by_row[:, :side], pltpu.roll(by_row[:, side:], 4, 0))
    for peer in range(n_plane):
        row_ref[peer] = by_row
    own = jnp.sum(jnp.where(diagonal_of(pos_ref), on, 0.0), axis=0, keepdims=True)
    slot = lax.broadcasted_iota(jnp.int32, (8, side), 0)
    by_col = jnp.zeros((8, side), f32)
    for k, value in enumerate(stats(0) + [own]):
        by_col = jnp.where(slot == k, value, by_col)
    col_ref[...] = by_col


def combine(got):
    top = jnp.max(got, axis=0)
    spread = jnp.exp(got - top[None])
    total = jnp.sum(spread, axis=0)
    lse = top + jnp.log(total)
    weight = pltpu.roll(spread, 1, 1)
    mean = jnp.sum(weight * got, axis=0) / pltpu.roll(total, 1, 0)
    return lse, mean


def row_kernel(got_ref, col_ref, lse_ref, send_ref):
    lse, mean = combine(got_ref[...])
    slot = lax.broadcasted_iota(jnp.int32, (8, side), 0)
    loss = jnp.sum(jnp.where((slot & 3) == 0, lse, jnp.where((slot & 3) == 2, -mix_weight * mean, 0.0)))
    lse_ref[...] = jnp.concatenate([lse] + [jnp.zeros((8, side), f32)] * 15, axis=0).T
    send = jnp.where(slot == 4, loss, col_ref[...])
    for peer in range(n_column):
        send_ref[peer] = send


def grad_kernel(
    pos_ref, on_ref, mom_ref, lse_ref, got_ref, mine_ref, other_ref, out_ref, g_mine_ref, g_other_ref, loss_ref
):
    width = mine_ref.shape[-1]
    got = got_ref[...]
    lse, mean = combine(got)
    sums = jnp.sum(got, axis=0)
    slot = lax.broadcasted_iota(jnp.int32, (8, side), 0)
    loss = jnp.where(slot == 3, -2.0 * (1.0 - mix_weight) * sums, 0.0)
    loss = jnp.where(slot == 0, lse, jnp.where(slot == 2, -mix_weight * mean, loss))
    loss = jnp.where(slot == 4, sums * (1.0 / (n_plane * side)), loss)
    loss_ref[...] = jnp.full(loss_ref.shape, jnp.sum(loss), f32)

    on, mom = on_ref[...], mom_ref[...]
    col_on, col_mom = lse[0:1], lse[1:2]
    row_on = jnp.concatenate([lse_ref[:, 0:1], lse_ref[:, 4:5]], axis=0)
    row_mom = jnp.concatenate([lse_ref[:, 1:2], lse_ref[:, 5:6]], axis=0)
    delta = jnp.where(diagonal_of(pos_ref), 1.0 - mix_weight, 0.0)
    target_row = mix_weight * jnp.exp(mom - row_mom) + delta
    target_col = mix_weight * jnp.exp(mom - col_mom) + delta
    grad = 0.5 * ((jnp.exp(on - row_on) - target_row) + (jnp.exp(on - col_on) - target_col))
    first = pos_ref[2] == 0
    low, high = grad[:side], grad[side:]
    mine, other = jnp.where(first, low, high), jnp.where(first, high, low)
    g_mine_ref[...] = mine
    g_other_ref[...] = other

    def down(part, ref):
        part = part.reshape(16, 1, rows, side)
        part = jnp.concatenate([part, jnp.zeros_like(part)], axis=1).reshape(2 * side, side)
        return lax.dot_general(
            part.astype(bf16), ref[...].reshape(2 * side, width), (((0,), (0,)), ((), ())), preferred_element_type=f32
        )

    by_text = (down(mine, mine_ref) + down(other, other_ref)).reshape(8, 2, rows, width)
    for k in range(2):
        out_ref[8 * k : 8 * k + 8] = by_text[:, k].astype(bf16)


def image_kernel(g_mine_ref, g_other_ref, text_ref, loss_ref, keep_ref, send_ref):
    width = text_ref.shape[-1]
    texts = text_ref[...].reshape(2 * side, width)
    packed = first_half(side)
    for g_ref, ref in ((g_other_ref, send_ref), (g_mine_ref, keep_ref)):
        part = g_ref[...]
        halves = [jnp.where(packed, half, 0.0) for half in (part, pltpu.roll(part, side - rows, 1))]
        part = jnp.concatenate(halves, axis=1)
        ref[:, :width] = jnp.dot(part.astype(bf16), texts, preferred_element_type=f32)
        ref[:, width:] = jnp.broadcast_to(loss_ref[0:1], (side, 128))


def core_kernel(keep_ref, got_ref, out_ref):
    total = keep_ref[...] + got_ref[...]
    width = total.shape[1] - 128
    loss = total[:, width:]
    lane = lax.broadcasted_iota(jnp.int32, loss.shape, 1)
    pieces = jnp.zeros_like(loss)
    for k in range(3):
        piece = loss.astype(bf16).astype(f32)
        pieces = jnp.where(lane == k, piece, pieces)
        loss = loss - piece
    out_ref[:, :, :width] = total[:, :width].reshape(16, rows, width).astype(bf16)
    out_ref[:, :, width:] = pieces.reshape(16, rows, 128).astype(bf16)


def last_kernel(image_ref, text_ref, grad_image_ref, grad_text_ref, loss_ref):
    total = jnp.sum(image_ref[...].astype(f32), axis=0)
    width = grad_image_ref.shape[1]
    grad_image_ref[...] = total[:, :width]
    grad_text_ref[...] = jnp.sum(text_ref[...].astype(f32), axis=0)
    loss_ref[0, 0] = jnp.sum(total[:1, width:]) * (1.0 / (2.0 * rows * n_plane * n_column))


def local(image, text, mimage, mtext):
    width = image.shape[1]
    wide = width + 128
    x, yh, yl, c, zh, zl = (lax.axis_index(a).astype(jnp.int32) for a in ("x", "yh", "yl", "c", "zh", "zl"))
    pos = jnp.stack([x, yh * 2 + yl, c, zh, zl, 0, 0, 0])
    yh, yl = yh[None], yl[None]

    def swap(block, axis="c"):
        return lax.ppermute(block, axis, [(0, 1), (1, 0)])

    both = jnp.concatenate([text, mtext], axis=0)
    pair = jnp.concatenate([image, mimage], axis=0)
    both, pair = lax.optimization_barrier((both, pair))
    sent = jnp.broadcast_to(both[None], (n_column,) + both.shape)
    texts = lax.all_to_all(sent, column, 0, 0, tiled=True)
    across = swap(pair, "yh")
    (pair,) = call(order_kernel, [shape(2, 16, width, dtype=bf16)], yh, pair, across, flops=2**35)
    (pair,) = call(order_kernel, [shape(2, 2, 16, width, dtype=bf16)], yl, pair, swap(pair, "yl"))
    mine = lax.all_gather(pair, "x").reshape(16, 16, width)
    other = swap(mine)

    on, mom, row_parts, col_parts = call(
        score_kernel,
        [shape(2 * side, side), shape(2 * side, side), shape(n_plane, 8, side), shape(8, side)],
        pos, mine, other, texts,
        flops=2**28, exps=2**18,
    )
    row_got = lax.all_to_all(row_parts, ("x", "yh", "yl", "c"), 0, 0, tiled=True)
    row_lse, col_sent = call(row_kernel, [shape(side, side), shape(n_column, 8, side)], row_got, col_parts, exps=2**14)
    col_got = lax.all_to_all(col_sent, column, 0, 0, tiled=True)

    by_text, g_mine, g_other, loss = call(
        grad_kernel,
        [shape(n_column, rows, width, dtype=bf16), shape(side, side), shape(side, side), shape(8, 128)],
        pos, on, mom, row_lse, col_got, mine, other,
        flops=2**27, exps=2**17,
    )
    keep, send = call(image_kernel, [shape(side, wide), shape(side, wide)], g_mine, g_other, texts, loss, flops=2**27)
    got = swap(send)
    got_text = lax.all_to_all(by_text, column, 0, 0, tiled=True)
    (by_image,) = call(core_kernel, [shape(16, rows, wide, dtype=bf16)], keep, got)
    by_image, got_text = lax.optimization_barrier((by_image, got_text))
    got_image = lax.all_to_all(by_image, ("x", "yl", "yh"), 0, 0, tiled=True)
    vmem = pl.BlockSpec(memory_space=pltpu.VMEM)
    grad_image, grad_text, loss = call(
        last_kernel, [shape(rows, width), shape(rows, width), shape(1, 1)], got_image, got_text,
        out_specs=[vmem, vmem, pl.BlockSpec(memory_space=pltpu.SMEM)],
    )
    return grad_image, grad_text, loss[0, 0]


def solution(mesh):
    fine = Mesh(mesh.devices.reshape(8, 2, 2, 2, 4, 2), ("zl", "yh", "yl", "zh", "x", "c"))
    by_image = P(("zh", "x", "c", "zl", "yh", "yl"), None)
    by_text = P(("zl", "yh", "yl", "zh", "x", "c"), None)
    return jax.shard_map(
        local,
        mesh=fine,
        in_specs=(by_image, by_text, by_image, by_text),
        out_specs=(by_image, by_text, P()),
        check_vma=False,
    )
```

```python
from functools import partial

import jax
import jax.numpy as jnp
from jax import lax
from jax.experimental import pallas as pl
from jax.experimental.pallas import tpu as pltpu
from jax.sharding import Mesh, PartitionSpec as P

mix_weight = 0.4
very_low = -1e30
column = ("zh", "zl")
n_plane, n_column, rows = 32, 16, 8
f32, bf16 = jnp.float32, jnp.bfloat16
side = 16 * rows


def call(body, outs, *args, flops=0, exps=0, **more):
    whole = pl.BlockSpec(memory_space=pltpu.VMEM)
    moved = sum(a.size * a.dtype.itemsize for a in list(args) + outs)
    params = dict(in_specs=[whole] * len(args), out_specs=[whole] * len(outs))
    params.update(more)
    return pl.pallas_call(
        body,
        out_shape=outs,
        cost_estimate=pl.CostEstimate(flops=flops, bytes_accessed=moved, transcendentals=exps),
        compiler_params=pltpu.CompilerParams(vmem_limit_bytes=40 * 2**20),
        **params,
    )(*args)


def shape(*dims, dtype=f32):
    return jax.ShapeDtypeStruct(dims, dtype)


def first_half(height):
    return (lax.broadcasted_iota(jnp.int32, (height, side), 1) & rows) == 0


def diagonal_of():
    x, yh, yl, c, zh, zl = (lax.axis_index(a) for a in ("x", "yh", "yl", "c", "zh", "zl"))
    y = yh * 2 + yl
    row = lax.broadcasted_iota(jnp.int32, (2 * side, 1), 0)
    pc, px, py = row >> 7, (row >> 5) & 3, ((row >> 3) & 1) * 2 + ((row >> 4) & 1)
    image = ((zh * 8 + px * 2 + pc) * 32 + zl * 4 + py) * rows + (row & 7)
    lane = lax.broadcasted_iota(jnp.int32, (1, side), 1)
    qh, ql = (lane >> 3) & 1, lane >> 4
    text = ((ql * 4 + y) * 16 + qh * 8 + x * 2 + c) * rows + (lane & 7)
    return image == text


def order_kernel(axis, own_ref, other_ref, out_ref):
    place = lax.axis_index(axis)
    out_ref[place] = own_ref[...]
    out_ref[1 - place] = other_ref[...]


def score_kernel(mine_ref, other_ref, text_ref, on_ref, mom_ref, row_ref, col_ref):
    width = text_ref.shape[-1]
    texts = text_ref[...].reshape(2 * side, width)

    def product(ref):
        out = lax.dot_general(
            ref[...].reshape(2 * side, width), texts, (((1,), (1,)), ((), ())), preferred_element_type=f32
        )
        return (out * width ** (-0.5)).reshape(16, 2, rows, 2 * side)

    mine, other = product(mine_ref), product(other_ref)
    first = lax.axis_index("c") == 0
    low, high = jnp.where(first, mine, other), jnp.where(first, other, mine)
    packed = first_half(2 * side)

    def both(which):
        whole = jnp.concatenate([part[:, which].reshape(side, 2 * side) for part in (low, high)], axis=0)
        return whole[:, :side], whole[:, side:]

    left, right = both(0)
    on = jnp.where(packed, left, pltpu.roll(right, rows, 1))
    left, right = both(1)
    mom = jnp.where(packed, pltpu.roll(left, side - rows, 1), right)
    on_ref[...] = on
    mom_ref[...] = mom

    def stats(along):
        max_on = jnp.max(on, axis=along, keepdims=True)
        sum_on = jnp.sum(jnp.exp(on - max_on), axis=along, keepdims=True)
        max_mom = jnp.max(mom, axis=along, keepdims=True)
        weight = jnp.exp(mom - max_mom)
        sum_mom = jnp.sum(weight, axis=along, keepdims=True)
        mean = jnp.sum(weight * on, axis=along, keepdims=True) / sum_mom
        return [max_on + jnp.log(sum_on), max_mom + jnp.log(sum_mom), mean]

    slot = lax.broadcasted_iota(jnp.int32, (2 * side, 128), 1)
    by_row = jnp.zeros((2 * side, 128), f32)
    for k, value in enumerate(stats(1)):
        by_row = jnp.where(slot == k, value, by_row)
    by_row = by_row.T[:8]
    slot = lax.broadcasted_iota(jnp.int32, (8, side), 0)
    by_row = jnp.where(slot < 4, by_row[:, :side], pltpu.roll(by_row[:, side:], 4, 0))
    for peer in range(n_plane):
        row_ref[peer] = by_row
    own = jnp.sum(jnp.where(diagonal_of(), on, 0.0), axis=0, keepdims=True)
    slot = lax.broadcasted_iota(jnp.int32, (8, side), 0)
    by_col = jnp.zeros((8, side), f32)
    for k, value in enumerate(stats(0) + [own]):
        by_col = jnp.where(slot == k, value, by_col)
    col_ref[...] = by_col


def combine(got):
    top = jnp.max(got, axis=0)
    spread = jnp.exp(got - top[None])
    total = jnp.sum(spread, axis=0)
    lse = top + jnp.log(total)
    weight = pltpu.roll(spread, 1, 1)
    mean = jnp.sum(weight * got, axis=0) / pltpu.roll(total, 1, 0)
    return lse, mean


def row_kernel(got_ref, col_ref, lse_ref, send_ref):
    lse, mean = combine(got_ref[...])
    slot = lax.broadcasted_iota(jnp.int32, (8, side), 0)
    loss = jnp.sum(jnp.where((slot & 3) == 0, lse, jnp.where((slot & 3) == 2, -mix_weight * mean, 0.0)))
    lse_ref[...] = jnp.concatenate([lse] + [jnp.zeros((8, side), f32)] * 15, axis=0).T
    send = jnp.where(slot == 4, loss, col_ref[...])
    for peer in range(n_column):
        send_ref[peer] = send


def grad_kernel(
    on_ref, mom_ref, lse_ref, got_ref, mine_ref, other_ref, out_ref, g_mine_ref, g_other_ref, loss_ref
):
    width = mine_ref.shape[-1]
    got = got_ref[...]
    lse, mean = combine(got)
    sums = jnp.sum(got, axis=0)
    slot = lax.broadcasted_iota(jnp.int32, (8, side), 0)
    loss = jnp.where(slot == 3, -2.0 * (1.0 - mix_weight) * sums, 0.0)
    loss = jnp.where(slot == 0, lse, jnp.where(slot == 2, -mix_weight * mean, loss))
    loss = jnp.where(slot == 4, sums * (1.0 / (n_plane * side)), loss)
    loss_ref[...] = jnp.full(loss_ref.shape, jnp.sum(loss), f32)

    on, mom = on_ref[...], mom_ref[...]
    col_on, col_mom = lse[0:1], lse[1:2]
    row_on = jnp.concatenate([lse_ref[:, 0:1], lse_ref[:, 4:5]], axis=0)
    row_mom = jnp.concatenate([lse_ref[:, 1:2], lse_ref[:, 5:6]], axis=0)
    delta = jnp.where(diagonal_of(), 1.0 - mix_weight, 0.0)
    target_row = mix_weight * jnp.exp(mom - row_mom) + delta
    target_col = mix_weight * jnp.exp(mom - col_mom) + delta
    grad = 0.5 * ((jnp.exp(on - row_on) - target_row) + (jnp.exp(on - col_on) - target_col))
    first = lax.axis_index("c") == 0
    low, high = grad[:side], grad[side:]
    mine, other = jnp.where(first, low, high), jnp.where(first, high, low)
    g_mine_ref[...] = mine
    g_other_ref[...] = other

    def down(part, ref):
        part = part.reshape(16, 1, rows, side)
        part = jnp.concatenate([part, jnp.zeros_like(part)], axis=1).reshape(2 * side, side)
        return lax.dot_general(
            part.astype(bf16), ref[...].reshape(2 * side, width), (((0,), (0,)), ((), ())), preferred_element_type=f32
        )

    by_text = (down(mine, mine_ref) + down(other, other_ref)).reshape(8, 2, rows, width)
    for k in range(2):
        out_ref[8 * k : 8 * k + 8] = by_text[:, k].astype(bf16)


def image_kernel(g_mine_ref, g_other_ref, text_ref, loss_ref, keep_ref, send_ref):
    width = text_ref.shape[-1]
    texts = text_ref[...].reshape(2 * side, width)
    packed = first_half(side)
    for g_ref, ref in ((g_other_ref, send_ref), (g_mine_ref, keep_ref)):
        part = g_ref[...]
        halves = [jnp.where(packed, half, 0.0) for half in (part, pltpu.roll(part, side - rows, 1))]
        part = jnp.concatenate(halves, axis=1)
        ref[:, :width] = jnp.dot(part.astype(bf16), texts, preferred_element_type=f32)
        ref[:, width:] = jnp.broadcast_to(loss_ref[0:1], (side, 128))


def core_kernel(keep_ref, got_ref, out_ref):
    total = keep_ref[...] + got_ref[...]
    width = total.shape[1] - 128
    loss = total[:, width:]
    lane = lax.broadcasted_iota(jnp.int32, loss.shape, 1)
    pieces = jnp.zeros_like(loss)
    for k in range(3):
        piece = loss.astype(bf16).astype(f32)
        pieces = jnp.where(lane == k, piece, pieces)
        loss = loss - piece
    out_ref[:, :, :width] = total[:, :width].reshape(16, rows, width).astype(bf16)
    out_ref[:, :, width:] = pieces.reshape(16, rows, 128).astype(bf16)


def last_kernel(image_ref, text_ref, grad_image_ref, grad_text_ref, loss_ref):
    total = jnp.sum(image_ref[...].astype(f32), axis=0)
    width = grad_image_ref.shape[1]
    grad_image_ref[...] = total[:, :width]
    grad_text_ref[...] = jnp.sum(text_ref[...].astype(f32), axis=0)
    loss_ref[0, 0] = jnp.sum(total[:1, width:]) * (1.0 / (2.0 * rows * n_plane * n_column))


def local(image, text, mimage, mtext):
    width = image.shape[1]
    wide = width + 128

    def swap(block, axis="c"):
        return lax.ppermute(block, axis, [(0, 1), (1, 0)])

    both = jnp.concatenate([text, mtext], axis=0)
    pair = jnp.concatenate([image, mimage], axis=0)
    both, pair = lax.optimization_barrier((both, pair))
    sent = jnp.broadcast_to(both[None], (n_column,) + both.shape)
    texts = lax.all_to_all(sent, column, 0, 0, tiled=True)
    across = swap(pair, "yh")
    (pair,) = call(partial(order_kernel, "yh"), [shape(2, 16, width, dtype=bf16)], pair, across, flops=2**35)
    (pair,) = call(partial(order_kernel, "yl"), [shape(2, 2, 16, width, dtype=bf16)], pair, swap(pair, "yl"))
    mine = lax.all_gather(pair, "x").reshape(16, 16, width)
    other = swap(mine)

    on, mom, row_parts, col_parts = call(
        score_kernel,
        [shape(2 * side, side), shape(2 * side, side), shape(n_plane, 8, side), shape(8, side)],
        mine, other, texts,
        flops=2**28, exps=2**18,
    )
    row_got = lax.all_to_all(row_parts, ("x", "yh", "yl", "c"), 0, 0, tiled=True)
    row_lse, col_sent = call(row_kernel, [shape(side, side), shape(n_column, 8, side)], row_got, col_parts, exps=2**14)
    col_got = lax.all_to_all(col_sent, column, 0, 0, tiled=True)

    by_text, g_mine, g_other, loss = call(
        grad_kernel,
        [shape(n_column, rows, width, dtype=bf16), shape(side, side), shape(side, side), shape(8, 128)],
        on, mom, row_lse, col_got, mine, other,
        flops=2**27, exps=2**17,
    )
    keep, send = call(image_kernel, [shape(side, wide), shape(side, wide)], g_mine, g_other, texts, loss, flops=2**27)
    got = swap(send)
    got_text = lax.all_to_all(by_text, column, 0, 0, tiled=True)
    (by_image,) = call(core_kernel, [shape(16, rows, wide, dtype=bf16)], keep, got)
    by_image, got_text = lax.optimization_barrier((by_image, got_text))
    got_image = lax.all_to_all(by_image, ("x", "yl", "yh"), 0, 0, tiled=True)
    vmem = pl.BlockSpec(memory_space=pltpu.VMEM)
    grad_image, grad_text, loss = call(
        last_kernel, [shape(rows, width), shape(rows, width), shape(1, 1)], got_image, got_text,
        out_specs=[vmem, vmem, pl.BlockSpec(memory_space=pltpu.SMEM)],
    )
    return grad_image, grad_text, loss[0, 0]


def solution(mesh):
    fine = Mesh(mesh.devices.reshape(8, 2, 2, 2, 4, 2), ("zl", "yh", "yl", "zh", "x", "c"))
    by_image = P(("zh", "x", "c", "zl", "yh", "yl"), None)
    by_text = P(("zl", "yh", "yl", "zh", "x", "c"), None)
    return jax.shard_map(
        local,
        mesh=fine,
        in_specs=(by_image, by_text, by_image, by_text),
        out_specs=(by_image, by_text, P()),
        check_vma=False,
    )
```

```python
from functools import partial

import jax
import jax.numpy as jnp
from jax import lax
from jax.experimental import pallas as pl
from jax.experimental.pallas import tpu as pltpu
from jax.sharding import Mesh, PartitionSpec as P

mix_weight = 0.4
very_low = -1e30
column = ("zh", "zl")
n_plane, n_column, rows = 32, 16, 8
f32, bf16 = jnp.float32, jnp.bfloat16
side = 16 * rows


def call(body, outs, *args, flops=0, exps=0, **more):
    whole = pl.BlockSpec(memory_space=pltpu.VMEM)
    moved = sum(a.size * a.dtype.itemsize for a in list(args) + outs)
    params = dict(in_specs=[whole] * len(args), out_specs=[whole] * len(outs))
    params.update(more)
    return pl.pallas_call(
        body,
        out_shape=outs,
        cost_estimate=pl.CostEstimate(flops=flops, bytes_accessed=moved, transcendentals=exps),
        compiler_params=pltpu.CompilerParams(vmem_limit_bytes=40 * 2**20),
        **params,
    )(*args)


def shape(*dims, dtype=f32):
    return jax.ShapeDtypeStruct(dims, dtype)


def first_half(height):
    return (lax.broadcasted_iota(jnp.int32, (height, side), 1) & rows) == 0


def diagonal_of():
    x, yh, yl, c, zh, zl = (lax.axis_index(a) for a in ("x", "yh", "yl", "c", "zh", "zl"))
    y = yh * 2 + yl
    row = lax.broadcasted_iota(jnp.int32, (2 * side, 1), 0)
    pc, px, py = row >> 7, (row >> 5) & 3, ((row >> 3) & 1) * 2 + ((row >> 4) & 1)
    image = ((zh * 8 + px * 2 + pc) * 32 + zl * 4 + py) * rows + (row & 7)
    lane = lax.broadcasted_iota(jnp.int32, (1, side), 1)
    qh, ql = (lane >> 3) & 1, lane >> 4
    text = ((ql * 4 + y) * 16 + qh * 8 + x * 2 + c) * rows + (lane & 7)
    return image == text


def order_kernel(axis, own_ref, other_ref, out_ref):
    place = lax.axis_index(axis)
    out_ref[place] = own_ref[...]
    out_ref[1 - place] = other_ref[...]


def score_kernel(mine_ref, other_ref, text_ref, on_ref, mom_ref, row_ref, col_ref):
    width = text_ref.shape[-1]
    texts = text_ref[...].reshape(2 * side, width)

    def product(ref):
        out = lax.dot_general(
            ref[...].reshape(2 * side, width), texts, (((1,), (1,)), ((), ())), preferred_element_type=f32
        )
        return (out * width ** (-0.5)).reshape(16, 2, rows, 2 * side)

    mine, other = product(mine_ref), product(other_ref)
    first = lax.axis_index("c") == 0
    low, high = jnp.where(first, mine, other), jnp.where(first, other, mine)
    packed = first_half(2 * side)

    def both(which):
        whole = jnp.concatenate([part[:, which].reshape(side, 2 * side) for part in (low, high)], axis=0)
        return whole[:, :side], whole[:, side:]

    left, right = both(0)
    on = jnp.where(packed, left, pltpu.roll(right, rows, 1))
    left, right = both(1)
    mom = jnp.where(packed, pltpu.roll(left, side - rows, 1), right)
    on_ref[...] = on
    mom_ref[...] = mom

    def stats(along):
        max_on = jnp.max(on, axis=along, keepdims=True)
        sum_on = jnp.sum(jnp.exp(on - max_on), axis=along, keepdims=True)
        max_mom = jnp.max(mom, axis=along, keepdims=True)
        weight = jnp.exp(mom - max_mom)
        sum_mom = jnp.sum(weight, axis=along, keepdims=True)
        mean = jnp.sum(weight * on, axis=along, keepdims=True) / sum_mom
        return [max_on + jnp.log(sum_on), max_mom + jnp.log(sum_mom), mean]

    slot = lax.broadcasted_iota(jnp.int32, (2 * side, 128), 1)
    by_row = jnp.zeros((2 * side, 128), f32)
    for k, value in enumerate(stats(1)):
        by_row = jnp.where(slot == k, value, by_row)
    by_row = by_row.T[:8]
    slot = lax.broadcasted_iota(jnp.int32, (8, side), 0)
    by_row = jnp.where(slot < 4, by_row[:, :side], pltpu.roll(by_row[:, side:], 4, 0))
    for peer in range(n_plane):
        row_ref[peer] = by_row
    own = jnp.sum(jnp.where(diagonal_of(), on, 0.0), axis=0, keepdims=True)
    slot = lax.broadcasted_iota(jnp.int32, (8, side), 0)
    by_col = jnp.zeros((8, side), f32)
    for k, value in enumerate(stats(0) + [own]):
        by_col = jnp.where(slot == k, value, by_col)
    col_ref[...] = by_col


def combine(got):
    top = jnp.max(got, axis=0)
    spread = jnp.exp(got - top[None])
    total = jnp.sum(spread, axis=0)
    lse = top + jnp.log(total)
    weight = pltpu.roll(spread, 1, 1)
    mean = jnp.sum(weight * got, axis=0) / pltpu.roll(total, 1, 0)
    return lse, mean


def row_kernel(got_ref, col_ref, lse_ref, send_ref):
    lse, mean = combine(got_ref[...])
    slot = lax.broadcasted_iota(jnp.int32, (8, side), 0)
    loss = jnp.sum(jnp.where((slot & 3) == 0, lse, jnp.where((slot & 3) == 2, -mix_weight * mean, 0.0)))
    lse_ref[...] = jnp.concatenate([lse] + [jnp.zeros((8, side), f32)] * 15, axis=0).T
    send = jnp.where(slot == 4, loss, col_ref[...])
    for peer in range(n_column):
        send_ref[peer] = send


def grad_kernel(
    on_ref, mom_ref, lse_ref, got_ref, mine_ref, other_ref, out_ref, g_mine_ref, g_other_ref, loss_ref
):
    width = mine_ref.shape[-1]
    got = got_ref[...]
    lse, mean = combine(got)
    sums = jnp.sum(got, axis=0)
    slot = lax.broadcasted_iota(jnp.int32, (8, side), 0)
    loss = jnp.where(slot == 3, -2.0 * (1.0 - mix_weight) * sums, 0.0)
    loss = jnp.where(slot == 0, lse, jnp.where(slot == 2, -mix_weight * mean, loss))
    loss = jnp.where(slot == 4, sums * (1.0 / (n_plane * side)), loss)
    loss_ref[...] = jnp.full(loss_ref.shape, jnp.sum(loss), f32)

    on, mom = on_ref[...], mom_ref[...]
    col_on, col_mom = lse[0:1], lse[1:2]
    row_on = jnp.concatenate([lse_ref[:, 0:1], lse_ref[:, 4:5]], axis=0)
    row_mom = jnp.concatenate([lse_ref[:, 1:2], lse_ref[:, 5:6]], axis=0)
    delta = jnp.where(diagonal_of(), 1.0 - mix_weight, 0.0)
    target_row = mix_weight * jnp.exp(mom - row_mom) + delta
    target_col = mix_weight * jnp.exp(mom - col_mom) + delta
    grad = 0.5 * ((jnp.exp(on - row_on) - target_row) + (jnp.exp(on - col_on) - target_col))
    first = lax.axis_index("c") == 0
    low, high = grad[:side], grad[side:]
    mine, other = jnp.where(first, low, high), jnp.where(first, high, low)
    g_mine_ref[...] = mine
    g_other_ref[...] = other

    def down(part, ref):
        part = part.reshape(16, 1, rows, side)
        part = jnp.concatenate([part, jnp.zeros_like(part)], axis=1).reshape(2 * side, side)
        return lax.dot_general(
            part.astype(bf16), ref[...].reshape(2 * side, width), (((0,), (0,)), ((), ())), preferred_element_type=f32
        )

    by_text = (down(mine, mine_ref) + down(other, other_ref)).reshape(8, 2, rows, width)
    for k in range(2):
        out_ref[8 * k : 8 * k + 8] = by_text[:, k].astype(bf16)


def image_kernel(g_mine_ref, g_other_ref, text_ref, loss_ref, keep_ref, send_ref):
    width = text_ref.shape[-1]
    texts = text_ref[...].reshape(2 * side, width)
    packed = first_half(side)
    for g_ref, ref in ((g_other_ref, send_ref), (g_mine_ref, keep_ref)):
        part = g_ref[...]
        halves = [jnp.where(packed, half, 0.0) for half in (part, pltpu.roll(part, side - rows, 1))]
        part = jnp.concatenate(halves, axis=1)
        ref[:, :width] = jnp.dot(part.astype(bf16), texts, preferred_element_type=f32)
        ref[:, width:] = jnp.broadcast_to(loss_ref[0:1], (side, 128))


def core_kernel(keep_ref, got_ref, own_ref, send_ref):
    total = (keep_ref[...] + got_ref[...]).reshape(8, 2, rows, keep_ref.shape[1])
    first = lax.axis_index("yh") == 0
    own_ref[...] = jnp.where(first, total[:, 0], total[:, 1])
    send_ref[...] = jnp.where(first, total[:, 1], total[:, 0])


def across_kernel(keep_ref, got_ref, out_ref):
    total = keep_ref[...] + got_ref[...]
    width = total.shape[2] - 128
    loss = total[:, :, width:]
    lane = lax.broadcasted_iota(jnp.int32, loss.shape, 2)
    pieces = jnp.zeros_like(loss)
    for k in range(3):
        piece = loss.astype(bf16).astype(f32)
        pieces = jnp.where(lane == k, piece, pieces)
        loss = loss - piece
    out_ref[:, :, :width] = total[:, :, :width].astype(bf16)
    out_ref[:, :, width:] = pieces.astype(bf16)


def last_kernel(image_ref, text_ref, grad_image_ref, grad_text_ref, loss_ref):
    total = jnp.sum(image_ref[...].astype(f32), axis=0)
    width = grad_image_ref.shape[1]
    grad_image_ref[...] = total[:, :width]
    grad_text_ref[...] = jnp.sum(text_ref[...].astype(f32), axis=0)
    loss_ref[0, 0] = jnp.sum(total[:1, width:]) * (1.0 / (2.0 * rows * n_plane * n_column))


def local(image, text, mimage, mtext):
    width = image.shape[1]
    wide = width + 128

    def swap(block, axis="c"):
        return lax.ppermute(block, axis, [(0, 1), (1, 0)])

    both = jnp.concatenate([text, mtext], axis=0)
    pair = jnp.concatenate([image, mimage], axis=0)
    both, pair = lax.optimization_barrier((both, pair))
    sent = jnp.broadcast_to(both[None], (n_column,) + both.shape)
    texts = lax.all_to_all(sent, column, 0, 0, tiled=True)
    across = swap(pair, "yh")
    (pair,) = call(partial(order_kernel, "yh"), [shape(2, 16, width, dtype=bf16)], pair, across, flops=2**35)
    (pair,) = call(partial(order_kernel, "yl"), [shape(2, 2, 16, width, dtype=bf16)], pair, swap(pair, "yl"))
    mine = lax.all_gather(pair, "x").reshape(16, 16, width)
    other = swap(mine)

    on, mom, row_parts, col_parts = call(
        score_kernel,
        [shape(2 * side, side), shape(2 * side, side), shape(n_plane, 8, side), shape(8, side)],
        mine, other, texts,
        flops=2**28, exps=2**18,
    )
    row_got = lax.all_to_all(row_parts, ("x", "yh", "yl", "c"), 0, 0, tiled=True)
    row_lse, col_sent = call(row_kernel, [shape(side, side), shape(n_column, 8, side)], row_got, col_parts, exps=2**14)
    col_got = lax.all_to_all(col_sent, column, 0, 0, tiled=True)

    by_text, g_mine, g_other, loss = call(
        grad_kernel,
        [shape(n_column, rows, width, dtype=bf16), shape(side, side), shape(side, side), shape(8, 128)],
        on, mom, row_lse, col_got, mine, other,
        flops=2**27, exps=2**17,
    )
    keep, send = call(image_kernel, [shape(side, wide), shape(side, wide)], g_mine, g_other, texts, loss, flops=2**27)
    got = swap(send)
    got_text = lax.all_to_all(by_text, column, 0, 0, tiled=True)
    keep, send = call(core_kernel, [shape(8, rows, wide)] * 2, keep, got)
    (by_image,) = call(across_kernel, [shape(8, rows, wide, dtype=bf16)], keep, swap(send, "yh"))
    by_image, got_text = lax.optimization_barrier((by_image, got_text))
    got_image = lax.all_to_all(by_image, ("x", "yl"), 0, 0, tiled=True)
    vmem = pl.BlockSpec(memory_space=pltpu.VMEM)
    grad_image, grad_text, loss = call(
        last_kernel, [shape(rows, width), shape(rows, width), shape(1, 1)], got_image, got_text,
        out_specs=[vmem, vmem, pl.BlockSpec(memory_space=pltpu.SMEM)],
    )
    return grad_image, grad_text, loss[0, 0]


def solution(mesh):
    fine = Mesh(mesh.devices.reshape(8, 2, 2, 2, 4, 2), ("zl", "yh", "yl", "zh", "x", "c"))
    by_image = P(("zh", "x", "c", "zl", "yh", "yl"), None)
    by_text = P(("zl", "yh", "yl", "zh", "x", "c"), None)
    return jax.shard_map(
        local,
        mesh=fine,
        in_specs=(by_image, by_text, by_image, by_text),
        out_specs=(by_image, by_text, P()),
        check_vma=False,
    )
```

```python
from functools import partial

import jax
import jax.numpy as jnp
from jax import lax
from jax.experimental import pallas as pl
from jax.experimental.pallas import tpu as pltpu
from jax.sharding import Mesh, PartitionSpec as P

mix_weight = 0.4
very_low = -1e30
column = ("zh", "zl")
n_plane, n_column, rows = 32, 16, 8
f32, bf16 = jnp.float32, jnp.bfloat16
side = 16 * rows


def call(body, outs, *args, flops=0, exps=0, **more):
    whole = pl.BlockSpec(memory_space=pltpu.VMEM)
    moved = sum(a.size * a.dtype.itemsize for a in list(args) + outs)
    params = dict(in_specs=[whole] * len(args), out_specs=[whole] * len(outs))
    params.update(more)
    return pl.pallas_call(
        body,
        out_shape=outs,
        cost_estimate=pl.CostEstimate(flops=flops, bytes_accessed=moved, transcendentals=exps),
        compiler_params=pltpu.CompilerParams(vmem_limit_bytes=40 * 2**20),
        **params,
    )(*args)


def shape(*dims, dtype=f32):
    return jax.ShapeDtypeStruct(dims, dtype)


def first_half(height):
    return (lax.broadcasted_iota(jnp.int32, (height, side), 1) & rows) == 0


def diagonal_of():
    x, yh, yl, c, zh, zl = (lax.axis_index(a) for a in ("x", "yh", "yl", "c", "zh", "zl"))
    y = yh * 2 + yl
    row = lax.broadcasted_iota(jnp.int32, (2 * side, 1), 0)
    pc, px, py = row >> 7, (row >> 5) & 3, ((row >> 3) & 1) * 2 + ((row >> 4) & 1)
    image = ((zh * 8 + px * 2 + pc) * 32 + zl * 4 + py) * rows + (row & 7)
    lane = lax.broadcasted_iota(jnp.int32, (1, side), 1)
    qh, ql = (lane >> 3) & 1, lane >> 4
    text = ((ql * 4 + y) * 16 + qh * 8 + x * 2 + c) * rows + (lane & 7)
    return image == text


def order_kernel(axis, own_ref, other_ref, out_ref):
    place = lax.axis_index(axis)
    out_ref[place] = own_ref[...]
    out_ref[1 - place] = other_ref[...]


def score_kernel(mine_ref, other_ref, text_ref, on_ref, mom_ref, row_ref, col_ref):
    width = text_ref.shape[-1]
    texts = text_ref[...].reshape(2 * side, width)

    def product(ref):
        out = lax.dot_general(
            ref[...].reshape(2 * side, width), texts, (((1,), (1,)), ((), ())), preferred_element_type=f32
        )
        return (out * width ** (-0.5)).reshape(16, 2, rows, 2 * side)

    mine, other = product(mine_ref), product(other_ref)
    first = lax.axis_index("c") == 0
    low, high = jnp.where(first, mine, other), jnp.where(first, other, mine)
    packed = first_half(2 * side)

    def both(which):
        whole = jnp.concatenate([part[:, which].reshape(side, 2 * side) for part in (low, high)], axis=0)
        return whole[:, :side], whole[:, side:]

    left, right = both(0)
    on = jnp.where(packed, left, pltpu.roll(right, rows, 1))
    left, right = both(1)
    mom = jnp.where(packed, pltpu.roll(left, side - rows, 1), right)
    on_ref[...] = on
    mom_ref[...] = mom

    def stats(along):
        max_on = jnp.max(on, axis=along, keepdims=True)
        sum_on = jnp.sum(jnp.exp(on - max_on), axis=along, keepdims=True)
        max_mom = jnp.max(mom, axis=along, keepdims=True)
        weight = jnp.exp(mom - max_mom)
        sum_mom = jnp.sum(weight, axis=along, keepdims=True)
        mean = jnp.sum(weight * on, axis=along, keepdims=True) / sum_mom
        return [max_on + jnp.log(sum_on), max_mom + jnp.log(sum_mom), mean]

    slot = lax.broadcasted_iota(jnp.int32, (2 * side, 128), 1)
    by_row = jnp.zeros((2 * side, 128), f32)
    for k, value in enumerate(stats(1)):
        by_row = jnp.where(slot == k, value, by_row)
    by_row = by_row.T[:8]
    slot = lax.broadcasted_iota(jnp.int32, (8, side), 0)
    by_row = jnp.where(slot < 4, by_row[:, :side], pltpu.roll(by_row[:, side:], 4, 0))
    for peer in range(n_plane):
        row_ref[peer] = by_row
    own = jnp.sum(jnp.where(diagonal_of(), on, 0.0), axis=0, keepdims=True)
    slot = lax.broadcasted_iota(jnp.int32, (8, side), 0)
    by_col = jnp.zeros((8, side), f32)
    for k, value in enumerate(stats(0) + [own]):
        by_col = jnp.where(slot == k, value, by_col)
    col_ref[...] = by_col


def combine(got):
    top = jnp.max(got, axis=0)
    spread = jnp.exp(got - top[None])
    total = jnp.sum(spread, axis=0)
    lse = top + jnp.log(total)
    weight = pltpu.roll(spread, 1, 1)
    mean = jnp.sum(weight * got, axis=0) / pltpu.roll(total, 1, 0)
    return lse, mean


def row_kernel(got_ref, col_ref, lse_ref, send_ref):
    lse, mean = combine(got_ref[...])
    slot = lax.broadcasted_iota(jnp.int32, (8, side), 0)
    loss = jnp.sum(jnp.where((slot & 3) == 0, lse, jnp.where((slot & 3) == 2, -mix_weight * mean, 0.0)))
    lse_ref[...] = jnp.concatenate([lse] + [jnp.zeros((8, side), f32)] * 15, axis=0).T
    send = jnp.where(slot == 4, loss, col_ref[...])
    for peer in range(n_column):
        send_ref[peer] = send


def grad_kernel(
    on_ref, mom_ref, lse_ref, got_ref, mine_ref, other_ref, out_ref, g_mine_ref, g_other_ref, loss_ref
):
    width = mine_ref.shape[-1]
    got = got_ref[...]
    lse, mean = combine(got)
    sums = jnp.sum(got, axis=0)
    slot = lax.broadcasted_iota(jnp.int32, (8, side), 0)
    loss = jnp.where(slot == 3, -2.0 * (1.0 - mix_weight) * sums, 0.0)
    loss = jnp.where(slot == 0, lse, jnp.where(slot == 2, -mix_weight * mean, loss))
    loss = jnp.where(slot == 4, sums * (1.0 / (n_plane * side)), loss)
    loss_ref[...] = jnp.full(loss_ref.shape, jnp.sum(loss), f32)

    on, mom = on_ref[...], mom_ref[...]
    col_on, col_mom = lse[0:1], lse[1:2]
    row_on = jnp.concatenate([lse_ref[:, 0:1], lse_ref[:, 4:5]], axis=0)
    row_mom = jnp.concatenate([lse_ref[:, 1:2], lse_ref[:, 5:6]], axis=0)
    delta = jnp.where(diagonal_of(), 1.0 - mix_weight, 0.0)
    target_row = mix_weight * jnp.exp(mom - row_mom) + delta
    target_col = mix_weight * jnp.exp(mom - col_mom) + delta
    grad = 0.5 * ((jnp.exp(on - row_on) - target_row) + (jnp.exp(on - col_on) - target_col))
    first = lax.axis_index("c") == 0
    low, high = grad[:side], grad[side:]
    mine, other = jnp.where(first, low, high), jnp.where(first, high, low)
    g_mine_ref[...] = mine
    g_other_ref[...] = other

    def down(part, ref):
        part = part.reshape(16, 1, rows, side)
        part = jnp.concatenate([part, jnp.zeros_like(part)], axis=1).reshape(2 * side, side)
        return lax.dot_general(
            part.astype(bf16), ref[...].reshape(2 * side, width), (((0,), (0,)), ((), ())), preferred_element_type=f32
        )

    by_text = (down(mine, mine_ref) + down(other, other_ref)).reshape(8, 2, rows, width)
    for k in range(2):
        out_ref[8 * k : 8 * k + 8] = by_text[:, k].astype(bf16)


def image_kernel(g_mine_ref, g_other_ref, text_ref, loss_ref, keep_ref, send_ref):
    width = text_ref.shape[-1]
    texts = text_ref[...].reshape(2 * side, width)
    packed = first_half(side)
    for g_ref, ref in ((g_other_ref, send_ref), (g_mine_ref, keep_ref)):
        part = g_ref[...]
        halves = [jnp.where(packed, half, 0.0) for half in (part, pltpu.roll(part, side - rows, 1))]
        part = jnp.concatenate(halves, axis=1)
        ref[:, :width] = jnp.dot(part.astype(bf16), texts, preferred_element_type=f32)
        ref[:, width:] = jnp.broadcast_to(loss_ref[0:1], (side, 128))


def core_kernel(keep_ref, got_ref, own_ref, send_ref):
    total = (keep_ref[...] + got_ref[...]).reshape(4, 2, 2 * rows, keep_ref.shape[1])
    first = lax.axis_index("yl") == 0
    own_ref[...] = jnp.where(first, total[:, 0], total[:, 1]).reshape(own_ref.shape)
    send_ref[...] = jnp.where(first, total[:, 1], total[:, 0]).reshape(own_ref.shape)


def across_kernel(keep_ref, got_ref, out_ref):
    total = keep_ref[...] + got_ref[...]
    width = total.shape[2] - 128
    loss = total[:, :, width:]
    lane = lax.broadcasted_iota(jnp.int32, loss.shape, 2)
    pieces = jnp.zeros_like(loss)
    for k in range(3):
        piece = loss.astype(bf16).astype(f32)
        pieces = jnp.where(lane == k, piece, pieces)
        loss = loss - piece
    out_ref[:, :, :width] = total[:, :, :width].astype(bf16)
    out_ref[:, :, width:] = pieces.astype(bf16)


def last_kernel(image_ref, text_ref, grad_image_ref, grad_text_ref, loss_ref):
    total = jnp.sum(image_ref[...].astype(f32), axis=0)
    width = grad_image_ref.shape[1]
    grad_image_ref[...] = total[:, :width]
    grad_text_ref[...] = jnp.sum(text_ref[...].astype(f32), axis=0)
    loss_ref[0, 0] = jnp.sum(total[:1, width:]) * (1.0 / (2.0 * rows * n_plane * n_column))


def local(image, text, mimage, mtext):
    width = image.shape[1]
    wide = width + 128

    def swap(block, axis="c"):
        return lax.ppermute(block, axis, [(0, 1), (1, 0)])

    both = jnp.concatenate([text, mtext], axis=0)
    pair = jnp.concatenate([image, mimage], axis=0)
    both, pair = lax.optimization_barrier((both, pair))
    sent = jnp.broadcast_to(both[None], (n_column,) + both.shape)
    texts = lax.all_to_all(sent, column, 0, 0, tiled=True)
    across = swap(pair, "yh")
    (pair,) = call(partial(order_kernel, "yh"), [shape(2, 16, width, dtype=bf16)], pair, across, flops=2**35)
    (pair,) = call(partial(order_kernel, "yl"), [shape(2, 2, 16, width, dtype=bf16)], pair, swap(pair, "yl"))
    mine = lax.all_gather(pair, "x").reshape(16, 16, width)
    other = swap(mine)

    on, mom, row_parts, col_parts = call(
        score_kernel,
        [shape(2 * side, side), shape(2 * side, side), shape(n_plane, 8, side), shape(8, side)],
        mine, other, texts,
        flops=2**28, exps=2**18,
    )
    row_got = lax.all_to_all(row_parts, ("x", "yh", "yl", "c"), 0, 0, tiled=True)
    row_lse, col_sent = call(row_kernel, [shape(side, side), shape(n_column, 8, side)], row_got, col_parts, exps=2**14)
    col_got = lax.all_to_all(col_sent, column, 0, 0, tiled=True)

    by_text, g_mine, g_other, loss = call(
        grad_kernel,
        [shape(n_column, rows, width, dtype=bf16), shape(side, side), shape(side, side), shape(8, 128)],
        on, mom, row_lse, col_got, mine, other,
        flops=2**27, exps=2**17,
    )
    keep, send = call(image_kernel, [shape(side, wide), shape(side, wide)], g_mine, g_other, texts, loss, flops=2**27)
    got = swap(send)
    got_text = lax.all_to_all(by_text, column, 0, 0, tiled=True)
    keep, send = call(core_kernel, [shape(8, rows, wide)] * 2, keep, got)
    (by_image,) = call(across_kernel, [shape(8, rows, wide, dtype=bf16)], keep, swap(send, "yl"))
    by_image, got_text = lax.optimization_barrier((by_image, got_text))
    got_image = lax.all_to_all(by_image, ("x", "yh"), 0, 0, tiled=True)
    vmem = pl.BlockSpec(memory_space=pltpu.VMEM)
    grad_image, grad_text, loss = call(
        last_kernel, [shape(rows, width), shape(rows, width), shape(1, 1)], got_image, got_text,
        out_specs=[vmem, vmem, pl.BlockSpec(memory_space=pltpu.SMEM)],
    )
    return grad_image, grad_text, loss[0, 0]


def solution(mesh):
    fine = Mesh(mesh.devices.reshape(8, 2, 2, 2, 4, 2), ("zl", "yh", "yl", "zh", "x", "c"))
    by_image = P(("zh", "x", "c", "zl", "yh", "yl"), None)
    by_text = P(("zl", "yh", "yl", "zh", "x", "c"), None)
    return jax.shard_map(
        local,
        mesh=fine,
        in_specs=(by_image, by_text, by_image, by_text),
        out_specs=(by_image, by_text, P()),
        check_vma=False,
    )
```

```python
from functools import partial

import jax
import jax.numpy as jnp
from jax import lax
from jax.experimental import pallas as pl
from jax.experimental.pallas import tpu as pltpu
from jax.sharding import Mesh, PartitionSpec as P

mix_weight = 0.4
very_low = -1e30
column = ("zh", "zl")
n_plane, n_column, rows = 32, 16, 8
f32, bf16 = jnp.float32, jnp.bfloat16
side = 16 * rows


def call(body, outs, *args, flops=0, exps=0, **more):
    whole = pl.BlockSpec(memory_space=pltpu.VMEM)
    moved = sum(a.size * a.dtype.itemsize for a in list(args) + outs)
    params = dict(in_specs=[whole] * len(args), out_specs=[whole] * len(outs))
    params.update(more)
    return pl.pallas_call(
        body,
        out_shape=outs,
        cost_estimate=pl.CostEstimate(flops=flops, bytes_accessed=moved, transcendentals=exps),
        compiler_params=pltpu.CompilerParams(vmem_limit_bytes=40 * 2**20),
        **params,
    )(*args)


def shape(*dims, dtype=f32):
    return jax.ShapeDtypeStruct(dims, dtype)


def first_half(height):
    return (lax.broadcasted_iota(jnp.int32, (height, side), 1) & rows) == 0


def diagonal_of():
    x, yh, yl, c, zh, zl = (lax.axis_index(a) for a in ("x", "yh", "yl", "c", "zh", "zl"))
    y = yh * 2 + yl
    row = lax.broadcasted_iota(jnp.int32, (2 * side, 1), 0)
    pc, px, py = row >> 7, (row >> 5) & 3, ((row >> 3) & 1) * 2 + ((row >> 4) & 1)
    image = ((zh * 8 + px * 2 + pc) * 32 + zl * 4 + py) * rows + (row & 7)
    lane = lax.broadcasted_iota(jnp.int32, (1, side), 1)
    qh, ql = (lane >> 3) & 1, lane >> 4
    text = ((ql * 4 + y) * 16 + qh * 8 + x * 2 + c) * rows + (lane & 7)
    return image == text


def order_kernel(axis, own_ref, other_ref, out_ref):
    place = lax.axis_index(axis)
    out_ref[place] = own_ref[...]
    out_ref[1 - place] = other_ref[...]


def score_kernel(mine_ref, other_ref, text_ref, on_ref, mom_ref, row_ref, col_ref):
    width = text_ref.shape[-1]
    texts = text_ref[...].reshape(2 * side, width)

    def product(ref):
        out = lax.dot_general(
            ref[...].reshape(2 * side, width), texts, (((1,), (1,)), ((), ())), preferred_element_type=f32
        )
        return (out * width ** (-0.5)).reshape(16, 2, rows, 2 * side)

    mine, other = product(mine_ref), product(other_ref)
    first = lax.axis_index("c") == 0
    low, high = jnp.where(first, mine, other), jnp.where(first, other, mine)
    packed = first_half(2 * side)

    def both(which):
        whole = jnp.concatenate([part[:, which].reshape(side, 2 * side) for part in (low, high)], axis=0)
        return whole[:, :side], whole[:, side:]

    left, right = both(0)
    on = jnp.where(packed, left, pltpu.roll(right, rows, 1))
    left, right = both(1)
    mom = jnp.where(packed, pltpu.roll(left, side - rows, 1), right)
    on_ref[...] = on
    mom_ref[...] = mom

    def stats(along):
        max_on = jnp.max(on, axis=along, keepdims=True)
        sum_on = jnp.sum(jnp.exp(on - max_on), axis=along, keepdims=True)
        max_mom = jnp.max(mom, axis=along, keepdims=True)
        weight = jnp.exp(mom - max_mom)
        sum_mom = jnp.sum(weight, axis=along, keepdims=True)
        mean = jnp.sum(weight * on, axis=along, keepdims=True) / sum_mom
        return [max_on + jnp.log(sum_on), max_mom + jnp.log(sum_mom), mean]

    slot = lax.broadcasted_iota(jnp.int32, (2 * side, 128), 1)
    by_row = jnp.zeros((2 * side, 128), f32)
    for k, value in enumerate(stats(1)):
        by_row = jnp.where(slot == k, value, by_row)
    by_row = by_row.T[:8]
    slot = lax.broadcasted_iota(jnp.int32, (8, side), 0)
    by_row = jnp.where(slot < 4, by_row[:, :side], pltpu.roll(by_row[:, side:], 4, 0))
    for peer in range(n_plane):
        row_ref[peer] = by_row
    own = jnp.sum(jnp.where(diagonal_of(), on, 0.0), axis=0, keepdims=True)
    slot = lax.broadcasted_iota(jnp.int32, (8, side), 0)
    by_col = jnp.zeros((8, side), f32)
    for k, value in enumerate(stats(0) + [own]):
        by_col = jnp.where(slot == k, value, by_col)
    col_ref[...] = by_col


def combine(got):
    top = jnp.max(got, axis=0)
    spread = jnp.exp(got - top[None])
    total = jnp.sum(spread, axis=0)
    lse = top + jnp.log(total)
    weight = pltpu.roll(spread, 1, 1)
    mean = jnp.sum(weight * got, axis=0) / pltpu.roll(total, 1, 0)
    return lse, mean


def row_kernel(got_ref, col_ref, lse_ref, send_ref):
    lse, mean = combine(got_ref[...])
    slot = lax.broadcasted_iota(jnp.int32, (8, side), 0)
    loss = jnp.sum(jnp.where((slot & 3) == 0, lse, jnp.where((slot & 3) == 2, -mix_weight * mean, 0.0)))
    lse_ref[...] = jnp.concatenate([lse] + [jnp.zeros((8, side), f32)] * 15, axis=0).T
    send = jnp.where(slot == 4, loss, col_ref[...])
    for peer in range(n_column):
        send_ref[peer] = send


def grad_kernel(
    on_ref, mom_ref, lse_ref, got_ref, mine_ref, other_ref, out_ref, g_mine_ref, g_other_ref, loss_ref
):
    width = mine_ref.shape[-1]
    got = got_ref[...]
    lse, mean = combine(got)
    sums = jnp.sum(got, axis=0)
    slot = lax.broadcasted_iota(jnp.int32, (8, side), 0)
    loss = jnp.where(slot == 3, -2.0 * (1.0 - mix_weight) * sums, 0.0)
    loss = jnp.where(slot == 0, lse, jnp.where(slot == 2, -mix_weight * mean, loss))
    loss = jnp.where(slot == 4, sums * (1.0 / (n_plane * side)), loss)
    loss_ref[...] = jnp.full(loss_ref.shape, jnp.sum(loss), f32)

    on, mom = on_ref[...], mom_ref[...]
    col_on, col_mom = lse[0:1], lse[1:2]
    row_on = jnp.concatenate([lse_ref[:, 0:1], lse_ref[:, 4:5]], axis=0)
    row_mom = jnp.concatenate([lse_ref[:, 1:2], lse_ref[:, 5:6]], axis=0)
    delta = jnp.where(diagonal_of(), 1.0 - mix_weight, 0.0)
    target_row = mix_weight * jnp.exp(mom - row_mom) + delta
    target_col = mix_weight * jnp.exp(mom - col_mom) + delta
    grad = 0.5 * ((jnp.exp(on - row_on) - target_row) + (jnp.exp(on - col_on) - target_col))
    first = lax.axis_index("c") == 0
    low, high = grad[:side], grad[side:]
    mine, other = jnp.where(first, low, high), jnp.where(first, high, low)
    g_mine_ref[...] = mine
    g_other_ref[...] = other

    def down(part, ref):
        part = part.reshape(16, 1, rows, side)
        part = jnp.concatenate([part, jnp.zeros_like(part)], axis=1).reshape(2 * side, side)
        return lax.dot_general(
            part.astype(bf16), ref[...].reshape(2 * side, width), (((0,), (0,)), ((), ())), preferred_element_type=f32
        )

    by_text = (down(mine, mine_ref) + down(other, other_ref)).reshape(8, 2, rows, width)
    for k in range(2):
        out_ref[8 * k : 8 * k + 8] = by_text[:, k].astype(bf16)


def image_kernel(g_mine_ref, g_other_ref, text_ref, loss_ref, keep_ref, send_ref):
    width = text_ref.shape[-1]
    texts = text_ref[...].reshape(2 * side, width)
    packed = first_half(side)
    for g_ref, ref in ((g_other_ref, send_ref), (g_mine_ref, keep_ref)):
        part = g_ref[...]
        halves = [jnp.where(packed, half, 0.0) for half in (part, pltpu.roll(part, side - rows, 1))]
        part = jnp.concatenate(halves, axis=1)
        ref[:, :width] = jnp.dot(part.astype(bf16), texts, preferred_element_type=f32)
        ref[:, width:] = jnp.broadcast_to(loss_ref[0:1], (side, 128))


def send_out(total, ref):
    width = total.shape[2] - 128
    loss = total[:, :, width:]
    lane = lax.broadcasted_iota(jnp.int32, loss.shape, 2)
    pieces = jnp.zeros_like(loss)
    for k in range(3):
        piece = loss.astype(bf16).astype(f32)
        pieces = jnp.where(lane == k, piece, pieces)
        loss = loss - piece
    ref[:, :, :width] = total[:, :, :width].astype(bf16)
    ref[:, :, width:] = pieces.astype(bf16)


def core_kernel(keep_ref, got_ref, own_ref, send_ref):
    total = (keep_ref[...] + got_ref[...]).reshape(8, 2, rows, keep_ref.shape[1])
    first = lax.axis_index("yh") == 0
    own_ref[...] = jnp.where(first, total[:, 0], total[:, 1])
    send_out(jnp.where(first, total[:, 1], total[:, 0]), send_ref)


def across_kernel(keep_ref, got_ref, out_ref):
    keep, got = keep_ref[...], got_ref[...].astype(f32)
    width = keep.shape[2] - 128
    loss = keep[:, :, width:] + jnp.sum(got[:, :, width:], axis=2, keepdims=True)
    send_out(jnp.concatenate([keep[:, :, :width] + got[:, :, :width], loss], axis=2), out_ref)


def last_kernel(image_ref, text_ref, grad_image_ref, grad_text_ref, loss_ref):
    total = jnp.sum(image_ref[...].astype(f32), axis=0)
    width = grad_image_ref.shape[1]
    grad_image_ref[...] = total[:, :width]
    grad_text_ref[...] = jnp.sum(text_ref[...].astype(f32), axis=0)
    loss_ref[0, 0] = jnp.sum(total[:1, width:]) * (1.0 / (2.0 * rows * n_plane * n_column))


def local(image, text, mimage, mtext):
    width = image.shape[1]
    wide = width + 128

    def swap(block, axis="c"):
        return lax.ppermute(block, axis, [(0, 1), (1, 0)])

    both = jnp.concatenate([text, mtext], axis=0)
    pair = jnp.concatenate([image, mimage], axis=0)
    both, pair = lax.optimization_barrier((both, pair))
    sent = jnp.broadcast_to(both[None], (n_column,) + both.shape)
    texts = lax.all_to_all(sent, column, 0, 0, tiled=True)
    across = swap(pair, "yh")
    (pair,) = call(partial(order_kernel, "yh"), [shape(2, 16, width, dtype=bf16)], pair, across, flops=2**35)
    (pair,) = call(partial(order_kernel, "yl"), [shape(2, 2, 16, width, dtype=bf16)], pair, swap(pair, "yl"))
    mine = lax.all_gather(pair, "x").reshape(16, 16, width)
    other = swap(mine)

    on, mom, row_parts, col_parts = call(
        score_kernel,
        [shape(2 * side, side), shape(2 * side, side), shape(n_plane, 8, side), shape(8, side)],
        mine, other, texts,
        flops=2**28, exps=2**18,
    )
    row_got = lax.all_to_all(row_parts, ("x", "yh", "yl", "c"), 0, 0, tiled=True)
    row_lse, col_sent = call(row_kernel, [shape(side, side), shape(n_column, 8, side)], row_got, col_parts, exps=2**14)
    col_got = lax.all_to_all(col_sent, column, 0, 0, tiled=True)

    by_text, g_mine, g_other, loss = call(
        grad_kernel,
        [shape(n_column, rows, width, dtype=bf16), shape(side, side), shape(side, side), shape(8, 128)],
        on, mom, row_lse, col_got, mine, other,
        flops=2**27, exps=2**17,
    )
    keep, send = call(image_kernel, [shape(side, wide), shape(side, wide)], g_mine, g_other, texts, loss, flops=2**27)
    got = swap(send)
    got_text = lax.all_to_all(by_text, column, 0, 0, tiled=True)
    keep, send = call(core_kernel, [shape(8, rows, wide), shape(8, rows, wide, dtype=bf16)], keep, got)
    (by_image,) = call(across_kernel, [shape(8, rows, wide, dtype=bf16)], keep, swap(send, "yh"))
    by_image, got_text = lax.optimization_barrier((by_image, got_text))
    got_image = lax.all_to_all(by_image, ("x", "yl"), 0, 0, tiled=True)
    vmem = pl.BlockSpec(memory_space=pltpu.VMEM)
    grad_image, grad_text, loss = call(
        last_kernel, [shape(rows, width), shape(rows, width), shape(1, 1)], got_image, got_text,
        out_specs=[vmem, vmem, pl.BlockSpec(memory_space=pltpu.SMEM)],
    )
    return grad_image, grad_text, loss[0, 0]


def solution(mesh):
    fine = Mesh(mesh.devices.reshape(8, 2, 2, 2, 4, 2), ("zl", "yh", "yl", "zh", "x", "c"))
    by_image = P(("zh", "x", "c", "zl", "yh", "yl"), None)
    by_text = P(("zl", "yh", "yl", "zh", "x", "c"), None)
    return jax.shard_map(
        local,
        mesh=fine,
        in_specs=(by_image, by_text, by_image, by_text),
        out_specs=(by_image, by_text, P()),
        check_vma=False,
    )
```

```python
from functools import partial

import jax
import jax.numpy as jnp
from jax import lax
from jax.experimental import pallas as pl
from jax.experimental.pallas import tpu as pltpu
from jax.sharding import Mesh, PartitionSpec as P

mix_weight = 0.4
very_low = -1e30
column = ("zh", "zl")
n_plane, n_column, rows = 32, 16, 8
f32, bf16 = jnp.float32, jnp.bfloat16
side = 16 * rows


def call(body, outs, *args, flops=0, exps=0, **more):
    whole = pl.BlockSpec(memory_space=pltpu.VMEM)
    moved = sum(a.size * a.dtype.itemsize for a in list(args) + outs)
    params = dict(in_specs=[whole] * len(args), out_specs=[whole] * len(outs))
    params.update(more)
    return pl.pallas_call(
        body,
        out_shape=outs,
        cost_estimate=pl.CostEstimate(flops=flops, bytes_accessed=moved, transcendentals=exps),
        compiler_params=pltpu.CompilerParams(vmem_limit_bytes=40 * 2**20),
        **params,
    )(*args)


def shape(*dims, dtype=f32):
    return jax.ShapeDtypeStruct(dims, dtype)


def first_half(height):
    return (lax.broadcasted_iota(jnp.int32, (height, side), 1) & rows) == 0


def diagonal_of():
    x, yh, yl, c, zh, zl = (lax.axis_index(a) for a in ("x", "yh", "yl", "c", "zh", "zl"))
    y = yh * 2 + yl
    row = lax.broadcasted_iota(jnp.int32, (2 * side, 1), 0)
    pc, px, py = row >> 7, (row >> 5) & 3, ((row >> 3) & 1) * 2 + ((row >> 4) & 1)
    image = ((zh * 8 + px * 2 + pc) * 32 + zl * 4 + py) * rows + (row & 7)
    lane = lax.broadcasted_iota(jnp.int32, (1, side), 1)
    qh, ql = (lane >> 3) & 1, lane >> 4
    text = ((ql * 4 + y) * 16 + qh * 8 + x * 2 + c) * rows + (lane & 7)
    return image == text


def order_kernel(axis, own_ref, other_ref, out_ref):
    place = lax.axis_index(axis)
    out_ref[place] = own_ref[...]
    out_ref[1 - place] = other_ref[...]


def score_kernel(mine_ref, other_ref, text_ref, on_ref, mom_ref, row_ref, col_ref):
    width = text_ref.shape[-1]
    texts = text_ref[...].reshape(2 * side, width)

    def product(ref):
        out = lax.dot_general(
            ref[...].reshape(2 * side, width), texts, (((1,), (1,)), ((), ())), preferred_element_type=f32
        )
        return (out * width ** (-0.5)).reshape(16, 2, rows, 2 * side)

    mine, other = product(mine_ref), product(other_ref)
    first = lax.axis_index("c") == 0
    low, high = jnp.where(first, mine, other), jnp.where(first, other, mine)
    packed = first_half(2 * side)

    def both(which):
        whole = jnp.concatenate([part[:, which].reshape(side, 2 * side) for part in (low, high)], axis=0)
        return whole[:, :side], whole[:, side:]

    left, right = both(0)
    on = jnp.where(packed, left, pltpu.roll(right, rows, 1))
    left, right = both(1)
    mom = jnp.where(packed, pltpu.roll(left, side - rows, 1), right)
    on_ref[...] = on
    mom_ref[...] = mom

    def stats(along):
        max_on = jnp.max(on, axis=along, keepdims=True)
        sum_on = jnp.sum(jnp.exp(on - max_on), axis=along, keepdims=True)
        max_mom = jnp.max(mom, axis=along, keepdims=True)
        weight = jnp.exp(mom - max_mom)
        sum_mom = jnp.sum(weight, axis=along, keepdims=True)
        mean = jnp.sum(weight * on, axis=along, keepdims=True) / sum_mom
        return [max_on + jnp.log(sum_on), max_mom + jnp.log(sum_mom), mean]

    slot = lax.broadcasted_iota(jnp.int32, (2 * side, 128), 1)
    by_row = jnp.zeros((2 * side, 128), f32)
    for k, value in enumerate(stats(1)):
        by_row = jnp.where(slot == k, value, by_row)
    by_row = by_row.T[:8]
    slot = lax.broadcasted_iota(jnp.int32, (8, side), 0)
    by_row = jnp.where(slot < 4, by_row[:, :side], pltpu.roll(by_row[:, side:], 4, 0))
    for peer in range(n_plane):
        row_ref[peer] = by_row
    own = jnp.sum(jnp.where(diagonal_of(), on, 0.0), axis=0, keepdims=True)
    slot = lax.broadcasted_iota(jnp.int32, (8, side), 0)
    by_col = jnp.zeros((8, side), f32)
    for k, value in enumerate(stats(0) + [own]):
        by_col = jnp.where(slot == k, value, by_col)
    col_ref[...] = by_col


def combine(got):
    top = jnp.max(got, axis=0)
    spread = jnp.exp(got - top[None])
    total = jnp.sum(spread, axis=0)
    lse = top + jnp.log(total)
    weight = pltpu.roll(spread, 1, 1)
    mean = jnp.sum(weight * got, axis=0) / pltpu.roll(total, 1, 0)
    return lse, mean


def row_kernel(got_ref, col_ref, lse_ref, send_ref):
    lse, mean = combine(got_ref[...])
    slot = lax.broadcasted_iota(jnp.int32, (8, side), 0)
    loss = jnp.sum(jnp.where((slot & 3) == 0, lse, jnp.where((slot & 3) == 2, -mix_weight * mean, 0.0)))
    lse_ref[...] = jnp.concatenate([lse] + [jnp.zeros((8, side), f32)] * 15, axis=0).T
    send = jnp.where(slot == 4, loss, col_ref[...])
    for peer in range(n_column):
        send_ref[peer] = send


def grad_kernel(
    on_ref, mom_ref, lse_ref, got_ref, mine_ref, other_ref, out_ref, g_mine_ref, g_other_ref, loss_ref
):
    width = mine_ref.shape[-1]
    got = got_ref[...]
    lse, mean = combine(got)
    sums = jnp.sum(got, axis=0)
    slot = lax.broadcasted_iota(jnp.int32, (8, side), 0)
    loss = jnp.where(slot == 3, -2.0 * (1.0 - mix_weight) * sums, 0.0)
    loss = jnp.where(slot == 0, lse, jnp.where(slot == 2, -mix_weight * mean, loss))
    loss = jnp.where(slot == 4, sums * (1.0 / (n_plane * side)), loss)
    loss_ref[...] = jnp.full(loss_ref.shape, jnp.sum(loss), f32)

    on, mom = on_ref[...], mom_ref[...]
    col_on, col_mom = lse[0:1], lse[1:2]
    row_on = jnp.concatenate([lse_ref[:, 0:1], lse_ref[:, 4:5]], axis=0)
    row_mom = jnp.concatenate([lse_ref[:, 1:2], lse_ref[:, 5:6]], axis=0)
    delta = jnp.where(diagonal_of(), 1.0 - mix_weight, 0.0)
    target_row = mix_weight * jnp.exp(mom - row_mom) + delta
    target_col = mix_weight * jnp.exp(mom - col_mom) + delta
    grad = 0.5 * ((jnp.exp(on - row_on) - target_row) + (jnp.exp(on - col_on) - target_col))
    first = lax.axis_index("c") == 0
    low, high = grad[:side], grad[side:]
    mine, other = jnp.where(first, low, high), jnp.where(first, high, low)
    g_mine_ref[...] = mine
    g_other_ref[...] = other

    def down(part, ref):
        part = part.reshape(16, 1, rows, side)
        part = jnp.concatenate([part, jnp.zeros_like(part)], axis=1).reshape(2 * side, side)
        return lax.dot_general(
            part.astype(bf16), ref[...].reshape(2 * side, width), (((0,), (0,)), ((), ())), preferred_element_type=f32
        )

    by_text = (down(mine, mine_ref) + down(other, other_ref)).reshape(8, 2, rows, width)
    for k in range(2):
        out_ref[8 * k : 8 * k + 8] = by_text[:, k].astype(bf16)


def image_kernel(g_mine_ref, g_other_ref, text_ref, loss_ref, keep_ref, send_ref):
    width = text_ref.shape[-1]
    texts = text_ref[...].reshape(2 * side, width)
    packed = first_half(side)
    for g_ref, ref in ((g_other_ref, send_ref), (g_mine_ref, keep_ref)):
        part = g_ref[...]
        halves = [jnp.where(packed, half, 0.0) for half in (part, pltpu.roll(part, side - rows, 1))]
        part = jnp.concatenate(halves, axis=1)
        ref[:, :width] = jnp.dot(part.astype(bf16), texts, preferred_element_type=f32)
        ref[:, width:] = jnp.broadcast_to(loss_ref[0:1], (side, 128))


def core_kernel(keep_ref, got_ref, own_ref, *send_refs):
    y = lax.axis_index("yh") * 2 + lax.axis_index("yl")
    for k, ref in enumerate((own_ref,) + send_refs):
        to = (y + k) & 3
        for x in range(4):
            at = pl.ds(pl.multiple_of(x * 4 * rows + ((to & 1) * 2 + (to >> 1)) * rows, rows), rows)
            ref[x] = keep_ref[at, :] + got_ref[at, :]


def across_kernel(keep_ref, a_ref, b_ref, c_ref, out_ref):
    total = (keep_ref[...] + a_ref[...]) + (b_ref[...] + c_ref[...])
    width = total.shape[2] - 128
    loss = total[:, :, width:]
    lane = lax.broadcasted_iota(jnp.int32, loss.shape, 2)
    pieces = jnp.zeros_like(loss)
    for k in range(3):
        piece = loss.astype(bf16).astype(f32)
        pieces = jnp.where(lane == k, piece, pieces)
        loss = loss - piece
    out_ref[:, :, :width] = total[:, :, :width].astype(bf16)
    out_ref[:, :, width:] = pieces.astype(bf16)


def last_kernel(image_ref, text_ref, grad_image_ref, grad_text_ref, loss_ref):
    total = jnp.sum(image_ref[...].astype(f32), axis=0)
    width = grad_image_ref.shape[1]
    grad_image_ref[...] = total[:, :width]
    grad_text_ref[...] = jnp.sum(text_ref[...].astype(f32), axis=0)
    loss_ref[0, 0] = jnp.sum(total[:1, width:]) * (1.0 / (2.0 * rows * n_plane * n_column))


def local(image, text, mimage, mtext):
    width = image.shape[1]
    wide = width + 128

    def swap(block, axis="c"):
        return lax.ppermute(block, axis, [(0, 1), (1, 0)])

    both = jnp.concatenate([text, mtext], axis=0)
    pair = jnp.concatenate([image, mimage], axis=0)
    both, pair = lax.optimization_barrier((both, pair))
    sent = jnp.broadcast_to(both[None], (n_column,) + both.shape)
    texts = lax.all_to_all(sent, column, 0, 0, tiled=True)
    across = swap(pair, "yh")
    (pair,) = call(partial(order_kernel, "yh"), [shape(2, 16, width, dtype=bf16)], pair, across, flops=2**35)
    (pair,) = call(partial(order_kernel, "yl"), [shape(2, 2, 16, width, dtype=bf16)], pair, swap(pair, "yl"))
    mine = lax.all_gather(pair, "x").reshape(16, 16, width)
    other = swap(mine)

    on, mom, row_parts, col_parts = call(
        score_kernel,
        [shape(2 * side, side), shape(2 * side, side), shape(n_plane, 8, side), shape(8, side)],
        mine, other, texts,
        flops=2**28, exps=2**18,
    )
    row_got = lax.all_to_all(row_parts, ("x", "yh", "yl", "c"), 0, 0, tiled=True)
    row_lse, col_sent = call(row_kernel, [shape(side, side), shape(n_column, 8, side)], row_got, col_parts, exps=2**14)
    col_got = lax.all_to_all(col_sent, column, 0, 0, tiled=True)

    by_text, g_mine, g_other, loss = call(
        grad_kernel,
        [shape(n_column, rows, width, dtype=bf16), shape(side, side), shape(side, side), shape(8, 128)],
        on, mom, row_lse, col_got, mine, other,
        flops=2**27, exps=2**17,
    )
    keep, send = call(image_kernel, [shape(side, wide), shape(side, wide)], g_mine, g_other, texts, loss, flops=2**27)
    got = swap(send)
    got_text = lax.all_to_all(by_text, column, 0, 0, tiled=True)
    keep, *send = call(core_kernel, [shape(4, rows, wide)] * 4, keep, got)
    along = [
        lax.ppermute(block, ("yh", "yl"), [(i, (i + k) % 4) for i in range(4)]) for k, block in enumerate(send, 1)
    ]
    (by_image,) = call(across_kernel, [shape(4, rows, wide, dtype=bf16)], keep, *along)
    by_image, got_text = lax.optimization_barrier((by_image, got_text))
    got_image = lax.all_to_all(by_image, "x", 0, 0, tiled=True)
    vmem = pl.BlockSpec(memory_space=pltpu.VMEM)
    grad_image, grad_text, loss = call(
        last_kernel, [shape(rows, width), shape(rows, width), shape(1, 1)], got_image, got_text,
        out_specs=[vmem, vmem, pl.BlockSpec(memory_space=pltpu.SMEM)],
    )
    return grad_image, grad_text, loss[0, 0]


def solution(mesh):
    fine = Mesh(mesh.devices.reshape(8, 2, 2, 2, 4, 2), ("zl", "yh", "yl", "zh", "x", "c"))
    by_image = P(("zh", "x", "c", "zl", "yh", "yl"), None)
    by_text = P(("zl", "yh", "yl", "zh", "x", "c"), None)
    return jax.shard_map(
        local,
        mesh=fine,
        in_specs=(by_image, by_text, by_image, by_text),
        out_specs=(by_image, by_text, P()),
        check_vma=False,
    )
```

```python
from functools import partial

import jax
import jax.numpy as jnp
from jax import lax
from jax.experimental import pallas as pl
from jax.experimental.pallas import tpu as pltpu
from jax.sharding import Mesh, PartitionSpec as P

mix_weight = 0.4
very_low = -1e30
column = ("zh", "zl")
n_plane, n_column, rows = 32, 16, 8
f32, bf16 = jnp.float32, jnp.bfloat16
side = 16 * rows


def call(body, outs, *args, flops=0, exps=0, **more):
    whole = pl.BlockSpec(memory_space=pltpu.VMEM)
    moved = sum(a.size * a.dtype.itemsize for a in list(args) + outs)
    params = dict(in_specs=[whole] * len(args), out_specs=[whole] * len(outs))
    params.update(more)
    return pl.pallas_call(
        body,
        out_shape=outs,
        cost_estimate=pl.CostEstimate(flops=flops, bytes_accessed=moved, transcendentals=exps),
        compiler_params=pltpu.CompilerParams(vmem_limit_bytes=40 * 2**20),
        **params,
    )(*args)


def shape(*dims, dtype=f32):
    return jax.ShapeDtypeStruct(dims, dtype)


def first_half(height):
    return (lax.broadcasted_iota(jnp.int32, (height, side), 1) & rows) == 0


def diagonal_of():
    x, yh, yl, c, zh, zl = (lax.axis_index(a) for a in ("x", "yh", "yl", "c", "zh", "zl"))
    y = yh * 2 + yl
    row = lax.broadcasted_iota(jnp.int32, (2 * side, 1), 0)
    pc, px, py = row >> 7, (row >> 5) & 3, ((row >> 3) & 1) * 2 + ((row >> 4) & 1)
    image = ((zh * 8 + px * 2 + pc) * 32 + zl * 4 + py) * rows + (row & 7)
    lane = lax.broadcasted_iota(jnp.int32, (1, side), 1)
    qh, ql = (lane >> 3) & 1, lane >> 4
    text = ((ql * 4 + y) * 16 + qh * 8 + x * 2 + c) * rows + (lane & 7)
    return image == text


def order_kernel(axis, own_ref, other_ref, out_ref):
    place = lax.axis_index(axis)
    out_ref[place] = own_ref[...]
    out_ref[1 - place] = other_ref[...]


def score_kernel(mine_ref, other_ref, text_ref, on_ref, mom_ref, row_ref, col_ref):
    width = text_ref.shape[-1]
    texts = text_ref[...].reshape(2 * side, width)

    def product(ref):
        out = lax.dot_general(
            ref[...].reshape(2 * side, width), texts, (((1,), (1,)), ((), ())), preferred_element_type=f32
        )
        return (out * width ** (-0.5)).reshape(16, 2, rows, 2 * side)

    mine, other = product(mine_ref), product(other_ref)
    first = lax.axis_index("c") == 0
    low, high = jnp.where(first, mine, other), jnp.where(first, other, mine)
    packed = first_half(2 * side)

    def both(which):
        whole = jnp.concatenate([part[:, which].reshape(side, 2 * side) for part in (low, high)], axis=0)
        return whole[:, :side], whole[:, side:]

    left, right = both(0)
    on = jnp.where(packed, left, pltpu.roll(right, rows, 1))
    left, right = both(1)
    mom = jnp.where(packed, pltpu.roll(left, side - rows, 1), right)
    on_ref[...] = on
    mom_ref[...] = mom

    def stats(along):
        max_on = jnp.max(on, axis=along, keepdims=True)
        sum_on = jnp.sum(jnp.exp(on - max_on), axis=along, keepdims=True)
        max_mom = jnp.max(mom, axis=along, keepdims=True)
        weight = jnp.exp(mom - max_mom)
        sum_mom = jnp.sum(weight, axis=along, keepdims=True)
        mean = jnp.sum(weight * on, axis=along, keepdims=True) / sum_mom
        return [max_on + jnp.log(sum_on), max_mom + jnp.log(sum_mom), mean]

    slot = lax.broadcasted_iota(jnp.int32, (2 * side, 128), 1)
    by_row = jnp.zeros((2 * side, 128), f32)
    for k, value in enumerate(stats(1)):
        by_row = jnp.where(slot == k, value, by_row)
    by_row = by_row.T[:8]
    slot = lax.broadcasted_iota(jnp.int32, (8, side), 0)
    by_row = jnp.where(slot < 4, by_row[:, :side], pltpu.roll(by_row[:, side:], 4, 0))
    for peer in range(n_plane):
        row_ref[peer] = by_row
    own = jnp.sum(jnp.where(diagonal_of(), on, 0.0), axis=0, keepdims=True)
    slot = lax.broadcasted_iota(jnp.int32, (8, side), 0)
    by_col = jnp.zeros((8, side), f32)
    for k, value in enumerate(stats(0) + [own]):
        by_col = jnp.where(slot == k, value, by_col)
    col_ref[...] = by_col


def combine(got):
    top = jnp.max(got, axis=0)
    spread = jnp.exp(got - top[None])
    total = jnp.sum(spread, axis=0)
    lse = top + jnp.log(total)
    weight = pltpu.roll(spread, 1, 1)
    mean = jnp.sum(weight * got, axis=0) / pltpu.roll(total, 1, 0)
    return lse, mean


def row_kernel(got_ref, col_ref, lse_ref, send_ref):
    lse, mean = combine(got_ref[...])
    slot = lax.broadcasted_iota(jnp.int32, (8, side), 0)
    loss = jnp.sum(jnp.where((slot & 3) == 0, lse, jnp.where((slot & 3) == 2, -mix_weight * mean, 0.0)))
    lse_ref[...] = jnp.concatenate([lse] + [jnp.zeros((8, side), f32)] * 15, axis=0).T
    send = jnp.where(slot == 4, loss, col_ref[...])
    for peer in range(n_column):
        send_ref[peer] = send


def grad_kernel(
    on_ref, mom_ref, lse_ref, got_ref, mine_ref, other_ref, out_ref, g_mine_ref, g_other_ref, loss_ref
):
    width = mine_ref.shape[-1]
    got = got_ref[...]
    lse, mean = combine(got)
    sums = jnp.sum(got, axis=0)
    slot = lax.broadcasted_iota(jnp.int32, (8, side), 0)
    loss = jnp.where(slot == 3, -2.0 * (1.0 - mix_weight) * sums, 0.0)
    loss = jnp.where(slot == 0, lse, jnp.where(slot == 2, -mix_weight * mean, loss))
    loss = jnp.where(slot == 4, sums * (1.0 / (n_plane * side)), loss)
    loss_ref[...] = jnp.full(loss_ref.shape, jnp.sum(loss), f32)

    on, mom = on_ref[...], mom_ref[...]
    col_on, col_mom = lse[0:1], lse[1:2]
    row_on = jnp.concatenate([lse_ref[:, 0:1], lse_ref[:, 4:5]], axis=0)
    row_mom = jnp.concatenate([lse_ref[:, 1:2], lse_ref[:, 5:6]], axis=0)
    delta = jnp.where(diagonal_of(), 1.0 - mix_weight, 0.0)
    target_row = mix_weight * jnp.exp(mom - row_mom) + delta
    target_col = mix_weight * jnp.exp(mom - col_mom) + delta
    grad = 0.5 * ((jnp.exp(on - row_on) - target_row) + (jnp.exp(on - col_on) - target_col))
    first = lax.axis_index("c") == 0
    low, high = grad[:side], grad[side:]
    mine, other = jnp.where(first, low, high), jnp.where(first, high, low)
    g_mine_ref[...] = mine
    g_other_ref[...] = other

    def down(part, ref):
        part = part.reshape(16, 1, rows, side)
        part = jnp.concatenate([part, jnp.zeros_like(part)], axis=1).reshape(2 * side, side)
        return lax.dot_general(
            part.astype(bf16), ref[...].reshape(2 * side, width), (((0,), (0,)), ((), ())), preferred_element_type=f32
        )

    by_text = (down(mine, mine_ref) + down(other, other_ref)).reshape(8, 2, rows, width)
    for k in range(2):
        out_ref[8 * k : 8 * k + 8] = by_text[:, k].astype(bf16)


def image_kernel(g_mine_ref, g_other_ref, text_ref, loss_ref, keep_ref, send_ref):
    width = text_ref.shape[-1]
    texts = text_ref[...].reshape(2 * side, width)
    packed = first_half(side)
    for g_ref, ref in ((g_other_ref, send_ref), (g_mine_ref, keep_ref)):
        part = g_ref[...]
        halves = [jnp.where(packed, half, 0.0) for half in (part, pltpu.roll(part, side - rows, 1))]
        part = jnp.concatenate(halves, axis=1)
        ref[:, :width] = jnp.dot(part.astype(bf16), texts, preferred_element_type=f32)
        ref[:, width:] = jnp.broadcast_to(loss_ref[0:1], (side, 128))


def send_out(total, ref):
    width = total.shape[2] - 128
    loss = total[:, :, width:]
    lane = lax.broadcasted_iota(jnp.int32, loss.shape, 2)
    pieces = jnp.zeros_like(loss)
    for k in range(3):
        piece = loss.astype(bf16).astype(f32)
        pieces = jnp.where(lane == k, piece, pieces)
        loss = loss - piece
    ref[:, :, :width] = total[:, :, :width].astype(bf16)
    ref[:, :, width:] = pieces.astype(bf16)


def core_kernel(keep_ref, got_ref, own_ref, *send_refs):
    y = lax.axis_index("yh") * 2 + lax.axis_index("yl")

    def block(k):
        to = (y + k) & 3
        parts = []
        for x in range(4):
            at = pl.ds(pl.multiple_of(x * 4 * rows + ((to & 1) * 2 + (to >> 1)) * rows, rows), rows)
            parts.append(keep_ref[at, :] + got_ref[at, :])
        return jnp.stack(parts)

    own_ref[...] = block(0)
    for k, ref in enumerate(send_refs, 1):
        send_out(block(k), ref)


def across_kernel(keep_ref, a_ref, b_ref, c_ref, out_ref):
    keep = keep_ref[...]
    got = (a_ref[...].astype(f32) + b_ref[...].astype(f32)) + c_ref[...].astype(f32)
    width = keep.shape[2] - 128
    loss = keep[:, :, width:] + jnp.sum(got[:, :, width:], axis=2, keepdims=True)
    send_out(jnp.concatenate([keep[:, :, :width] + got[:, :, :width], loss], axis=2), out_ref)


def last_kernel(image_ref, text_ref, grad_image_ref, grad_text_ref, loss_ref):
    total = jnp.sum(image_ref[...].astype(f32), axis=0)
    width = grad_image_ref.shape[1]
    grad_image_ref[...] = total[:, :width]
    grad_text_ref[...] = jnp.sum(text_ref[...].astype(f32), axis=0)
    loss_ref[0, 0] = jnp.sum(total[:1, width:]) * (1.0 / (2.0 * rows * n_plane * n_column))


def local(image, text, mimage, mtext):
    width = image.shape[1]
    wide = width + 128

    def swap(block, axis="c"):
        return lax.ppermute(block, axis, [(0, 1), (1, 0)])

    both = jnp.concatenate([text, mtext], axis=0)
    pair = jnp.concatenate([image, mimage], axis=0)
    both, pair = lax.optimization_barrier((both, pair))
    sent = jnp.broadcast_to(both[None], (n_column,) + both.shape)
    texts = lax.all_to_all(sent, column, 0, 0, tiled=True)
    across = swap(pair, "yh")
    (pair,) = call(partial(order_kernel, "yh"), [shape(2, 16, width, dtype=bf16)], pair, across, flops=2**35)
    (pair,) = call(partial(order_kernel, "yl"), [shape(2, 2, 16, width, dtype=bf16)], pair, swap(pair, "yl"))
    mine = lax.all_gather(pair, "x").reshape(16, 16, width)
    other = swap(mine)

    on, mom, row_parts, col_parts = call(
        score_kernel,
        [shape(2 * side, side), shape(2 * side, side), shape(n_plane, 8, side), shape(8, side)],
        mine, other, texts,
        flops=2**28, exps=2**18,
    )
    row_got = lax.all_to_all(row_parts, ("x", "yh", "yl", "c"), 0, 0, tiled=True)
    row_lse, col_sent = call(row_kernel, [shape(side, side), shape(n_column, 8, side)], row_got, col_parts, exps=2**14)
    col_got = lax.all_to_all(col_sent, column, 0, 0, tiled=True)

    by_text, g_mine, g_other, loss = call(
        grad_kernel,
        [shape(n_column, rows, width, dtype=bf16), shape(side, side), shape(side, side), shape(8, 128)],
        on, mom, row_lse, col_got, mine, other,
        flops=2**27, exps=2**17,
    )
    keep, send = call(image_kernel, [shape(side, wide), shape(side, wide)], g_mine, g_other, texts, loss, flops=2**27)
    got = swap(send)
    got_text = lax.all_to_all(by_text, column, 0, 0, tiled=True)
    keep, *send = call(core_kernel, [shape(4, rows, wide)] + [shape(4, rows, wide, dtype=bf16)] * 3, keep, got)
    along = [
        lax.ppermute(block, ("yh", "yl"), [(i, (i + k) % 4) for i in range(4)]) for k, block in enumerate(send, 1)
    ]
    (by_image,) = call(across_kernel, [shape(4, rows, wide, dtype=bf16)], keep, *along)
    by_image, got_text = lax.optimization_barrier((by_image, got_text))
    got_image = lax.all_to_all(by_image, "x", 0, 0, tiled=True)
    vmem = pl.BlockSpec(memory_space=pltpu.VMEM)
    grad_image, grad_text, loss = call(
        last_kernel, [shape(rows, width), shape(rows, width), shape(1, 1)], got_image, got_text,
        out_specs=[vmem, vmem, pl.BlockSpec(memory_space=pltpu.SMEM)],
    )
    return grad_image, grad_text, loss[0, 0]


def solution(mesh):
    fine = Mesh(mesh.devices.reshape(8, 2, 2, 2, 4, 2), ("zl", "yh", "yl", "zh", "x", "c"))
    by_image = P(("zh", "x", "c", "zl", "yh", "yl"), None)
    by_text = P(("zl", "yh", "yl", "zh", "x", "c"), None)
    return jax.shard_map(
        local,
        mesh=fine,
        in_specs=(by_image, by_text, by_image, by_text),
        out_specs=(by_image, by_text, P()),
        check_vma=False,
    )
```

```python
from functools import partial

import jax
import jax.numpy as jnp
from jax import lax
from jax.experimental import pallas as pl
from jax.experimental.pallas import tpu as pltpu
from jax.sharding import Mesh, PartitionSpec as P

mix_weight = 0.4
very_low = -1e30
column = ("zh", "zl")
n_plane, n_column, rows = 32, 16, 8
f32, bf16 = jnp.float32, jnp.bfloat16
side = 16 * rows


def call(body, outs, *args, flops=0, exps=0, **more):
    whole = pl.BlockSpec(memory_space=pltpu.VMEM)
    moved = sum(a.size * a.dtype.itemsize for a in list(args) + outs)
    params = dict(in_specs=[whole] * len(args), out_specs=[whole] * len(outs))
    params.update(more)
    return pl.pallas_call(
        body,
        out_shape=outs,
        cost_estimate=pl.CostEstimate(flops=flops, bytes_accessed=moved, transcendentals=exps),
        compiler_params=pltpu.CompilerParams(vmem_limit_bytes=40 * 2**20),
        **params,
    )(*args)


def shape(*dims, dtype=f32):
    return jax.ShapeDtypeStruct(dims, dtype)


def first_half(height):
    return (lax.broadcasted_iota(jnp.int32, (height, side), 1) & rows) == 0


def diagonal_of():
    x, yh, yl, c, zh, zl = (lax.axis_index(a) for a in ("x", "yh", "yl", "c", "zh", "zl"))
    y = yh * 2 + yl
    row = lax.broadcasted_iota(jnp.int32, (2 * side, 1), 0)
    pc, px, py = row >> 7, (row >> 5) & 3, ((row >> 3) & 1) * 2 + ((row >> 4) & 1)
    image = ((zh * 8 + px * 2 + pc) * 32 + zl * 4 + py) * rows + (row & 7)
    lane = lax.broadcasted_iota(jnp.int32, (1, side), 1)
    qh, ql = (lane >> 3) & 1, lane >> 4
    text = ((ql * 4 + y) * 16 + qh * 8 + x * 2 + c) * rows + (lane & 7)
    return image == text


def order_kernel(axis, own_ref, other_ref, out_ref):
    place = lax.axis_index(axis)
    out_ref[place] = own_ref[...]
    out_ref[1 - place] = other_ref[...]


def score_kernel(mine_ref, other_ref, text_ref, on_ref, mom_ref, row_ref, col_ref):
    width = text_ref.shape[-1]
    texts = text_ref[...].reshape(2 * side, width)

    def product(ref):
        out = lax.dot_general(
            ref[...].reshape(2 * side, width), texts, (((1,), (1,)), ((), ())), preferred_element_type=f32
        )
        return (out * width ** (-0.5)).reshape(16, 2, rows, 2 * side)

    mine, other = product(mine_ref), product(other_ref)
    first = lax.axis_index("c") == 0
    low, high = jnp.where(first, mine, other), jnp.where(first, other, mine)
    packed = first_half(2 * side)

    def both(which):
        whole = jnp.concatenate([part[:, which].reshape(side, 2 * side) for part in (low, high)], axis=0)
        return whole[:, :side], whole[:, side:]

    left, right = both(0)
    on = jnp.where(packed, left, pltpu.roll(right, rows, 1))
    left, right = both(1)
    mom = jnp.where(packed, pltpu.roll(left, side - rows, 1), right)
    on_ref[...] = on
    mom_ref[...] = mom

    def stats(along):
        max_on = jnp.max(on, axis=along, keepdims=True)
        sum_on = jnp.sum(jnp.exp(on - max_on), axis=along, keepdims=True)
        max_mom = jnp.max(mom, axis=along, keepdims=True)
        weight = jnp.exp(mom - max_mom)
        sum_mom = jnp.sum(weight, axis=along, keepdims=True)
        mean = jnp.sum(weight * on, axis=along, keepdims=True) / sum_mom
        return [max_on + jnp.log(sum_on), max_mom + jnp.log(sum_mom), mean]

    slot = lax.broadcasted_iota(jnp.int32, (2 * side, 128), 1)
    by_row = jnp.zeros((2 * side, 128), f32)
    for k, value in enumerate(stats(1)):
        by_row = jnp.where(slot == k, value, by_row)
    by_row = by_row.T[:8]
    slot = lax.broadcasted_iota(jnp.int32, (8, side), 0)
    by_row = jnp.where(slot < 4, by_row[:, :side], pltpu.roll(by_row[:, side:], 4, 0))
    for peer in range(n_plane):
        row_ref[peer] = by_row
    own = jnp.sum(jnp.where(diagonal_of(), on, 0.0), axis=0, keepdims=True)
    slot = lax.broadcasted_iota(jnp.int32, (8, side), 0)
    by_col = jnp.zeros((8, side), f32)
    for k, value in enumerate(stats(0) + [own]):
        by_col = jnp.where(slot == k, value, by_col)
    col_ref[...] = by_col


def combine(got):
    top = jnp.max(got, axis=0)
    spread = jnp.exp(got - top[None])
    total = jnp.sum(spread, axis=0)
    lse = top + jnp.log(total)
    weight = pltpu.roll(spread, 1, 1)
    mean = jnp.sum(weight * got, axis=0) / pltpu.roll(total, 1, 0)
    return lse, mean


def row_kernel(got_ref, col_ref, lse_ref, send_ref):
    lse, mean = combine(got_ref[...])
    slot = lax.broadcasted_iota(jnp.int32, (8, side), 0)
    loss = jnp.sum(jnp.where((slot & 3) == 0, lse, jnp.where((slot & 3) == 2, -mix_weight * mean, 0.0)))
    lse_ref[...] = jnp.concatenate([lse] + [jnp.zeros((8, side), f32)] * 15, axis=0).T
    send = jnp.where(slot == 4, loss, col_ref[...])
    for peer in range(n_column):
        send_ref[peer] = send


def grad_kernel(
    on_ref, mom_ref, lse_ref, got_ref, mine_ref, other_ref, out_ref, g_mine_ref, g_other_ref, loss_ref
):
    width = mine_ref.shape[-1]
    got = got_ref[...]
    lse, mean = combine(got)
    sums = jnp.sum(got, axis=0)
    slot = lax.broadcasted_iota(jnp.int32, (8, side), 0)
    loss = jnp.where(slot == 3, -2.0 * (1.0 - mix_weight) * sums, 0.0)
    loss = jnp.where(slot == 0, lse, jnp.where(slot == 2, -mix_weight * mean, loss))
    loss = jnp.where(slot == 4, sums * (1.0 / (n_plane * side)), loss)
    loss_ref[...] = jnp.full(loss_ref.shape, jnp.sum(loss), f32)

    on, mom = on_ref[...], mom_ref[...]
    col_on, col_mom = lse[0:1], lse[1:2]
    row_on = jnp.concatenate([lse_ref[:, 0:1], lse_ref[:, 4:5]], axis=0)
    row_mom = jnp.concatenate([lse_ref[:, 1:2], lse_ref[:, 5:6]], axis=0)
    delta = jnp.where(diagonal_of(), 1.0 - mix_weight, 0.0)
    target_row = mix_weight * jnp.exp(mom - row_mom) + delta
    target_col = mix_weight * jnp.exp(mom - col_mom) + delta
    grad = 0.5 * ((jnp.exp(on - row_on) - target_row) + (jnp.exp(on - col_on) - target_col))
    first = lax.axis_index("c") == 0
    low, high = grad[:side], grad[side:]
    mine, other = jnp.where(first, low, high), jnp.where(first, high, low)
    g_mine_ref[...] = mine
    g_other_ref[...] = other

    def down(part, ref):
        part = part.reshape(16, 1, rows, side)
        part = jnp.concatenate([part, jnp.zeros_like(part)], axis=1).reshape(2 * side, side)
        return lax.dot_general(
            part.astype(bf16), ref[...].reshape(2 * side, width), (((0,), (0,)), ((), ())), preferred_element_type=f32
        )

    by_text = (down(mine, mine_ref) + down(other, other_ref)).reshape(8, 2, rows, width)
    for k in range(2):
        out_ref[8 * k : 8 * k + 8] = by_text[:, k].astype(bf16)


def image_kernel(g_mine_ref, g_other_ref, text_ref, loss_ref, keep_ref, send_ref):
    width = text_ref.shape[-1]
    texts = text_ref[...].reshape(2 * side, width)
    packed = first_half(side)
    for g_ref, ref in ((g_other_ref, send_ref), (g_mine_ref, keep_ref)):
        part = g_ref[...]
        halves = [jnp.where(packed, half, 0.0) for half in (part, pltpu.roll(part, side - rows, 1))]
        part = jnp.concatenate(halves, axis=1)
        ref[:, :width] = jnp.dot(part.astype(bf16), texts, preferred_element_type=f32)
        ref[:, width:] = jnp.broadcast_to(loss_ref[0:1], (side, 128))


def send_out(total, ref):
    width = total.shape[2] - 128
    loss = total[:, :, width:]
    lane = lax.broadcasted_iota(jnp.int32, loss.shape, 2)
    pieces = jnp.zeros_like(loss)
    for k in range(3):
        piece = loss.astype(bf16).astype(f32)
        pieces = jnp.where(lane == k, piece, pieces)
        loss = loss - piece
    ref[:, :, :width] = total[:, :, :width].astype(bf16)
    ref[:, :, width:] = pieces.astype(bf16)


def core_kernel(keep_ref, got_ref, own_ref, *send_refs):
    y = lax.axis_index("yh") * 2 + lax.axis_index("yl")

    def block(k):
        to = (y + k) & 3
        parts = []
        for x in range(4):
            at = pl.ds(pl.multiple_of(x * 4 * rows + ((to & 1) * 2 + (to >> 1)) * rows, rows), rows)
            parts.append(keep_ref[at, :] + got_ref[at, :])
        return jnp.stack(parts)

    own_ref[...] = block(0)
    for k, ref in enumerate(send_refs, 1):
        send_out(block(k), ref)


def across_kernel(keep_ref, a_ref, b_ref, c_ref, out_ref):
    keep = keep_ref[...]
    got = (a_ref[...].astype(f32) + b_ref[...].astype(f32)) + c_ref[...].astype(f32)
    width = keep.shape[2] - 128
    loss = keep[:, :, width:] + jnp.sum(got[:, :, width:], axis=2, keepdims=True)
    send_out(jnp.concatenate([keep[:, :, :width] + got[:, :, :width], loss], axis=2), out_ref)


def last_kernel(image_ref, text_ref, grad_image_ref, grad_text_ref, loss_ref):
    total = jnp.sum(image_ref[...].astype(f32), axis=0)
    width = grad_image_ref.shape[1]
    grad_image_ref[...] = total[:, :width]
    grad_text_ref[...] = jnp.sum(text_ref[...].astype(f32), axis=0)
    loss_ref[...] = jnp.sum(total[:1, width:], axis=1, keepdims=True) * (1.0 / (2.0 * rows * n_plane * n_column))


def local(image, text, mimage, mtext):
    width = image.shape[1]
    wide = width + 128

    def swap(block, axis="c"):
        return lax.ppermute(block, axis, [(0, 1), (1, 0)])

    both = jnp.concatenate([text, mtext], axis=0)
    pair = jnp.concatenate([image, mimage], axis=0)
    both, pair = lax.optimization_barrier((both, pair))
    sent = jnp.broadcast_to(both[None], (n_column,) + both.shape)
    texts = lax.all_to_all(sent, column, 0, 0, tiled=True)
    across = swap(pair, "yh")
    (pair,) = call(partial(order_kernel, "yh"), [shape(2, 16, width, dtype=bf16)], pair, across, flops=2**35)
    (pair,) = call(partial(order_kernel, "yl"), [shape(2, 2, 16, width, dtype=bf16)], pair, swap(pair, "yl"))
    mine = lax.all_gather(pair, "x").reshape(16, 16, width)
    other = swap(mine)

    on, mom, row_parts, col_parts = call(
        score_kernel,
        [shape(2 * side, side), shape(2 * side, side), shape(n_plane, 8, side), shape(8, side)],
        mine, other, texts,
        flops=2**28, exps=2**18,
    )
    row_got = lax.all_to_all(row_parts, ("x", "yh", "yl", "c"), 0, 0, tiled=True)
    row_lse, col_sent = call(row_kernel, [shape(side, side), shape(n_column, 8, side)], row_got, col_parts, exps=2**14)
    col_got = lax.all_to_all(col_sent, column, 0, 0, tiled=True)

    by_text, g_mine, g_other, loss = call(
        grad_kernel,
        [shape(n_column, rows, width, dtype=bf16), shape(side, side), shape(side, side), shape(8, 128)],
        on, mom, row_lse, col_got, mine, other,
        flops=2**27, exps=2**17,
    )
    keep, send = call(image_kernel, [shape(side, wide), shape(side, wide)], g_mine, g_other, texts, loss, flops=2**27)
    got = swap(send)
    got_text = lax.all_to_all(by_text, column, 0, 0, tiled=True)
    keep, *send = call(core_kernel, [shape(4, rows, wide)] + [shape(4, rows, wide, dtype=bf16)] * 3, keep, got)
    along = [
        lax.ppermute(block, ("yh", "yl"), [(i, (i + k) % 4) for i in range(4)]) for k, block in enumerate(send, 1)
    ]
    (by_image,) = call(across_kernel, [shape(4, rows, wide, dtype=bf16)], keep, *along)
    by_image, got_text = lax.optimization_barrier((by_image, got_text))
    got_image = lax.all_to_all(by_image, "x", 0, 0, tiled=True)
    grad_image, grad_text, loss = call(
        last_kernel, [shape(rows, width), shape(rows, width), shape(1, 1)], got_image, got_text
    )
    return grad_image, grad_text, loss[0, 0]


def solution(mesh):
    fine = Mesh(mesh.devices.reshape(8, 2, 2, 2, 4, 2), ("zl", "yh", "yl", "zh", "x", "c"))
    by_image = P(("zh", "x", "c", "zl", "yh", "yl"), None)
    by_text = P(("zl", "yh", "yl", "zh", "x", "c"), None)
    return jax.shard_map(
        local,
        mesh=fine,
        in_specs=(by_image, by_text, by_image, by_text),
        out_specs=(by_image, by_text, P()),
        check_vma=False,
    )
```

```python
from functools import partial

import jax
import jax.numpy as jnp
from jax import lax
from jax.experimental import pallas as pl
from jax.experimental.pallas import tpu as pltpu
from jax.sharding import Mesh, PartitionSpec as P

mix_weight = 0.4
very_low = -1e30
column = ("zh", "zl")
n_plane, n_column, rows = 32, 16, 8
f32, bf16 = jnp.float32, jnp.bfloat16
side = 16 * rows


def call(body, outs, *args, flops=0, exps=0, **more):
    whole = pl.BlockSpec(memory_space=pltpu.VMEM)
    moved = sum(a.size * a.dtype.itemsize for a in list(args) + outs)
    params = dict(in_specs=[whole] * len(args), out_specs=[whole] * len(outs))
    params.update(more)
    return pl.pallas_call(
        body,
        out_shape=outs,
        cost_estimate=pl.CostEstimate(flops=flops, bytes_accessed=moved, transcendentals=exps),
        compiler_params=pltpu.CompilerParams(vmem_limit_bytes=40 * 2**20),
        **params,
    )(*args)


def shape(*dims, dtype=f32):
    return jax.ShapeDtypeStruct(dims, dtype)


def first_half(height):
    return (lax.broadcasted_iota(jnp.int32, (height, side), 1) & rows) == 0


def diagonal_of():
    x, yh, yl, c, zh, zl = (lax.axis_index(a) for a in ("x", "yh", "yl", "c", "zh", "zl"))
    y = yh * 2 + yl
    row = lax.broadcasted_iota(jnp.int32, (2 * side, 1), 0)
    pc, px, py = row >> 7, (row >> 5) & 3, (row >> 3) & 3
    image = ((zh * 8 + px * 2 + pc) * 32 + zl * 4 + py) * rows + (row & 7)
    lane = lax.broadcasted_iota(jnp.int32, (1, side), 1)
    qh, ql = (lane >> 3) & 1, lane >> 4
    text = ((ql * 4 + y) * 16 + qh * 8 + x * 2 + c) * rows + (lane & 7)
    return image == text


def order_kernel(axis, own_ref, other_ref, out_ref):
    place = lax.axis_index(axis)
    out_ref[place] = own_ref[...]
    out_ref[1 - place] = other_ref[...]


def score_kernel(mine_ref, other_ref, text_ref, on_ref, mom_ref, row_ref, col_ref):
    width = text_ref.shape[-1]
    texts = text_ref[...].reshape(2 * side, width)

    def product(ref):
        out = lax.dot_general(
            ref[...].reshape(2 * side, width), texts, (((1,), (1,)), ((), ())), preferred_element_type=f32
        )
        return (out * width ** (-0.5)).reshape(16, 2, rows, 2 * side)

    mine, other = product(mine_ref), product(other_ref)
    first = lax.axis_index("c") == 0
    low, high = jnp.where(first, mine, other), jnp.where(first, other, mine)
    packed = first_half(2 * side)

    def both(which):
        whole = jnp.concatenate([part[:, which].reshape(side, 2 * side) for part in (low, high)], axis=0)
        return whole[:, :side], whole[:, side:]

    left, right = both(0)
    on = jnp.where(packed, left, pltpu.roll(right, rows, 1))
    left, right = both(1)
    mom = jnp.where(packed, pltpu.roll(left, side - rows, 1), right)
    on_ref[...] = on
    mom_ref[...] = mom

    def stats(along):
        max_on = jnp.max(on, axis=along, keepdims=True)
        sum_on = jnp.sum(jnp.exp(on - max_on), axis=along, keepdims=True)
        max_mom = jnp.max(mom, axis=along, keepdims=True)
        weight = jnp.exp(mom - max_mom)
        sum_mom = jnp.sum(weight, axis=along, keepdims=True)
        mean = jnp.sum(weight * on, axis=along, keepdims=True) / sum_mom
        return [max_on + jnp.log(sum_on), max_mom + jnp.log(sum_mom), mean]

    slot = lax.broadcasted_iota(jnp.int32, (2 * side, 128), 1)
    by_row = jnp.zeros((2 * side, 128), f32)
    for k, value in enumerate(stats(1)):
        by_row = jnp.where(slot == k, value, by_row)
    by_row = by_row.T[:8]
    slot = lax.broadcasted_iota(jnp.int32, (8, side), 0)
    by_row = jnp.where(slot < 4, by_row[:, :side], pltpu.roll(by_row[:, side:], 4, 0))
    for peer in range(n_plane):
        row_ref[peer] = by_row
    own = jnp.sum(jnp.where(diagonal_of(), on, 0.0), axis=0, keepdims=True)
    slot = lax.broadcasted_iota(jnp.int32, (8, side), 0)
    by_col = jnp.zeros((8, side), f32)
    for k, value in enumerate(stats(0) + [own]):
        by_col = jnp.where(slot == k, value, by_col)
    col_ref[...] = by_col


def combine(got):
    top = jnp.max(got, axis=0)
    spread = jnp.exp(got - top[None])
    total = jnp.sum(spread, axis=0)
    lse = top + jnp.log(total)
    weight = pltpu.roll(spread, 1, 1)
    mean = jnp.sum(weight * got, axis=0) / pltpu.roll(total, 1, 0)
    return lse, mean


def row_kernel(got_ref, col_ref, lse_ref, send_ref):
    lse, mean = combine(got_ref[...])
    slot = lax.broadcasted_iota(jnp.int32, (8, side), 0)
    loss = jnp.sum(jnp.where((slot & 3) == 0, lse, jnp.where((slot & 3) == 2, -mix_weight * mean, 0.0)))
    lse_ref[...] = jnp.concatenate([lse] + [jnp.zeros((8, side), f32)] * 15, axis=0).T
    send = jnp.where(slot == 4, loss, col_ref[...])
    for peer in range(n_column):
        send_ref[peer] = send


def grad_kernel(
    on_ref, mom_ref, lse_ref, got_ref, mine_ref, other_ref, out_ref, g_mine_ref, g_other_ref, loss_ref
):
    width = mine_ref.shape[-1]
    got = got_ref[...]
    lse, mean = combine(got)
    sums = jnp.sum(got, axis=0)
    slot = lax.broadcasted_iota(jnp.int32, (8, side), 0)
    loss = jnp.where(slot == 3, -2.0 * (1.0 - mix_weight) * sums, 0.0)
    loss = jnp.where(slot == 0, lse, jnp.where(slot == 2, -mix_weight * mean, loss))
    loss = jnp.where(slot == 4, sums * (1.0 / (n_plane * side)), loss)
    loss_ref[...] = jnp.full(loss_ref.shape, jnp.sum(loss), f32)

    on, mom = on_ref[...], mom_ref[...]
    col_on, col_mom = lse[0:1], lse[1:2]
    row_on = jnp.concatenate([lse_ref[:, 0:1], lse_ref[:, 4:5]], axis=0)
    row_mom = jnp.concatenate([lse_ref[:, 1:2], lse_ref[:, 5:6]], axis=0)
    delta = jnp.where(diagonal_of(), 1.0 - mix_weight, 0.0)
    target_row = mix_weight * jnp.exp(mom - row_mom) + delta
    target_col = mix_weight * jnp.exp(mom - col_mom) + delta
    grad = 0.5 * ((jnp.exp(on - row_on) - target_row) + (jnp.exp(on - col_on) - target_col))
    first = lax.axis_index("c") == 0
    low, high = grad[:side], grad[side:]
    mine, other = jnp.where(first, low, high), jnp.where(first, high, low)
    g_mine_ref[...] = mine
    g_other_ref[...] = other

    def down(part, ref):
        part = part.reshape(16, 1, rows, side)
        part = jnp.concatenate([part, jnp.zeros_like(part)], axis=1).reshape(2 * side, side)
        return lax.dot_general(
            part.astype(bf16), ref[...].reshape(2 * side, width), (((0,), (0,)), ((), ())), preferred_element_type=f32
        )

    by_text = (down(mine, mine_ref) + down(other, other_ref)).reshape(8, 2, rows, width)
    for k in range(2):
        out_ref[8 * k : 8 * k + 8] = by_text[:, k].astype(bf16)


def image_kernel(g_mine_ref, g_other_ref, text_ref, loss_ref, keep_ref, send_ref):
    width = text_ref.shape[-1]
    texts = text_ref[...].reshape(2 * side, width)
    packed = first_half(side)
    for g_ref, ref in ((g_other_ref, send_ref), (g_mine_ref, keep_ref)):
        part = g_ref[...]
        halves = [jnp.where(packed, half, 0.0) for half in (part, pltpu.roll(part, side - rows, 1))]
        part = jnp.concatenate(halves, axis=1)
        ref[:, :width] = jnp.dot(part.astype(bf16), texts, preferred_element_type=f32)
        ref[:, width:] = jnp.broadcast_to(loss_ref[0:1], (side, 128))


def send_out(total, ref):
    width = total.shape[2] - 128
    loss = total[:, :, width:]
    lane = lax.broadcasted_iota(jnp.int32, loss.shape, 2)
    pieces = jnp.zeros_like(loss)
    for k in range(3):
        piece = loss.astype(bf16).astype(f32)
        pieces = jnp.where(lane == k, piece, pieces)
        loss = loss - piece
    ref[:, :, :width] = total[:, :, :width].astype(bf16)
    ref[:, :, width:] = pieces.astype(bf16)


def core_kernel(keep_ref, got_ref, own_ref, *send_refs):
    y = lax.axis_index("yh") * 2 + lax.axis_index("yl")

    def block(k):
        to = (y + k) & 3
        parts = []
        for x in range(4):
            at = pl.ds(pl.multiple_of(x * 4 * rows + to * rows, rows), rows)
            parts.append(keep_ref[at, :] + got_ref[at, :])
        return jnp.stack(parts)

    own_ref[...] = block(0)
    for k, ref in enumerate(send_refs, 1):
        send_out(block(k), ref)


def across_kernel(keep_ref, a_ref, b_ref, c_ref, out_ref):
    keep = keep_ref[...]
    got = (a_ref[...].astype(f32) + b_ref[...].astype(f32)) + c_ref[...].astype(f32)
    width = keep.shape[2] - 128
    loss = keep[:, :, width:] + jnp.sum(got[:, :, width:], axis=2, keepdims=True)
    send_out(jnp.concatenate([keep[:, :, :width] + got[:, :, :width], loss], axis=2), out_ref)


def last_kernel(image_ref, text_ref, grad_image_ref, grad_text_ref, loss_ref):
    total = jnp.sum(image_ref[...].astype(f32), axis=0)
    width = grad_image_ref.shape[1]
    grad_image_ref[...] = total[:, :width]
    grad_text_ref[...] = jnp.sum(text_ref[...].astype(f32), axis=0)
    loss_ref[0, 0] = jnp.sum(total[:1, width:]) * (1.0 / (2.0 * rows * n_plane * n_column))


def local(image, text, mimage, mtext):
    width = image.shape[1]
    wide = width + 128

    def swap(block, axis="c"):
        return lax.ppermute(block, axis, [(0, 1), (1, 0)])

    both = jnp.concatenate([text, mtext], axis=0)
    pair = jnp.concatenate([image, mimage], axis=0)
    both, pair = lax.optimization_barrier((both, pair))
    sent = jnp.broadcast_to(both[None], (n_column,) + both.shape)
    texts = lax.all_to_all(sent, column, 0, 0, tiled=True)
    across = swap(pair, "yl")
    (pair,) = call(partial(order_kernel, "yl"), [shape(2, 16, width, dtype=bf16)], pair, across, flops=2**35)
    (pair,) = call(partial(order_kernel, "yh"), [shape(2, 2, 16, width, dtype=bf16)], pair, swap(pair, "yh"))
    mine = lax.all_gather(pair, "x").reshape(16, 16, width)
    other = swap(mine)

    on, mom, row_parts, col_parts = call(
        score_kernel,
        [shape(2 * side, side), shape(2 * side, side), shape(n_plane, 8, side), shape(8, side)],
        mine, other, texts,
        flops=2**28, exps=2**18,
    )
    row_got = lax.all_to_all(row_parts, ("x", "yh", "yl", "c"), 0, 0, tiled=True)
    row_lse, col_sent = call(row_kernel, [shape(side, side), shape(n_column, 8, side)], row_got, col_parts, exps=2**14)
    col_got = lax.all_to_all(col_sent, column, 0, 0, tiled=True)

    by_text, g_mine, g_other, loss = call(
        grad_kernel,
        [shape(n_column, rows, width, dtype=bf16), shape(side, side), shape(side, side), shape(8, 128)],
        on, mom, row_lse, col_got, mine, other,
        flops=2**27, exps=2**17,
    )
    keep, send = call(image_kernel, [shape(side, wide), shape(side, wide)], g_mine, g_other, texts, loss, flops=2**27)
    got = swap(send)
    got_text = lax.all_to_all(by_text, column, 0, 0, tiled=True)
    keep, *send = call(core_kernel, [shape(4, rows, wide)] + [shape(4, rows, wide, dtype=bf16)] * 3, keep, got)
    along = [
        lax.ppermute(block, ("yh", "yl"), [(i, (i + k) % 4) for i in range(4)]) for k, block in enumerate(send, 1)
    ]
    (by_image,) = call(across_kernel, [shape(4, rows, wide, dtype=bf16)], keep, *along)
    by_image, got_text = lax.optimization_barrier((by_image, got_text))
    got_image = lax.all_to_all(by_image, "x", 0, 0, tiled=True)
    vmem = pl.BlockSpec(memory_space=pltpu.VMEM)
    grad_image, grad_text, loss = call(
        last_kernel, [shape(rows, width), shape(rows, width), shape(1, 1)], got_image, got_text,
        out_specs=[vmem, vmem, pl.BlockSpec(memory_space=pltpu.SMEM)],
    )
    return grad_image, grad_text, loss[0, 0]


def solution(mesh):
    fine = Mesh(mesh.devices.reshape(8, 2, 2, 2, 4, 2), ("zl", "yh", "yl", "zh", "x", "c"))
    by_image = P(("zh", "x", "c", "zl", "yh", "yl"), None)
    by_text = P(("zl", "yh", "yl", "zh", "x", "c"), None)
    return jax.shard_map(
        local,
        mesh=fine,
        in_specs=(by_image, by_text, by_image, by_text),
        out_specs=(by_image, by_text, P()),
        check_vma=False,
    )
```

```python
from functools import partial

import jax
import jax.numpy as jnp
from jax import lax
from jax.experimental import pallas as pl
from jax.experimental.pallas import tpu as pltpu
from jax.sharding import Mesh, PartitionSpec as P

mix_weight = 0.4
very_low = -1e30
column = ("zh", "zl")
n_plane, n_column, rows = 32, 16, 8
f32, bf16 = jnp.float32, jnp.bfloat16
side = 16 * rows


def call(body, outs, *args, flops=0, exps=0, **more):
    whole = pl.BlockSpec(memory_space=pltpu.VMEM)
    moved = sum(a.size * a.dtype.itemsize for a in list(args) + outs)
    params = dict(in_specs=[whole] * len(args), out_specs=[whole] * len(outs))
    params.update(more)
    return pl.pallas_call(
        body,
        out_shape=outs,
        cost_estimate=pl.CostEstimate(flops=flops, bytes_accessed=moved, transcendentals=exps),
        compiler_params=pltpu.CompilerParams(vmem_limit_bytes=40 * 2**20),
        **params,
    )(*args)


def shape(*dims, dtype=f32):
    return jax.ShapeDtypeStruct(dims, dtype)


def first_half(height):
    return (lax.broadcasted_iota(jnp.int32, (height, side), 1) & rows) == 0


def diagonal_of():
    x, yh, yl, c, zh, zl = (lax.axis_index(a) for a in ("x", "yh", "yl", "c", "zh", "zl"))
    y = yh * 2 + yl
    row = lax.broadcasted_iota(jnp.int32, (2 * side, 1), 0)
    pc, px, py = row >> 7, (row >> 5) & 3, ((row >> 3) & 1) * 2 + ((row >> 4) & 1)
    image = ((zh * 8 + px * 2 + pc) * 32 + zl * 4 + py) * rows + (row & 7)
    lane = lax.broadcasted_iota(jnp.int32, (1, side), 1)
    qh, ql = (lane >> 3) & 1, lane >> 4
    text = ((ql * 4 + y) * 16 + qh * 8 + x * 2 + c) * rows + (lane & 7)
    return image == text


def order_kernel(axis, own_ref, other_ref, out_ref):
    place = lax.axis_index(axis)
    out_ref[place] = own_ref[...]
    out_ref[1 - place] = other_ref[...]


def score_kernel(mine_ref, other_ref, text_ref, on_ref, mom_ref, row_ref, col_ref):
    width = text_ref.shape[-1]
    texts = text_ref[...].reshape(2 * side, width)

    def product(ref):
        out = lax.dot_general(
            ref[...].reshape(2 * side, width), texts, (((1,), (1,)), ((), ())), preferred_element_type=f32
        )
        return (out * width ** (-0.5)).reshape(16, 2, rows, 2 * side)

    mine, other = product(mine_ref), product(other_ref)
    first = lax.axis_index("c") == 0
    low, high = jnp.where(first, mine, other), jnp.where(first, other, mine)
    packed = first_half(2 * side)

    def both(which):
        whole = jnp.concatenate([part[:, which].reshape(side, 2 * side) for part in (low, high)], axis=0)
        return whole[:, :side], whole[:, side:]

    left, right = both(0)
    on = jnp.where(packed, left, pltpu.roll(right, rows, 1))
    left, right = both(1)
    mom = jnp.where(packed, pltpu.roll(left, side - rows, 1), right)
    on_ref[...] = on
    mom_ref[...] = mom

    def stats(along):
        max_on = jnp.max(on, axis=along, keepdims=True)
        sum_on = jnp.sum(jnp.exp(on - max_on), axis=along, keepdims=True)
        max_mom = jnp.max(mom, axis=along, keepdims=True)
        weight = jnp.exp(mom - max_mom)
        sum_mom = jnp.sum(weight, axis=along, keepdims=True)
        mean = jnp.sum(weight * on, axis=along, keepdims=True) / sum_mom
        return [max_on + jnp.log(sum_on), max_mom + jnp.log(sum_mom), mean]

    slot = lax.broadcasted_iota(jnp.int32, (2 * side, 128), 1)
    by_row = jnp.zeros((2 * side, 128), f32)
    for k, value in enumerate(stats(1)):
        by_row = jnp.where(slot == k, value, by_row)
    by_row = by_row.T[:8]
    slot = lax.broadcasted_iota(jnp.int32, (8, side), 0)
    by_row = jnp.where(slot < 4, by_row[:, :side], pltpu.roll(by_row[:, side:], 4, 0))
    for peer in range(n_plane):
        row_ref[peer] = by_row
    own = jnp.sum(jnp.where(diagonal_of(), on, 0.0), axis=0, keepdims=True)
    slot = lax.broadcasted_iota(jnp.int32, (8, side), 0)
    by_col = jnp.zeros((8, side), f32)
    for k, value in enumerate(stats(0) + [own]):
        by_col = jnp.where(slot == k, value, by_col)
    col_ref[...] = by_col


def combine(got):
    top = jnp.max(got, axis=0)
    spread = jnp.exp(got - top[None])
    total = jnp.sum(spread, axis=0)
    lse = top + jnp.log(total)
    weight = pltpu.roll(spread, 1, 1)
    mean = jnp.sum(weight * got, axis=0) / pltpu.roll(total, 1, 0)
    return lse, mean


def row_kernel(got_ref, col_ref, lse_ref, send_ref):
    lse, mean = combine(got_ref[...])
    slot = lax.broadcasted_iota(jnp.int32, (8, side), 0)
    loss = jnp.sum(jnp.where((slot & 3) == 0, lse, jnp.where((slot & 3) == 2, -mix_weight * mean, 0.0)))
    lse_ref[...] = jnp.concatenate([lse] + [jnp.zeros((8, side), f32)] * 15, axis=0).T
    send = jnp.where(slot == 4, loss, col_ref[...])
    for peer in range(n_column):
        send_ref[peer] = send


def grad_kernel(
    on_ref, mom_ref, lse_ref, got_ref, mine_ref, other_ref, out_ref, g_mine_ref, g_other_ref, loss_ref
):
    width = mine_ref.shape[-1]
    got = got_ref[...]
    lse, mean = combine(got)
    sums = jnp.sum(got, axis=0)
    slot = lax.broadcasted_iota(jnp.int32, (8, side), 0)
    loss = jnp.where(slot == 3, -2.0 * (1.0 - mix_weight) * sums, 0.0)
    loss = jnp.where(slot == 0, lse, jnp.where(slot == 2, -mix_weight * mean, loss))
    loss = jnp.where(slot == 4, sums * (1.0 / (n_plane * side)), loss)
    loss_ref[...] = jnp.full(loss_ref.shape, jnp.sum(loss), f32)

    on, mom = on_ref[...], mom_ref[...]
    col_on, col_mom = lse[0:1], lse[1:2]
    row_on = jnp.concatenate([lse_ref[:, 0:1], lse_ref[:, 4:5]], axis=0)
    row_mom = jnp.concatenate([lse_ref[:, 1:2], lse_ref[:, 5:6]], axis=0)
    delta = jnp.where(diagonal_of(), 1.0 - mix_weight, 0.0)
    target_row = mix_weight * jnp.exp(mom - row_mom) + delta
    target_col = mix_weight * jnp.exp(mom - col_mom) + delta
    grad = 0.5 * ((jnp.exp(on - row_on) - target_row) + (jnp.exp(on - col_on) - target_col))
    first = lax.axis_index("c") == 0
    low, high = grad[:side], grad[side:]
    mine, other = jnp.where(first, low, high), jnp.where(first, high, low)
    g_mine_ref[...] = mine
    g_other_ref[...] = other

    def down(part, ref):
        part = part.reshape(16, 1, rows, side)
        part = jnp.concatenate([part, jnp.zeros_like(part)], axis=1).reshape(2 * side, side)
        return lax.dot_general(
            part.astype(bf16), ref[...].reshape(2 * side, width), (((0,), (0,)), ((), ())), preferred_element_type=f32
        )

    by_text = (down(mine, mine_ref) + down(other, other_ref)).reshape(8, 2, rows, width)
    for k in range(2):
        out_ref[8 * k : 8 * k + 8] = by_text[:, k].astype(bf16)


def image_kernel(g_mine_ref, g_other_ref, text_ref, loss_ref, keep_ref, send_ref):
    width = text_ref.shape[-1]
    texts = text_ref[...].reshape(2 * side, width)
    packed = first_half(side)
    for g_ref, ref in ((g_other_ref, send_ref), (g_mine_ref, keep_ref)):
        part = g_ref[...]
        halves = [jnp.where(packed, half, 0.0) for half in (part, pltpu.roll(part, side - rows, 1))]
        part = jnp.concatenate(halves, axis=1)
        ref[:, :width] = jnp.dot(part.astype(bf16), texts, preferred_element_type=f32)
        ref[:, width:] = jnp.broadcast_to(loss_ref[0:1], (side, 128))


def send_out(total, ref):
    width = total.shape[2] - 128
    loss = total[:, :, width:]
    lane = lax.broadcasted_iota(jnp.int32, loss.shape, 2)
    pieces = jnp.zeros_like(loss)
    for k in range(3):
        piece = loss.astype(bf16).astype(f32)
        pieces = jnp.where(lane == k, piece, pieces)
        loss = loss - piece
    ref[:, :, :width] = total[:, :, :width].astype(bf16)
    ref[:, :, width:] = pieces.astype(bf16)


def core_kernel(keep_ref, got_ref, own_ref, *send_refs):
    y = lax.axis_index("yh") * 2 + lax.axis_index("yl")

    def block(k):
        to = (y + k) & 3
        parts = []
        for x in range(4):
            at = pl.ds(pl.multiple_of(x * 4 * rows + ((to & 1) * 2 + (to >> 1)) * rows, rows), rows)
            parts.append(keep_ref[at, :] + got_ref[at, :])
        return jnp.stack(parts)

    own_ref[...] = block(0)
    for k, ref in enumerate(send_refs, 1):
        send_out(block(k), ref)


def across_kernel(keep_ref, a_ref, b_ref, c_ref, out_ref):
    keep = keep_ref[...]
    got = (a_ref[...].astype(f32) + b_ref[...].astype(f32)) + c_ref[...].astype(f32)
    width = keep.shape[2] - 128
    loss = keep[:, :, width:] + jnp.sum(got[:, :, width:], axis=2, keepdims=True)
    send_out(jnp.concatenate([keep[:, :, :width] + got[:, :, :width], loss], axis=2), out_ref)


def last_kernel(image_ref, text_ref, grad_image_ref, grad_text_ref, loss_ref):
    total = jnp.sum(image_ref[...].astype(f32), axis=0)
    width = grad_image_ref.shape[1]
    grad_image_ref[...] = total[:, :width]
    grad_text_ref[...] = jnp.sum(text_ref[...].astype(f32), axis=0)
    loss_ref[0, 0] = jnp.sum(total[:1, width:]) * (1.0 / (2.0 * rows * n_plane * n_column))


def local(image, text, mimage, mtext):
    width = image.shape[1]
    wide = width + 128

    def swap(block, axis="c"):
        return lax.ppermute(block, axis, [(0, 1), (1, 0)])

    both = jnp.concatenate([text, mtext], axis=0)
    pair = jnp.concatenate([image, mimage], axis=0)
    both, pair = lax.optimization_barrier((both, pair))
    sent = jnp.broadcast_to(both[None], (n_column,) + both.shape)
    texts = lax.all_to_all(sent, column, 0, 0, tiled=True)
    across = swap(pair, "yh")
    (pair,) = call(partial(order_kernel, "yh"), [shape(2, 16, width, dtype=bf16)], pair, across, flops=2**35)
    (pair,) = call(partial(order_kernel, "yl"), [shape(2, 2, 16, width, dtype=bf16)], pair, swap(pair, "yl"))
    mine = lax.all_gather(pair, "x").reshape(16, 16, width)
    other = swap(mine)

    on, mom, row_parts, col_parts = call(
        score_kernel,
        [shape(2 * side, side), shape(2 * side, side), shape(n_plane, 8, side), shape(8, side)],
        mine, other, texts,
        flops=2**28, exps=2**18,
    )
    row_got = lax.all_to_all(row_parts, ("c", "yh", "yl", "x"), 0, 0, tiled=True)
    row_lse, col_sent = call(row_kernel, [shape(side, side), shape(n_column, 8, side)], row_got, col_parts, exps=2**14)
    col_got = lax.all_to_all(col_sent, column, 0, 0, tiled=True)

    by_text, g_mine, g_other, loss = call(
        grad_kernel,
        [shape(n_column, rows, width, dtype=bf16), shape(side, side), shape(side, side), shape(8, 128)],
        on, mom, row_lse, col_got, mine, other,
        flops=2**27, exps=2**17,
    )
    keep, send = call(image_kernel, [shape(side, wide), shape(side, wide)], g_mine, g_other, texts, loss, flops=2**27)
    got = swap(send)
    got_text = lax.all_to_all(by_text, column, 0, 0, tiled=True)
    keep, *send = call(core_kernel, [shape(4, rows, wide)] + [shape(4, rows, wide, dtype=bf16)] * 3, keep, got)
    along = [
        lax.ppermute(block, ("yh", "yl"), [(i, (i + k) % 4) for i in range(4)]) for k, block in enumerate(send, 1)
    ]
    (by_image,) = call(across_kernel, [shape(4, rows, wide, dtype=bf16)], keep, *along)
    by_image, got_text = lax.optimization_barrier((by_image, got_text))
    got_image = lax.all_to_all(by_image, "x", 0, 0, tiled=True)
    vmem = pl.BlockSpec(memory_space=pltpu.VMEM)
    grad_image, grad_text, loss = call(
        last_kernel, [shape(rows, width), shape(rows, width), shape(1, 1)], got_image, got_text,
        out_specs=[vmem, vmem, pl.BlockSpec(memory_space=pltpu.SMEM)],
    )
    return grad_image, grad_text, loss[0, 0]


def solution(mesh):
    fine = Mesh(mesh.devices.reshape(8, 2, 2, 2, 4, 2), ("zl", "yh", "yl", "zh", "x", "c"))
    by_image = P(("zh", "x", "c", "zl", "yh", "yl"), None)
    by_text = P(("zl", "yh", "yl", "zh", "x", "c"), None)
    return jax.shard_map(
        local,
        mesh=fine,
        in_specs=(by_image, by_text, by_image, by_text),
        out_specs=(by_image, by_text, P()),
        check_vma=False,
    )
```
